32 devices in a mesh: dp: 8 (over z, x), mp: 4 (over y, core).
Axes of the slice: x: 2, y: 2, z: 4, core: 2. Of those that a mesh axis runs over, the one named last changes fastest.
Arguments:
- tokens: bfloat16 [24576, 768], P(('dp', 'mp')), may hold values from -6 to 6
- cotangent: bfloat16 [24576, 768], P(('dp', 'mp')), may hold values from -6 to 6
- row_item: int32 [24576], P('dp'), may hold values from -1 to 10, as said below
- w_qkv: float32 [768, 2304], P('dp', 'mp'), may hold values from -0.21875 to 0.21875
- w_out: float32 [768, 768], P('mp', 'dp'), may hold values from -4 to 4
- w_up: float32 [768, 3072], P('dp', 'mp'), may hold values from -0.21875 to 0.21875
- w_down: float32 [3072, 768], P('mp', 'dp'), may hold values from -0.109375 to 0.109375
- small_params: float32 [6, 768], replicated, as said below
- up_bias: float32 [3072], replicated, may hold values from -1.2 to 1.2
- first_qkv: float32 [768, 2304], P('dp', 'mp'), may hold values from -0.00030517578 to 0.00030517578
- first_out: float32 [768, 768], P('mp', 'dp'), may hold values from -2.2888184e-05 to 2.2888184e-05
- first_up: float32 [768, 3072], P('dp', 'mp'), may hold values from -0.00024414062 to 0.00024414062
- first_down: float32 [3072, 768], P('mp', 'dp'), may hold values from -0.00024414062 to 0.00024414062
- first_small: float32 [6, 768], replicated, may hold values from -0.00048828125 to 0.00048828125
- first_bias: float32 [3072], replicated, may hold values from -0.00024414062 to 0.00024414062
- second_qkv: float32 [768, 2304], P('dp', 'mp'), may hold values from 1.1585377e-10 to 1.8508346e-09
- second_out: float32 [768, 768], P('mp', 'dp'), may hold values from 5.9339735e-13 to 9.466101e-12
- second_up: float32 [768, 3072], P('dp', 'mp'), may hold values from 1.4834934e-11 to 2.3735894e-10
- second_down: float32 [3072, 768], P('mp', 'dp'), may hold values from 5.9339735e-11 to 9.4661e-10
- second_small: float32 [6, 768], replicated, may hold values from 2.359461e-10 to 3.772312e-09
- second_bias: float32 [3072], replicated, may hold values from 7.417467e-12 to 1.1867947e-10
Outputs:
- output: bfloat16 [24576, 768], P(('dp', 'mp'))
- input_grad: float32 [24576, 768], P(('dp', 'mp'))
- grad_norm: float32 [], replicated
- new_qkv: float32 [768, 2304], P('dp', 'mp')
- new_first_qkv: float32 [768, 2304], P('dp', 'mp')
- new_second_qkv: float32 [768, 2304], P('dp', 'mp')
- new_out: float32 [768, 768], P('mp', 'dp')
- new_first_out: float32 [768, 768], P('mp', 'dp')
- new_second_out: float32 [768, 768], P('mp', 'dp')
- new_up: float32 [768, 3072], P('dp', 'mp')
- new_first_up: float32 [768, 3072], P('dp', 'mp')
- new_second_up: float32 [768, 3072], P('dp', 'mp')
- new_down: float32 [3072, 768], P('mp', 'dp')
- new_first_down: float32 [3072, 768], P('mp', 'dp')
- new_second_down: float32 [3072, 768], P('mp', 'dp')
- new_small: float32 [6, 768], replicated
- new_first_small: float32 [6, 768], replicated
- new_second_small: float32 [6, 768], replicated
- new_bias: float32 [3072], replicated
- new_first_bias: float32 [3072], replicated
- new_second_bias: float32 [3072], replicated
The draws below stay inside these ranges and needn't reach their ends.
Inputs may be any that keep to these rules, and one draw needn't show every extreme that they name: `row_item`: within each aligned block of 3072 rows, items are runs of exactly 1025 rows numbered from 0, then runs of exactly 257 rows numbered on, as many as fit; the rows left at the block's end are padding with -1; the first block holds only items of 257 rows. `small_params`: rows 0 and 2 are gains near 1, the other rows are shifts and biases near 0.
All inputs are finite; a program needn't handle non-finite values.
Results may differ from the reference program's by a relative error of at most 0.014.
Values may be sent and summed in bfloat16 or wider, within the bound.
No kernel may reach another device: no remote copies, remote signals or barrier semaphores. Data moves between devices by JAX's collectives and lax.ppermute only.
A program may use at most 192 MiB of HBM per device.

```python
import math
from functools import partial
import jax
import jax.numpy as jnp
from jax import lax

HEADS = 12
HEAD_DIM = 64
FF = 3072
D = 768
SHORT = 257
LONG = 1025
STEP = 5
GROUP_ROWS = 3072
GROUPS = 8
TOKENS = 24576


def draw_row_item(key, part):
    groups = TOKENS // GROUP_ROWS
    most_long = GROUP_ROWS // LONG
    long_counts = jax.random.randint(key, (groups,), 0, most_long + 1)
    long_counts = jnp.where(jnp.arange(groups) == 0, 0, long_counts)
    position = jnp.arange(GROUP_ROWS, dtype=jnp.int32)[None, :]
    long_rows = long_counts[:, None] * LONG
    short_count = (GROUP_ROWS - long_rows) // SHORT
    after = position - long_rows
    short_ids = long_counts[:, None] + jnp.maximum(after, 0) // SHORT
    item_ids = jnp.where(position < long_rows, position // LONG, jnp.where(after < short_count * SHORT, short_ids, -1))
    return item_ids.reshape(TOKENS).astype(jnp.int32)


def draw_small_params(key, part):
    key_gain, key_shift = jax.random.split(jax.random.fold_in(key, 11))
    gain_rows = 1.0 + 0.12 * jax.random.normal(key_gain, (6, D), jnp.float32)
    shift_rows = 0.2 * jax.random.normal(key_shift, (6, D), jnp.float32)
    row_index = jnp.arange(6)[:, None]
    is_gain = (row_index == 0) | (row_index == 2)
    return jnp.where(is_gain, gain_rows, shift_rows).astype(jnp.float32)


def levels(rng, shape, cuts, smallest, top_value):
    loudness, own = 1.0, jax.random.fold_in(rng, 6)
    for dim, blocks in cuts:
        steps = jnp.exp(jax.random.uniform(jax.random.fold_in(own, dim), (blocks,), jnp.float32, smallest / len(cuts), top_value / len(cuts)))
        loudness = loudness * jnp.repeat(steps, shape[dim] // blocks).reshape([-1 if axis == dim else 1 for axis in range(len(shape))])
    return loudness


def gaussian(rng, shape, deviation, most, cuts=(), kind=jnp.bfloat16):
    result = jax.random.normal(rng, shape, jnp.float32) * deviation
    if len(cuts) > 0:
        result = levels(rng, shape, cuts, -0.22, 0.18) * result
    return jnp.clip(result, min=-most, max=most).astype(kind)


def setup_inputs(seed: int = 0) -> dict:
    seeds = jax.random.split(jax.random.key(seed), 22)
    tokens = gaussian(seeds[0], (TOKENS, D), 1.0, 6.0, ((0, 32),))
    cotangent = gaussian(seeds[1], (TOKENS, D), 1.0, 6.0, ((0, 32),))
    row_item = draw_row_item(jax.random.fold_in(seeds[21], 71), 0)
    w_qkv = gaussian(seeds[3], (D, 3 * D), D ** -0.5, 0.21875, ((0, 8), (1, 4)), jnp.float32)
    w_out = gaussian(seeds[4], (D, D), (max(D // SHORT, 1)) ** -0.5, 4.0, ((0, 4), (1, 8)), jnp.float32)
    w_up = gaussian(seeds[5], (D, FF), D ** -0.5, 0.21875, ((0, 8), (1, 4)), jnp.float32)
    w_down = gaussian(seeds[6], (FF, D), FF ** -0.5, 0.109375, ((0, 4), (1, 8)), jnp.float32)
    small_params = draw_small_params(jax.random.fold_in(seeds[21], 71), 0)
    up_bias = gaussian(seeds[8], (FF,), 0.2, 1.2, (), jnp.float32)
    first_qkv = gaussian(seeds[9], (D, 3 * D), (0.142 * (4 * D * D + 2 * D * FF) ** -0.5), 0.00030517578, ((0, 8), (1, 4)), jnp.float32)
    first_out = gaussian(seeds[10], (D, D), (0.0101 * (4 * D * D + 2 * D * FF) ** -0.5), 2.288818359375e-05, ((0, 4), (1, 8)), jnp.float32)
    first_up = gaussian(seeds[11], (D, FF), (0.101 * (4 * D * D + 2 * D * FF) ** -0.5), 0.00024414062, ((0, 8), (1, 4)), jnp.float32)
    first_down = gaussian(seeds[12], (FF, D), (0.101 * (4 * D * D + 2 * D * FF) ** -0.5), 0.00024414062, ((0, 4), (1, 8)), jnp.float32)
    first_small = gaussian(seeds[13], (6, D), (0.203 * (4 * D * D + 2 * D * FF) ** -0.5), 0.00048828125, (), jnp.float32)
    first_bias = gaussian(seeds[14], (FF,), (0.101 * (4 * D * D + 2 * D * FF) ** -0.5), 0.00024414062, (), jnp.float32)
    second_qkv = jnp.clip(jnp.exp(math.log(1.8508345966949946e-09) - 2.771063 * jax.random.uniform(seeds[15], (D, 3 * D), jnp.float32) ** levels(seeds[15], (D, 3 * D), ((0, 8), (1, 4)), -0.2, 0.2)), 1.1585377102107941e-10, 1.8508345966949946e-09)
    second_out = jnp.clip(jnp.exp(math.log(9.466100646393638e-12) - 2.769608 * jax.random.uniform(seeds[16], (D, D), jnp.float32) ** levels(seeds[16], (D, D), ((0, 4), (1, 8)), -0.2, 0.2)), 5.93397347318364e-13, 9.466100646393638e-12)
    second_up = jnp.clip(jnp.exp(math.log(2.3735893805998387e-10) - 2.7725887 * jax.random.uniform(seeds[17], (D, FF), jnp.float32) ** levels(seeds[17], (D, FF), ((0, 8), (1, 4)), -0.2, 0.2)), 1.4834933628748992e-11, 2.3735893805998387e-10)
    second_down = jnp.clip(jnp.exp(math.log(9.466100125976595e-10) - 2.769608 * jax.random.uniform(seeds[18], (FF, D), jnp.float32) ** levels(seeds[18], (FF, D), ((0, 4), (1, 8)), -0.2, 0.2)), 5.933973451499597e-11, 9.466100125976595e-10)
    second_small = jnp.clip(jnp.exp(jax.random.uniform(seeds[19], (6, D), jnp.float32, math.log(2.359460959944215e-10), math.log(3.772311796268468e-09))), 2.359460959944215e-10, 3.772311796268468e-09)
    second_bias = jnp.clip(jnp.exp(jax.random.uniform(seeds[20], (FF,), jnp.float32, math.log(7.417466814374496e-12), math.log(1.1867946902999194e-10))), 7.417466814374496e-12, 1.1867946902999194e-10)
    return {"tokens": tokens, "cotangent": cotangent, "row_item": row_item, "w_qkv": w_qkv, "w_out": w_out, "w_up": w_up, "w_down": w_down, "small_params": small_params, "up_bias": up_bias, "first_qkv": first_qkv, "first_out": first_out, "first_up": first_up, "first_down": first_down, "first_small": first_small, "first_bias": first_bias, "second_qkv": second_qkv, "second_out": second_out, "second_up": second_up, "second_down": second_down, "second_small": second_small, "second_bias": second_bias}


@jax.custom_vjp
def low(v):
    return lax.optimization_barrier(v.astype(jnp.bfloat16)).astype(jnp.float32)

@jax.custom_vjp
def low_back(v):
    return v

def low_keep(v):
    return (low(v), None)

def low_pass(kept, grad):
    return (grad,)

def back_keep(v):
    return (v, None)

def back_low(kept, grad):
    return (low(grad),)
low.defvjp(low_keep, low_pass)
low_back.defvjp(back_keep, back_low)
CLIP_NORM = 1.0
BETA_ONE = 0.9
BETA_TWO = 0.999
ADAM_EPS = 1e-08
DECAY = 0.03
NORM_EPS = 1e-05
NEG_LARGE = -1e+30

def matmul(left, right):
    return jnp.dot(left, right, precision=lax.Precision.HIGHEST, preferred_element_type=jnp.float32)

def layer_norm(values, gain_row, shift_row):
    centre = values - lax.optimization_barrier(jnp.mean(values, axis=-1, keepdims=True))
    spread = lax.optimization_barrier(jnp.mean(centre * centre, axis=-1, keepdims=True))
    return centre * lax.rsqrt(spread + NORM_EPS) * gain_row + shift_row

def head_attend(head_parts, item_ids):
    queries, key_rows, value_rows = (head_parts[0], head_parts[1], head_parts[2])
    raw_scores = low_back(matmul(queries, key_rows.T) * HEAD_DIM ** (-0.5))
    same_item = item_ids[:, None] == item_ids[None, :]
    masked = jnp.where(same_item, raw_scores, NEG_LARGE)
    row_top = lax.optimization_barrier(jnp.max(masked, axis=-1, keepdims=True))
    exp_scores = jnp.exp(masked - row_top)
    probs_low = low(exp_scores / lax.optimization_barrier(jnp.sum(exp_scores, axis=-1, keepdims=True)))
    return matmul(probs_low, value_rows)

def group_layer(group_tokens, item_ids, low_qkv, low_out, low_up, low_down, small_in, bias_in):
    row_total = group_tokens.shape[0]
    normed = low(layer_norm(group_tokens, small_in[0], small_in[1]))
    packed = low(low_back(matmul(normed, low_qkv)))
    packed = packed.reshape(row_total, HEADS, 3, HEAD_DIM).transpose(1, 2, 0, 3)
    attended = lax.map(jax.checkpoint(partial(head_attend, item_ids=item_ids)), packed)
    attended = low(low_back(attended.transpose(1, 0, 2).reshape(row_total, D)))
    mixed = group_tokens + low_back(matmul(attended, low_out)) + small_in[4]
    normed_two = low(layer_norm(mixed, small_in[2], small_in[3]))
    pre_act = low_back(matmul(normed_two, low_up) + bias_in)
    hidden = low(jax.nn.gelu(pre_act, approximate=False))
    return mixed + low_back(matmul(hidden, low_down)) + small_in[5]

def adam_update(weight, gradient, first, second, step_rate):
    first_new = BETA_ONE * first + (1.0 - BETA_ONE) * gradient
    second_new = BETA_TWO * second + (1.0 - BETA_TWO) * gradient * gradient
    first_hat = first_new / (1.0 - BETA_ONE ** STEP)
    second_hat = second_new / (1.0 - BETA_TWO ** STEP)
    weight_new = weight - step_rate * (first_hat / (jnp.sqrt(second_hat) + ADAM_EPS) + DECAY * weight)
    return (weight_new, first_new, second_new)

def learning_rates():
    return (2.0 * D ** (-0.5), 2.0 * max(D // SHORT, 1) ** (-0.5), 2.0 * D ** (-0.5), 2.0 * FF ** (-0.5), 0.4, 0.4)

def reference(tokens, cotangent, row_item, w_qkv, w_out, w_up, w_down, small_params, up_bias, first_qkv, first_out, first_up, first_down, first_small, first_bias, second_qkv, second_out, second_up, second_down, second_small, second_bias):
    x_all = tokens.astype(jnp.float32).reshape(GROUPS, GROUP_ROWS, D)
    ids_all = row_item.reshape(GROUPS, GROUP_ROWS)
    keep_rows = (ids_all >= 0).astype(jnp.float32)[..., None]
    upstream = cotangent.astype(jnp.float32).reshape(GROUPS, GROUP_ROWS, D) * keep_rows

    def forward(x_in, weight_qkv, weight_out, weight_up, weight_down, small_in, bias_in):
        low_qkv = low(weight_qkv)
        low_out = low(weight_out)
        low_up = low(weight_up)
        low_down = low(weight_down)

        def one_group(pair):
            return group_layer(pair[0], pair[1], low_qkv, low_out, low_up, low_down, small_in, bias_in)
        return lax.map(jax.checkpoint(one_group), (x_in, ids_all))
    outputs, pullback = jax.vjp(forward, x_all, w_qkv, w_out, w_up, w_down, small_params, up_bias)
    gradients = pullback(upstream)
    input_grad = gradients[0].reshape(TOKENS, D)
    averaged = [gradient / GROUPS for gradient in gradients[1:]]
    squares = jnp.float32(0.0)
    for gradient in averaged:
        squares = squares + jnp.sum(gradient * gradient)
    grad_norm = jnp.sqrt(squares)
    factor = CLIP_NORM / jnp.maximum(grad_norm, CLIP_NORM)
    weights = (w_qkv, w_out, w_up, w_down, small_params, up_bias)
    firsts = (first_qkv, first_out, first_up, first_down, first_small, first_bias)
    seconds = (second_qkv, second_out, second_up, second_down, second_small, second_bias)
    results = []
    for weight, gradient, first, second, step_rate in zip(weights, averaged, firsts, seconds, learning_rates()):
        results.extend(adam_update(weight, factor * gradient, first, second, step_rate))
    output = outputs.reshape(TOKENS, D).astype(jnp.bfloat16)
    return (output, input_grad, grad_norm, results[0], results[1], results[2], results[3], results[4], results[5], results[6], results[7], results[8], results[9], results[10], results[11], results[12], results[13], results[14], results[15], results[16], results[17])
```

```python
import jax
import jax.numpy as jnp
from jax import lax
from jax.experimental import pallas as pl
from jax.experimental.pallas import tpu as pltpu
from jax.sharding import Mesh, PartitionSpec as P

HEAD_DIM = 64
FF = 3072
D = 768
SHORT = 257
LONG = 1025
STEP = 5

CLIP_NORM = 1.0
BETA_ONE = 0.9
BETA_TWO = 0.999
ADAM_EPS = 1e-08
DECAY = 0.03
NORM_EPS = 1e-05

LOG2E = 1.4426950408889634
MASK_ROOT = 2.0**20
CLASSES = 16
FORWARD_TILE = 384
BACKWARD_TILE = 256
KEY_TILE = 384

bf16 = jnp.bfloat16
ONCE = pl.Buffered(1)
NO_COST = pl.CostEstimate(flops=0, transcendentals=0, bytes_accessed=0)
VMEM = pl.BlockSpec(memory_space=pltpu.VMEM)
f32 = jnp.float32


def far(*arrays):
    return [pltpu.with_memory_space_constraint(array, pltpu.HBM) for array in arrays]


def dot_nn(left, right):
    return lax.dot_general(left, right, (((1,), (0,)), ((), ())), preferred_element_type=f32)


def dot_nt(left, right):
    return lax.dot_general(left, right, (((1,), (1,)), ((), ())), preferred_element_type=f32)


def dot_tn(left, right):
    return lax.dot_general(left, right, (((0,), (0,)), ((), ())), preferred_element_type=f32)


def dot_tt(left, right):
    return lax.dot_general(left, right, (((0,), (1,)), ((), ())), preferred_element_type=f32)


def attend_forward(plan, own, halo, query_class, key_class):
    _, heads, width, n_own = own.shape
    n_halo = halo.shape[-1]
    n_keys = n_own + n_halo
    tile, chunk = FORWARD_TILE, KEY_TILE
    n_tiles = n_own // tile
    block, half = n_own // 2, n_halo // 2

    def body(plan_ref, q_ref, own_k, own_v, halo_k, halo_v, qc_ref, kc_ref, out_ref, lse_ref, keys, values):
        step = pl.program_id(0)

        @pl.when(step == 0)
        def _():
            ones = (lax.broadcasted_iota(jnp.int32, (CLASSES, n_keys), 0) == 0).astype(bf16)
            for head in range(heads):
                for part in range(2):
                    to = pl.ds(pl.multiple_of(plan_ref[n_tiles + part, 0], 128), block)
                    cut = slice(part * block, (part + 1) * block)
                    values[head, :width, to] = own_v[head, :, cut]
                    keys[head, to, :width] = own_k[head, :, cut].T
                    to = pl.ds(pl.multiple_of(plan_ref[n_tiles + part, 1], 128), half)
                    cut = slice(part * half, (part + 1) * half)
                    values[head, :width, to] = halo_v[head, :, cut]
                    keys[head, to, :width] = halo_k[head, :, cut].T
                values[head, width:, :] = ones
                keys[head, :, width:] = kc_ref[...].T

        first = plan_ref[step, 0]
        scale = jnp.asarray(width**-0.5, bf16)
        queries = [jnp.concatenate([q_ref[h] * scale, qc_ref[...]], axis=0) for h in range(heads)]

        def one_chunk(index, carry):
            at = pl.ds(pl.multiple_of(first + index * chunk, 128), chunk)
            scores = [dot_nn(keys[h, at, :], queries[h]) for h in range(heads)]
            result = []
            for h in range(heads):
                top, total = carry[h]
                new_top = jnp.maximum(top, jnp.max(scores[h], axis=0, keepdims=True))
                probs = jnp.exp2((scores[h] - new_top) * LOG2E)
                fade = jnp.exp2((top - new_top) * LOG2E)
                result.append((new_top, total * fade + dot_nn(values[h, :, at], probs.astype(bf16))))
            return tuple(result)

        start = tuple(
            (jnp.full((1, tile), -3e38, f32), jnp.zeros((width + CLASSES, tile), f32)) for _ in range(heads)
        )
        ends = lax.fori_loop(0, plan_ref[step, 1], one_chunk, start)
        for h in range(heads):
            top, total = ends[h]
            row_sum = total[width : width + 1]
            out_ref[h] = (total[:width] / row_sum).astype(bf16)
            lse_ref[h] = top + jnp.log(row_sum)

    whole_own = lambda p: pl.BlockSpec((None, heads, width, n_own), lambda t, r: (p, 0, 0, 0), pipeline_mode=ONCE)
    whole_halo = lambda p: pl.BlockSpec((None, heads, width, n_halo), lambda t, r: (p, 0, 0, 0), pipeline_mode=ONCE)
    tiled = lambda rows: pl.BlockSpec((heads, rows, tile), lambda t, r: (0, 0, t))
    grid = pltpu.PrefetchScalarGridSpec(
        num_scalar_prefetch=1,
        grid=(n_tiles,),
        in_specs=[
            pl.BlockSpec((None, heads, width, tile), lambda t, r: (0, 0, 0, t)),
            whole_own(1),
            whole_own(2),
            whole_halo(0),
            whole_halo(1),
            pl.BlockSpec((CLASSES, tile), lambda t, r: (0, t)),
            pl.BlockSpec((CLASSES, n_keys), lambda t, r: (0, 0), pipeline_mode=ONCE),
        ],
        out_specs=[tiled(width), tiled(1)],
        scratch_shapes=[
            pltpu.VMEM((heads, n_keys, width + CLASSES), bf16),
            pltpu.VMEM((heads, width + CLASSES, n_keys), bf16),
        ],
    )
    return pl.pallas_call(
        body,
        grid_spec=grid,
        out_shape=(
            jax.ShapeDtypeStruct((heads, width, n_own), bf16),
            jax.ShapeDtypeStruct((heads, 1, n_own), f32),
        ),
        compiler_params=pltpu.CompilerParams(dimension_semantics=("arbitrary",), vmem_limit_bytes=20 << 20),
        cost_estimate=pl.CostEstimate(
            flops=8 * heads * n_own * 1152 * 64, transcendentals=heads * n_own * 1152, bytes_accessed=4 << 20
        ),
        name="attend_forward",
    )(plan, *far(own, own, own, halo, halo), query_class, key_class)


def attend_backward(plan, own, halo, query_class, key_class, attended, lse, grad):
    _, heads, width, n_own = own.shape
    n_halo = halo.shape[-1]
    n_keys = n_own + n_halo
    tile, chunk = BACKWARD_TILE, KEY_TILE
    n_tiles = n_own // tile
    block, half = n_own // 2, n_halo // 2
    scale = width**-0.5

    def body(
        plan_ref, q_ref, own_k, own_v, halo_k, halo_v, qc_ref, kc_ref, att_ref, lse_ref, grad_ref,
        own_out, halo_out, keys, keys_t, values, key_sum, value_sum,
    ):
        step = pl.program_id(0)

        def places(part):
            return (
                pl.ds(pl.multiple_of(plan_ref[n_tiles + part, 0], 128), block),
                slice(part * block, (part + 1) * block),
                pl.ds(pl.multiple_of(plan_ref[n_tiles + part, 1], 128), half),
                slice(part * half, (part + 1) * half),
            )

        @pl.when(step == 0)
        def _():
            for head in range(heads):
                for part in range(2):
                    to, cut, to_halo, cut_halo = places(part)
                    keys_t[head, :, to] = own_k[head, :, cut]
                    keys[head, to, :width] = own_k[head, :, cut].T
                    values[head, to, :] = own_v[head, :, cut].T
                    keys_t[head, :, to_halo] = halo_k[head, :, cut_halo]
                    keys[head, to_halo, :width] = halo_k[head, :, cut_halo].T
                    values[head, to_halo, :] = halo_v[head, :, cut_halo].T
                keys[head, :, width:] = kc_ref[...].T
            key_sum[...] = jnp.zeros_like(key_sum)
            value_sum[...] = jnp.zeros_like(value_sum)

        first = plan_ref[step, 0]
        scaled = [q_ref[h] * jnp.asarray(scale, bf16) for h in range(heads)]
        queries = [jnp.concatenate([scaled[h], qc_ref[...]], axis=0) for h in range(heads)]
        grads = [grad_ref[h] for h in range(heads)]
        logs = [lse_ref[h] * LOG2E for h in range(heads)]
        deltas = [
            jnp.sum(grads[h].astype(f32) * att_ref[h].astype(f32), axis=0, keepdims=True) for h in range(heads)
        ]

        def one_chunk(index, carry):
            at = pl.ds(pl.multiple_of(first + index * chunk, 128), chunk)
            scores = [dot_nn(keys[h, at, :], queries[h]) for h in range(heads)]
            grad_probs = [dot_nn(values[h, at, :], grads[h]) for h in range(heads)]
            result = []
            for h in range(heads):
                probs = jnp.exp2(scores[h] * LOG2E - logs[h])
                grad_scores = (probs * (grad_probs[h] - deltas[h])).astype(bf16)
                value_sum[h, :, at] += dot_nt(grads[h], probs.astype(bf16))
                key_sum[h, :, at] += dot_nt(scaled[h], grad_scores)
                result.append(carry[h] + dot_nn(keys_t[h, :, at], grad_scores))
            return tuple(result)

        start = tuple(jnp.zeros((width, tile), f32) for _ in range(heads))
        ends = lax.fori_loop(0, plan_ref[step, 1], one_chunk, start)
        at_tile = pl.ds(pl.multiple_of(step * tile, 128), tile)
        for h in range(heads):
            own_out[0, h, :, at_tile] = (ends[h] * scale).astype(bf16)

        @pl.when(step == n_tiles - 1)
        def _():
            for head in range(heads):
                for part in range(2):
                    to, cut, to_halo, cut_halo = places(part)
                    own_out[1, head, :, cut] = key_sum[head, :, to].astype(bf16)
                    own_out[2, head, :, cut] = value_sum[head, :, to].astype(bf16)
                    halo_out[0, head, :, cut_halo] = key_sum[head, :, to_halo].astype(bf16)
                    halo_out[1, head, :, cut_halo] = value_sum[head, :, to_halo].astype(bf16)

    whole_own = lambda p: pl.BlockSpec((None, heads, width, n_own), lambda t, r: (p, 0, 0, 0), pipeline_mode=ONCE)
    whole_halo = lambda p: pl.BlockSpec((None, heads, width, n_halo), lambda t, r: (p, 0, 0, 0), pipeline_mode=ONCE)
    tiled = lambda rows: pl.BlockSpec((heads, rows, tile), lambda t, r: (0, 0, t))
    grid = pltpu.PrefetchScalarGridSpec(
        num_scalar_prefetch=1,
        grid=(n_tiles,),
        in_specs=[
            pl.BlockSpec((None, heads, width, tile), lambda t, r: (0, 0, 0, t)),
            whole_own(1),
            whole_own(2),
            whole_halo(0),
            whole_halo(1),
            pl.BlockSpec((CLASSES, tile), lambda t, r: (0, t)),
            pl.BlockSpec((CLASSES, n_keys), lambda t, r: (0, 0), pipeline_mode=ONCE),
            tiled(width),
            tiled(1),
            tiled(width),
        ],
        out_specs=[
            pl.BlockSpec((3, heads, width, n_own), lambda t, r: (0, 0, 0, 0), pipeline_mode=ONCE),
            pl.BlockSpec((2, heads, width, n_halo), lambda t, r: (0, 0, 0, 0), pipeline_mode=ONCE),
        ],
        scratch_shapes=[
            pltpu.VMEM((heads, n_keys, width + CLASSES), bf16),
            pltpu.VMEM((heads, width, n_keys), bf16),
            pltpu.VMEM((heads, n_keys, width), bf16),
            pltpu.VMEM((heads, width, n_keys), f32),
            pltpu.VMEM((heads, width, n_keys), f32),
        ],
    )
    return pl.pallas_call(
        body,
        grid_spec=grid,
        out_shape=(
            pltpu.HBM((3, heads, width, n_own), bf16),
            pltpu.HBM((2, heads, width, n_halo), bf16),
        ),
        compiler_params=pltpu.CompilerParams(dimension_semantics=("arbitrary",), vmem_limit_bytes=20 << 20),
        cost_estimate=pl.CostEstimate(
            flops=20 * heads * n_own * 1152 * 64, transcendentals=heads * n_own * 1152, bytes_accessed=8 << 20
        ),
        name="attend_backward",
    )(plan, *far(own, own, own, halo, halo), query_class, key_class, *far(attended, lse, grad))


def attention_plan(item_ids, high, low, n_own, n_halo, tile):
    total = item_ids.shape[0]
    chunk = KEY_TILE
    n_keys = n_own + n_halo
    block, half = n_own // 2, n_halo // 2
    position = jnp.arange(total, dtype=jnp.int32)
    opens = jnp.concatenate([jnp.ones((1,), bool), item_ids[1:] != item_ids[:-1]])
    closes = jnp.concatenate([opens[1:], jnp.ones((1,), bool)])
    key_base = high * (total - n_keys)
    row_base = high * (total - n_own)
    starts = jnp.arange(0, total, tile, dtype=jnp.int32)[:, None]
    tile_first = jnp.max(jnp.where(opens & (position <= starts), position, 0), axis=1)
    tile_last = jnp.min(jnp.where(closes & (position >= starts + tile - 1), position + 1, total), axis=1)
    per_block = block // tile

    def local_tiles(values):
        mine = lax.dynamic_slice_in_dim(values, (row_base + low * block) // tile, per_block)
        other = lax.dynamic_slice_in_dim(values, (row_base + (1 - low) * block) // tile, per_block)
        return jnp.concatenate([mine, other]) - key_base

    begin = local_tiles(tile_first) // 128 * 128
    count = (local_tiles(tile_last) - begin + chunk - 1) // chunk
    begin = jnp.minimum(begin, n_keys - count * chunk)
    own_base = high * (n_keys - n_own)
    halo_base = (1 - high) * n_own
    offsets = jnp.stack(
        [
            jnp.stack([own_base + low * block, halo_base + low * half]),
            jnp.stack([own_base + (1 - low) * block, halo_base + (1 - low) * half]),
        ]
    )
    plan = jnp.concatenate([jnp.stack([begin, count], axis=1), offsets]).astype(jnp.int32)
    classes = jnp.arange(CLASSES, dtype=jnp.int32)[:, None] - 1
    row_ids = jnp.concatenate(
        [
            lax.dynamic_slice_in_dim(item_ids, row_base + low * block, block),
            lax.dynamic_slice_in_dim(item_ids, row_base + (1 - low) * block, block),
        ]
    )
    key_ids = lax.dynamic_slice_in_dim(item_ids, key_base, n_keys)
    query_class = jnp.where(row_ids[None] == classes, 0.0, -MASK_ROOT).astype(bf16)
    key_class = jnp.where(key_ids[None] == classes, MASK_ROOT, 0.0).astype(bf16)
    return plan, query_class, key_class


def layer_norm_parts(values, gain_row, shift_row):
    centre = values - jnp.mean(values, axis=-1, keepdims=True)
    inverse = lax.rsqrt(jnp.mean(centre * centre, axis=-1, keepdims=True) + NORM_EPS)
    unit_rows = centre * inverse
    return (unit_rows * gain_row + shift_row, unit_rows, inverse)


def norm_backward(upstream, unit_rows, inverse, gain_row):
    scaled = upstream * gain_row
    centred = scaled - jnp.mean(scaled, axis=-1, keepdims=True)
    return (centred - unit_rows * jnp.mean(scaled * unit_rows, axis=-1, keepdims=True)) * inverse


def adam_update(weight, gradient, first, second, step_rate):
    first_new = BETA_ONE * first + (1.0 - BETA_ONE) * gradient
    second_new = BETA_TWO * second + (1.0 - BETA_TWO) * gradient * gradient
    first_hat = first_new / (1.0 - BETA_ONE**STEP)
    second_hat = second_new / (1.0 - BETA_TWO**STEP)
    weight_new = weight - step_rate * (first_hat / (jnp.sqrt(second_hat) + ADAM_EPS) + DECAY * weight)
    return (weight_new, first_new, second_new)


def learning_rates():
    return (
        2.0 * D ** (-0.5),
        2.0 * max(D // SHORT, 1) ** (-0.5),
        2.0 * D ** (-0.5),
        2.0 * FF ** (-0.5),
        0.4,
        0.4,
    )


def swap(values, axis, stride=1):
    size = lax.axis_size(axis)
    return lax.ppermute(values, axis, [(i, i ^ stride) for i in range(size)])


def bits(axis):
    size = lax.axis_size(axis)
    return [1 << k for k in range(size.bit_length() - 1)]


def sum_all(values):
    for axis in ("lo", "hi", "dp"):
        for stride in bits(axis):
            values = values + swap(values, axis, stride)
    return values


def gather_rows(values, axis):
    index = lax.axis_index(axis)
    tail = values.shape
    held = values[None]
    for stride in reversed(bits(axis)):
        got = swap(held, axis, stride)
        upper = (index // stride) % 2 == 1
        held = jnp.stack([jnp.where(upper, got, held), jnp.where(upper, held, got)], axis=1)
        held = held.reshape((-1,) + tail)
    return held.reshape((-1,) + tail[1:])


def scatter_halves(held, axis, stride):
    upper = (lax.axis_index(axis) // stride) % 2
    pairs = held.reshape((-1, 2) + held.shape[1:])
    keep = lax.dynamic_index_in_dim(pairs, upper, 1, keepdims=False)
    send = lax.dynamic_index_in_dim(pairs, 1 - upper, 1, keepdims=False)
    return keep, send.astype(bf16)


def qkv_gradient_specs(down, halo_down, width, chunk):
    halo_chunks = halo_down.shape[1] // chunk
    near = lambda i, *p: (0, jnp.minimum(i, halo_chunks - 1))
    return [
        pl.BlockSpec((down.shape[0], chunk), lambda i, *p: (0, i)),
        pl.BlockSpec((chunk, width), lambda i, *p: (i, 0)),
        pl.BlockSpec((halo_down.shape[0], chunk), near),
        pl.BlockSpec((chunk, width), lambda i, *p: near(i)[::-1]),
    ]


def qkv_gradient_step(halo_chunks, down, own_rows, halo_down, halo_rows, total):
    step = pl.program_id(0)
    part = dot_nn(down[...], own_rows[...])
    total[...] = jnp.where(step == 0, part, total[...] + part)

    @pl.when(step < halo_chunks)
    def _():
        queries = down.shape[0] - halo_down.shape[0]
        total[queries:] += dot_nn(halo_down[...], halo_rows[...])


def qkv_gradient_sent(down, own_rows, halo_down, halo_rows):
    shape = (down.shape[0], own_rows.shape[1])
    chunk = 512
    halo_chunks = halo_down.shape[1] // chunk

    def body(*refs):
        qkv_gradient_step(halo_chunks, *refs[:4], refs[5])

        @pl.when(pl.program_id(0) == pl.num_programs(0) - 1)
        def _():
            refs[4][...] = refs[5][...].astype(bf16)

    return pl.pallas_call(
        body,
        grid=(down.shape[1] // chunk,),
        in_specs=qkv_gradient_specs(down, halo_down, shape[1], chunk),
        out_specs=pl.BlockSpec(shape, lambda i: (0, 0)),
        out_shape=pltpu.HBM(shape, bf16),
        scratch_shapes=[pltpu.VMEM(shape, f32)],
        compiler_params=pltpu.CompilerParams(dimension_semantics=("arbitrary",), vmem_limit_bytes=16 << 20),
        cost_estimate=NO_COST,
        name="qkv_gradient_sent",
    )(*far(down, own_rows, halo_down, halo_rows))


def qkv_gradient_split(upper, n_blocks, down, own_rows, halo_down, halo_rows, received):
    n_columns, width = received.shape
    rows = width // n_blocks
    chunk = 512
    halo_chunks = halo_down.shape[1] // chunk

    def body(upper_ref, *refs):
        qkv_gradient_step(halo_chunks, *refs[:4], refs[7])

        @pl.when(pl.program_id(0) == pl.num_programs(0) - 1)
        def _():
            turned = (refs[7][...] + refs[4][...].astype(f32)).T
            is_upper = upper_ref[0] == 1
            for i in range(n_blocks // 2):
                lower_rows = turned[2 * i * rows : (2 * i + 1) * rows]
                upper_rows = turned[(2 * i + 1) * rows : (2 * i + 2) * rows]
                refs[5][i] = jnp.where(is_upper, upper_rows, lower_rows)
                refs[6][i] = jnp.where(is_upper, lower_rows, upper_rows).astype(bf16)

    shape = (n_blocks // 2, rows, n_columns)
    whole = pl.BlockSpec(shape, lambda i, p: (0, 0, 0))
    grid = pltpu.PrefetchScalarGridSpec(
        num_scalar_prefetch=1,
        grid=(down.shape[1] // chunk,),
        in_specs=qkv_gradient_specs(down, halo_down, width, chunk)
        + [pl.BlockSpec((n_columns, width), lambda i, p: (0, 0))],
        out_specs=[whole, whole],
        scratch_shapes=[pltpu.VMEM((n_columns, width), f32)],
    )
    return pl.pallas_call(
        body,
        grid_spec=grid,
        out_shape=(pltpu.HBM(shape, f32), pltpu.HBM(shape, bf16)),
        compiler_params=pltpu.CompilerParams(dimension_semantics=("arbitrary",), vmem_limit_bytes=20 << 20),
        cost_estimate=NO_COST,
        name="qkv_gradient_split",
    )(upper, *far(down, own_rows, halo_down, halo_rows, received))


def rows_back(at, pairs, received=()):
    n_rows, width = at.stop - at.start, pairs[0][1].shape[0]
    columns = pairs[0][0].shape[0]
    tile = 256
    first = at.start // tile

    def body(*refs):
        total = refs[2 * len(pairs)][...] if received else None
        for k in range(len(pairs)):
            part = dot_nt(refs[2 * k][...].T, refs[2 * k + 1][...])
            total = part if total is None else total + part
        refs[-1][...] = total

    one_pair = [
        pl.BlockSpec((columns, tile), lambda i: (0, first + i)),
        pl.BlockSpec((width, columns), lambda i: (0, 0), pipeline_mode=ONCE),
    ]
    row_tile = pl.BlockSpec((tile, width), lambda i: (i, 0))
    return pl.pallas_call(
        body,
        grid=(n_rows // tile,),
        in_specs=one_pair * len(pairs) + [row_tile] * len(received),
        out_specs=row_tile,
        out_shape=jax.ShapeDtypeStruct((n_rows, width), f32),
        compiler_params=pltpu.CompilerParams(dimension_semantics=("arbitrary",), vmem_limit_bytes=16 << 20),
        cost_estimate=NO_COST,
        name="rows_back",
    )(*far(*(array for pair in pairs for array in pair), *received))


def feed_rows(place, hidden, rest, extra=()):
    n_rows, n_columns = hidden.shape
    n_ff = n_columns // 2
    width = rest.shape[1]
    tile = 256

    def body(place_ref, hidden_ref, own_ref, peer_ref, *refs):
        total = dot_nt(hidden_ref[:, :n_ff], own_ref[...]) + dot_nt(hidden_ref[:, n_ff:], peer_ref[...])
        if extra:
            total = refs[0][...].astype(f32) + total + refs[1][...] + refs[2][5:6, :]
        refs[-1][...] = total.astype(bf16)

    rows_of = lambda columns: pl.BlockSpec((tile, columns), lambda i, p: (i, 0))
    weight_of = lambda pick: pl.BlockSpec((None, width, n_ff), lambda i, p: (pick(p[0]), 0, 1), pipeline_mode=ONCE)
    extra_specs = [rows_of(width), rows_of(width), pl.BlockSpec((6, width), lambda i, p: (0, 0))] if extra else []
    grid = pltpu.PrefetchScalarGridSpec(
        num_scalar_prefetch=1,
        grid=(n_rows // tile,),
        in_specs=[rows_of(n_columns), weight_of(lambda h: h), weight_of(lambda h: 1 - h)] + extra_specs,
        out_specs=rows_of(width),
    )
    return pl.pallas_call(
        body,
        grid_spec=grid,
        out_shape=jax.ShapeDtypeStruct((n_rows, width), bf16),
        compiler_params=pltpu.CompilerParams(dimension_semantics=("arbitrary",), vmem_limit_bytes=16 << 20),
        cost_estimate=NO_COST,
        name="feed_rows",
    )(place, *far(hidden, rest, rest, *extra))


def first_norm_back(place, mine, other, pair, tokens, grad_mixed, small_params, early_sums):
    rows, width = tokens.shape
    half = mine.shape[0]
    gap = 2 * rows - 2 * half
    step = 128

    def body(place_ref, mine_ref, other_ref, pair_ref, tok_ref, mixed_ref, small_ref, early_ref, grad_ref, sum_ref, order):
        order[0:gap] = jnp.zeros((gap, width), bf16)
        order[gap + 2 * half :] = jnp.zeros((gap, width), bf16)
        first = pl.multiple_of(gap + place_ref[0] * half, 128)
        second = pl.multiple_of(gap + (1 - place_ref[0]) * half, 128)
        order[pl.ds(first, half)] = mine_ref[...]
        order[pl.ds(second, half)] = other_ref[...]
        take = place_ref[1]
        gain_row = small_ref[0:1, :]
        gain_sum = jnp.zeros((1, width), f32)
        shift_sum = jnp.zeros((1, width), f32)
        for k in range(0, rows, step):
            at = slice(k, k + step)
            back = pair_ref[at] + order[pl.ds(pl.multiple_of(take + k, 128), step)].astype(f32)
            _, unit_rows, inverse = layer_norm_parts(tok_ref[at].astype(f32), 1.0, 0.0)
            gain_sum = gain_sum + jnp.sum(back * unit_rows, axis=0, keepdims=True)
            shift_sum = shift_sum + jnp.sum(back, axis=0, keepdims=True)
            grad_ref[at] = mixed_ref[at] + norm_backward(back, unit_rows, inverse, gain_row)
        sum_ref[...] = early_ref[...]
        sum_ref[0:1, :] = gain_sum
        sum_ref[1:2, :] = shift_sum

    return pl.pallas_call(
        body,
        in_specs=[pl.BlockSpec(memory_space=pltpu.SMEM)] + [VMEM] * 7,
        out_specs=[VMEM, VMEM],
        out_shape=(jax.ShapeDtypeStruct((rows, width), f32), jax.ShapeDtypeStruct((16, width), f32)),
        scratch_shapes=[pltpu.VMEM((2 * gap + 2 * half, width), bf16)],
        compiler_params=pltpu.CompilerParams(vmem_limit_bytes=16 << 20),
        cost_estimate=NO_COST,
        name="first_norm_back",
    )(place, mine, other, pair, tokens, grad_mixed, small_params, early_sums)


def gelu_parts(values):
    normal_cdf = 0.5 * (1.0 + lax.erf(values * (0.5**0.5)))
    return values * normal_cdf, normal_cdf + values * (0.3989422804014327 * jnp.exp(-0.5 * values * values))


def feed_forward(place, rows_in, upstream, rest, bias):
    n_rows, width = rows_in.shape
    n_ff = bias.shape[2]
    tile = 256

    def body(place_ref, x_ref, u_ref, rest_ref, bias_ref, hid_ref, pre_ref, back_ref, sum_ref, xt_ref, ut_ref):
        step = pl.program_id(0)
        x = x_ref[...]
        u = u_ref[...]
        xt_ref[...] = x.T
        ut_ref[...] = u.T
        back = None
        for j in range(2):
            s = place_ref[0] if j == 0 else 1 - place_ref[0]
            columns = slice(j * n_ff, (j + 1) * n_ff)
            up = rest_ref[s, :, :n_ff]
            hidden, slope = gelu_parts(dot_nn(x, up) + bias_ref[s])
            hid_ref[:, columns] = hidden.astype(bf16)
            grad_pre = (dot_nn(u, rest_ref[s, :, n_ff : 2 * n_ff]) * slope).astype(bf16)
            pre_ref[:, columns] = grad_pre
            sums = jnp.sum(grad_pre.astype(f32), axis=0, keepdims=True)
            sum_ref[:, columns] = jnp.where(step == 0, sums, sum_ref[:, columns] + sums)
            part = dot_nt(grad_pre, up)
            back = part if back is None else back + part
        back_ref[...] = back

    by_row = lambda columns: pl.BlockSpec((tile, columns), lambda i, p: (i, 0))
    grid = pltpu.PrefetchScalarGridSpec(
        num_scalar_prefetch=1,
        grid=(n_rows // tile,),
        in_specs=[
            by_row(width),
            by_row(width),
            pl.BlockSpec(rest.shape, lambda i, p: (0, 0, 0), pipeline_mode=ONCE),
            pl.BlockSpec(bias.shape, lambda i, p: (0, 0, 0), pipeline_mode=ONCE),
        ],
        out_specs=[
            by_row(2 * n_ff),
            by_row(2 * n_ff),
            by_row(width),
            pl.BlockSpec((1, 2 * n_ff), lambda i, p: (0, 0)),
            pl.BlockSpec((width, tile), lambda i, p: (0, i)),
            pl.BlockSpec((width, tile), lambda i, p: (0, i)),
        ],
    )
    return pl.pallas_call(
        body,
        grid_spec=grid,
        out_shape=(
            pltpu.HBM((n_rows, 2 * n_ff), bf16),
            pltpu.HBM((n_rows, 2 * n_ff), bf16),
            pltpu.HBM((n_rows, width), f32),
            jax.ShapeDtypeStruct((1, 2 * n_ff), f32),
            pltpu.HBM((width, n_rows), bf16),
            pltpu.HBM((width, n_rows), bf16),
        ),
        compiler_params=pltpu.CompilerParams(dimension_semantics=("arbitrary",), vmem_limit_bytes=24 << 20),
        cost_estimate=NO_COST,
        name="feed_forward",
    )(place, *far(rows_in, upstream, rest), bias)


def weight_grads(twos, grad_pres, ups, hiddens, mixeds, flat):
    width, n_rows = twos[0].shape
    n_ff = hiddens[0].shape[1]
    n_out = flat.shape[0]
    block = 512
    per = n_ff // block

    def body(x0, x1, p0, p1, u0, u1, h0, h1, m0, m1, flat_ref, out_ref):
        step = pl.program_id(0)

        @pl.when(step < per)
        def _():
            out_ref[...] = (dot_nn(x0[...], p0[...]) + dot_nn(x1[...], p1[...])).astype(bf16)

        @pl.when((step >= per) & (step < 2 * per))
        def _():
            out_ref[...] = (dot_nn(u0[...], h0[...]) + dot_nn(u1[...], h1[...])).astype(bf16)

        @pl.when(step == 2 * per)
        def _():
            total = dot_nn(flat_ref[:, :n_rows], m0[...]) + dot_nn(flat_ref[:, n_rows:], m1[...])
            out_ref[:, :n_out] = total.T.astype(bf16)
            out_ref[:, n_out:] = jnp.zeros((width, block - n_out), bf16)

    whole = lambda array: pl.BlockSpec(array.shape, lambda i: (0, 0), pipeline_mode=ONCE)
    early = pl.BlockSpec((n_rows, block), lambda i: (0, jnp.minimum(i, per - 1)))
    late = pl.BlockSpec((n_rows, block), lambda i: (0, jnp.clip(i - per, 0, per - 1)))
    return pl.pallas_call(
        body,
        grid=(2 * per + 1,),
        in_specs=[whole(twos[0])] * 2
        + [early] * 2
        + [whole(ups[0])] * 2
        + [late] * 2
        + [whole(mixeds[0])] * 2
        + [whole(flat)],
        out_specs=pl.BlockSpec((width, block), lambda i: (0, i)),
        out_shape=pltpu.HBM((width, 2 * n_ff + block), bf16),
        compiler_params=pltpu.CompilerParams(dimension_semantics=("arbitrary",), vmem_limit_bytes=24 << 20),
        cost_estimate=NO_COST,
        name="weight_grads",
    )(*twos, *far(*grad_pres), *ups, *far(*hiddens), *mixeds, flat)


def attended_grads(mixed_own, mixed_other, full_out):
    n_rows, width = mixed_own.shape
    columns = full_out.shape[1] // 2

    def body(own_ref, other_ref, out_ref, *grads):
        turned = out_ref[...].T
        for j in range(2):
            part = turned[j * columns : (j + 1) * columns]
            grads[j][:, :n_rows] = dot_nt(part, own_ref[...]).astype(bf16)
            grads[j][:, n_rows:] = dot_nt(part, other_ref[...]).astype(bf16)

    shape = (columns, 2 * n_rows)
    return pl.pallas_call(
        body,
        in_specs=[VMEM] * 3,
        out_specs=[VMEM] * 2,
        out_shape=(jax.ShapeDtypeStruct(shape, bf16),) * 2,
        compiler_params=pltpu.CompilerParams(vmem_limit_bytes=12 << 20),
        cost_estimate=NO_COST,
        name="attended_grads",
    )(mixed_own, mixed_other, full_out)


def second_norm_back(place, pair, received, mixed, cotangent, keep_rows, small_params, bias_grad):
    rows, width = mixed.shape
    step = 128

    def body(place_ref, pair_ref, got_ref, mixed_ref, cot_ref, keep_ref, small_ref, bias_ref, grad_ref, low_ref, sum_ref):
        sums = [jnp.zeros((1, width), f32) for _ in range(4)]
        for k in range(0, rows, step):
            at = slice(k, k + step)
            back = pair_ref[at] + got_ref[at]
            upstream = cot_ref[at].astype(f32) * keep_ref[at]
            _, unit_rows, inverse = layer_norm_parts(mixed_ref[at], 1.0, 0.0)
            grad = upstream + norm_backward(back, unit_rows, inverse, small_ref[2:3, :])
            grad_ref[at] = grad
            low_ref[at] = grad.astype(bf16)
            for i, term in enumerate((back * unit_rows, back, grad, upstream)):
                sums[i] = sums[i] + jnp.sum(term, axis=0, keepdims=True)
        sum_ref[...] = jnp.zeros_like(sum_ref)
        for i in range(4):
            sum_ref[i + 2 : i + 3, :] = sums[i]
        for i in range(4):
            own = jnp.where(place_ref[0] == i, bias_ref[0:1, :width], jnp.zeros((1, width), f32))
            peer = jnp.where(place_ref[1] == i, bias_ref[0:1, width:], jnp.zeros((1, width), f32))
            sum_ref[i + 6 : i + 7, :] = own + peer

    return pl.pallas_call(
        body,
        in_specs=[pl.BlockSpec(memory_space=pltpu.SMEM)] + [VMEM] * 7,
        out_specs=[VMEM] * 3,
        out_shape=(
            jax.ShapeDtypeStruct((rows, width), f32),
            jax.ShapeDtypeStruct((rows, width), bf16),
            jax.ShapeDtypeStruct((16, width), f32),
        ),
        compiler_params=pltpu.CompilerParams(vmem_limit_bytes=16 << 20),
        name="second_norm_back",
    )(place, pair, received, mixed, cotangent, keep_rows, small_params, bias_grad)


def finish_grads(n_data, keep, got, reduced, from_peer, late_sums, n_ff):
    d_local = reduced.shape[0]
    n_out = from_peer.shape[1] - 2 * n_ff

    def body(keep_ref, got_ref, red_ref, peer_ref, sum_ref, qkv_ref, out_ref, up_ref, down_ref, total_ref):
        qkv = keep_ref[0] + got_ref[0].astype(f32)
        qkv_ref[...] = qkv
        squares = jnp.sum(jnp.square(qkv * (1.0 / n_data)), keepdims=True)
        for ref, at, peer_at, columns in (
            (up_ref, 0, 0, n_ff),
            (down_ref, 2 * n_ff, n_ff, n_ff),
            (out_ref, 4 * n_ff, 2 * n_ff, n_out),
        ):
            grad = red_ref[:, at : at + columns].astype(f32) + peer_ref[:, peer_at : peer_at + columns].astype(f32)
            ref[...] = grad
            squares = squares + jnp.sum(jnp.square(grad * (1.0 / n_data)), keepdims=True)
        total_ref[...] = sum_ref[...]
        total_ref[10:11, :] = jnp.broadcast_to(squares, (1, sum_ref.shape[1]))

    shapes = [(d_local, keep.shape[2]), (d_local, n_out), (d_local, n_ff), (d_local, n_ff), late_sums.shape]
    return pl.pallas_call(
        body,
        in_specs=[VMEM] * 5,
        out_specs=[VMEM] * 5,
        out_shape=tuple(jax.ShapeDtypeStruct(shape, f32) for shape in shapes),
        compiler_params=pltpu.CompilerParams(vmem_limit_bytes=8 << 20),
        name="finish_grads",
    )(keep, got, reduced, from_peer, late_sums)


def optimizer(n_data, summed, grads, states):
    rates = learning_rates()
    flat = [array for group in states for array in group]
    n_states = len(states)
    heads = grads[0].shape[1] // (3 * HEAD_DIM)

    def body(*refs):
        summed_ref = refs[0]
        grad_refs = refs[1:5]
        state_refs = refs[5 : 5 + 3 * n_states]
        norm_ref = refs[5 + 3 * n_states]
        out_refs = refs[6 + 3 * n_states :]
        small = summed_ref[0:10, :] * (1.0 / n_data)
        total = jnp.sum(small * small, keepdims=True) + summed_ref[10:11, 0:1]
        norm = jnp.sqrt(total)
        norm_ref[...] = norm
        factor = CLIP_NORM / jnp.maximum(norm, CLIP_NORM)

        def update(index, gradient, take=(slice(None), slice(None))):
            w, m, v = (ref[take] for ref in state_refs[3 * index : 3 * index + 3])
            results = adam_update(w, gradient * factor, m, v, rates[index])
            for ref, value in zip(out_refs[3 * index : 3 * index + 3], results):
                ref[take] = value

        for head in range(heads):
            pieces = [
                grad_refs[0][:, (part * heads + head) * HEAD_DIM : (part * heads + head + 1) * HEAD_DIM]
                for part in range(3)
            ]
            at = slice(3 * head * HEAD_DIM, 3 * (head + 1) * HEAD_DIM)
            update(0, jnp.concatenate(pieces, axis=1) * (1.0 / n_data), (slice(None), at))
        update(1, grad_refs[1][...].T * (1.0 / n_data))
        update(2, grad_refs[2][...] * (1.0 / n_data))
        update(3, grad_refs[3][...] * (1.0 / n_data))
        update(4, small[0:6])
        update(5, small[6:10])

    return pl.pallas_call(
        body,
        out_shape=(
            jax.ShapeDtypeStruct((1, 1), f32),
            *(jax.ShapeDtypeStruct(array.shape, f32) for array in flat),
        ),
        compiler_params=pltpu.CompilerParams(vmem_limit_bytes=16 << 20),
        name="optimizer",
    )(summed, *grads, *flat)


def body(
    tokens,
    cotangent,
    row_item,
    w_qkv,
    w_out,
    w_up,
    w_down,
    small_params,
    up_bias,
    first_qkv,
    first_out,
    first_up,
    first_down,
    first_small,
    first_bias,
    second_qkv,
    second_out,
    second_up,
    second_down,
    second_small,
    second_bias,
):
    rows = tokens.shape[0]
    n_data = lax.axis_size("dp")
    high = lax.axis_index("hi")
    low = lax.axis_index("lo")
    heads_local = w_qkv.shape[1] // (3 * HEAD_DIM)
    head_width = heads_local * HEAD_DIM
    ff_local = w_up.shape[1]
    d_local = w_qkv.shape[0]
    n_own = 2 * rows
    n_halo = LONG - 1
    half = n_halo // 2

    shard_qkv = (
        w_qkv.astype(bf16)
        .reshape(d_local, heads_local, 3, HEAD_DIM)
        .transpose(0, 2, 1, 3)
        .reshape(d_local, 3 * head_width)
    )
    shard_rest = jnp.concatenate([w_up.astype(bf16), w_down.astype(bf16).T, w_out.astype(bf16).T], axis=1)
    qkv_mine = gather_rows(shard_qkv, "dp")
    qkv_theirs = swap(qkv_mine, "hi")
    rest = lax.all_gather(shard_rest, ("hi", "dp"), axis=0, tiled=True).reshape(2, D, -1)
    outs = rest[:, :, 2 * ff_local :]
    full_out = jnp.concatenate(
        [
            lax.dynamic_index_in_dim(outs, high, 0, keepdims=False),
            lax.dynamic_index_in_dim(outs, 1 - high, 0, keepdims=False),
        ],
        axis=1,
    )

    group_row = (2 * high + low) * rows
    own_ids = lax.dynamic_slice_in_dim(row_item, group_row, rows)
    keep_rows = (own_ids >= 0).astype(f32)[:, None]
    residual = tokens.astype(f32)
    normed, _, _ = layer_norm_parts(residual, small_params[0], small_params[1])
    normed = normed.astype(bf16)
    normed_other = swap(normed, "lo")
    send_at = (1 - high) * (512 - 256 * low) + high * low * 1280
    send_rows = lax.dynamic_slice_in_dim(
        jnp.concatenate([normed, normed_other, normed], axis=0), send_at, half, axis=0
    )
    halo_mine = swap(send_rows, "hi")
    halo_other = swap(halo_mine, "lo")
    own_rows = jnp.concatenate([normed, normed_other], axis=0)
    halo_rows = jnp.concatenate([halo_mine, halo_other], axis=0)
    own_rows, halo_rows = lax.optimization_barrier((own_rows, halo_rows))
    plan, query_class, key_class = attention_plan(row_item, high, low, n_own, n_halo, FORWARD_TILE)
    plan_back, _, _ = attention_plan(row_item, high, low, n_own, n_halo, BACKWARD_TILE)

    upstream = cotangent.astype(f32) * keep_rows
    upstream_low = upstream.astype(bf16)
    upstream_low = lax.optimization_barrier(upstream_low)
    upstream_other = swap(upstream_low, "lo")

    def project(weight):
        own = dot_tt(weight, own_rows).astype(bf16).reshape(3, heads_local, HEAD_DIM, n_own)
        halo = dot_tt(weight[:, head_width:], halo_rows).astype(bf16).reshape(2, heads_local, HEAD_DIM, n_halo)
        return own, halo

    own_m, halo_m = project(qkv_mine)
    att_m, lse_m = attend_forward(plan, own_m, halo_m, query_class, key_class)
    qkv_theirs, att_m = lax.optimization_barrier((qkv_theirs, att_m))
    own_t, halo_t = project(qkv_theirs)
    att_t, lse_t = attend_forward(plan, own_t, halo_t, query_class, key_class)
    flat = jnp.concatenate([att_m, att_t], axis=0).reshape(2 * head_width, n_own)

    first_half, second_half = slice(0, rows), slice(rows, n_own)

    def reduce_pair(part, kind=f32):
        got = swap(part(second_half).astype(kind), "lo")
        return part(first_half).astype(f32) + got.astype(f32)

    attention_part = reduce_pair(lambda at: dot_tt(flat[:, at], full_out))
    mixed = residual + attention_part + small_params[4]
    normed_two, _, _ = layer_norm_parts(mixed, small_params[2], small_params[3])
    normed_two = normed_two.astype(bf16)
    two_other = swap(normed_two, "lo")
    bias_parts = up_bias.reshape(2, 2, ff_local)
    bias_pair = lax.dynamic_index_in_dim(bias_parts, low, 1, keepdims=False).reshape(2, 1, ff_local)
    half_place = high.astype(jnp.int32).reshape(1)
    hidden_o, pre_o, back_o, bias_o, two_t_o, up_t_o = feed_forward(half_place, two_other, upstream_other, rest, bias_pair)
    two_got = swap(back_o, "lo")
    hidden_m, pre_m, two_pair, bias_m, two_t_m, up_t_m = feed_forward(half_place, normed_two, upstream_low, rest, bias_pair)
    bias_grad = bias_m + bias_o
    bias_place = jnp.stack([2 * high + low, 2 * (1 - high) + low]).astype(jnp.int32)
    grad_mixed, mixed_low, early_sums = second_norm_back(
        bias_place, two_pair, two_got, mixed, cotangent, keep_rows, small_params, bias_grad
    )
    mixed_other = swap(mixed_low, "lo")
    att_grad_m, att_grad_t = attended_grads(mixed_low, mixed_other, full_out)
    att_grad_m = att_grad_m.reshape(heads_local, HEAD_DIM, n_own)
    att_grad_t = att_grad_t.reshape(heads_local, HEAD_DIM, n_own)
    grad_rest = weight_grads(
        (two_t_m, two_t_o), (pre_m, pre_o), (up_t_m, up_t_o), (hidden_m, hidden_o), (mixed_low, mixed_other), flat
    )
    grad_rest, att_grad_t = lax.optimization_barrier((grad_rest, att_grad_t))
    grad_rest = lax.psum_scatter(grad_rest, "dp", scatter_dimension=0, tiled=True)

    down_t, halo_down_t = attend_backward(
        plan_back, own_t, halo_t, query_class, key_class, att_t, lse_t, att_grad_t
    )
    down_t = down_t.reshape(3 * head_width, n_own)
    halo_down_t = halo_down_t.reshape(2 * head_width, n_halo)

    qkv_for_peer = qkv_gradient_sent(down_t, own_rows, halo_down_t, halo_rows)
    feed_other = feed_rows(half_place, hidden_o, rest)
    qkv_for_peer, feed_other, att_grad_m = lax.optimization_barrier((qkv_for_peer, feed_other, att_grad_m))
    qkv_from_peer = swap(qkv_for_peer, "hi")
    feed_got = swap(feed_other, "lo")
    down_m, halo_down_m = attend_backward(
        plan_back, own_m, halo_m, query_class, key_class, att_m, lse_m, att_grad_m
    )
    down_m, halo_down_m, qkv_from_peer, feed_got = lax.optimization_barrier(
        (down_m, halo_down_m, qkv_from_peer, feed_got)
    )
    down_m = down_m.reshape(3 * head_width, n_own)
    halo_down_m = halo_down_m.reshape(2 * head_width, n_halo)

    def halo_part(at):
        return dot_tt(halo_down_t[:, at], qkv_theirs[:, head_width:]) + dot_tt(
            halo_down_m[:, at], qkv_mine[:, head_width:]
        )

    strides = bits("dp")
    pairs = ((down_t, qkv_theirs), (down_m, qkv_mine))
    halo_got = swap(halo_part(slice(half, n_halo)), "lo")
    back_got = swap(rows_back(second_half, pairs), "lo")
    upper = (lax.axis_index("dp") % 2).astype(jnp.int32).reshape(1)
    keep, send = qkv_gradient_split(upper, n_data, down_m, own_rows, halo_down_m, halo_rows, qkv_from_peer)
    halo_send = (halo_part(slice(0, half)) + halo_got).astype(bf16)
    halo_send, send, down_m, hidden, back_got = lax.optimization_barrier(
        (halo_send, send, down_m, hidden_m, back_got)
    )
    got = swap(send, "dp", strides[0])
    back_mine = swap(halo_send, "hi")
    back_pair = rows_back(first_half, ((down_t, qkv_theirs), (down_m, qkv_mine)), (back_got,))
    output = feed_rows(half_place, hidden, rest, (feed_got, mixed, small_params))
    got, back_mine, back_pair, output = lax.optimization_barrier((got, back_mine, back_pair, output))
    keep, send = scatter_halves(keep + got.astype(f32), "dp", strides[1])
    got = swap(send, "dp", strides[1])
    back_other = swap(back_mine, "lo")
    theirs = jnp.concatenate(
        [
            grad_rest[:, ff_local : 2 * ff_local],
            grad_rest[:, 3 * ff_local : 4 * ff_local],
            grad_rest[:, 4 * ff_local + head_width : 4 * ff_local + 2 * head_width],
        ],
        axis=1,
    )
    got, back_other, theirs = lax.optimization_barrier((got, back_other, theirs))
    from_peer = swap(theirs, "hi")
    keep, send = scatter_halves(keep + got.astype(f32), "dp", strides[2])
    got = swap(send, "dp", strides[2])
    place = jnp.stack([low, high * (n_own - n_halo) + low * rows]).astype(jnp.int32)
    input_grad, late_sums = first_norm_back(
        place, back_mine, back_other, back_pair, tokens, grad_mixed, small_params, early_sums
    )
    got, late_sums, from_peer = lax.optimization_barrier((got, late_sums, from_peer))
    for stride in strides[3:]:
        keep, send = scatter_halves(keep + got.astype(f32), "dp", stride)
        got = swap(send, "dp", stride)
    *grads, summed = finish_grads(n_data, keep, got, grad_rest, from_peer, late_sums, ff_local)
    summed = sum_all(summed)
    norm, *updated = optimizer(
        n_data,
        summed,
        grads,
        (
            (w_qkv, first_qkv, second_qkv),
            (w_out, first_out, second_out),
            (w_up, first_up, second_up),
            (w_down.T, first_down.T, second_down.T),
            (small_params, first_small, second_small),
            (up_bias.reshape(4, ff_local), first_bias.reshape(4, ff_local), second_bias.reshape(4, ff_local)),
        ),
    )
    updated[9:12] = [array.T for array in updated[9:12]]
    updated[15:18] = [array.reshape(-1) for array in updated[15:18]]
    return (output, input_grad, norm[0, 0], *updated)


def solution(mesh):
    n_data, n_model = mesh.devices.shape
    split = Mesh(mesh.devices.reshape(n_data, 2, n_model // 2), ("dp", "hi", "lo"))
    model = ("hi", "lo")
    rows = P(("dp", "hi", "lo"), None)
    by_row = P("dp", model)
    by_column = P(model, "dp")
    states = (by_row, by_column, by_row, by_column, P(), P())
    in_specs = (rows, rows, P("dp"), *states, *states, *states)
    updated = []
    for spec in states:
        updated.extend([spec, spec, spec])
    out_specs = (rows, rows, P(), *updated)
    return jax.shard_map(body, mesh=split, in_specs=in_specs, out_specs=out_specs, check_vma=False)
```

```python
import jax
import jax.numpy as jnp
from jax import lax
from jax.experimental import pallas as pl
from jax.experimental.pallas import tpu as pltpu
from jax.sharding import Mesh, PartitionSpec as P

HEAD_DIM = 64
FF = 3072
D = 768
SHORT = 257
LONG = 1025
STEP = 5

CLIP_NORM = 1.0
BETA_ONE = 0.9
BETA_TWO = 0.999
ADAM_EPS = 1e-08
DECAY = 0.03
NORM_EPS = 1e-05

LOG2E = 1.4426950408889634
MASK_ROOT = 2.0**20
CLASSES = 16
FORWARD_TILE = 384
BACKWARD_TILE = 256
KEY_TILE = 384

bf16 = jnp.bfloat16
ONCE = pl.Buffered(1)
NO_COST = pl.CostEstimate(flops=0, transcendentals=0, bytes_accessed=0)
VMEM = pl.BlockSpec(memory_space=pltpu.VMEM)
f32 = jnp.float32


def far(*arrays):
    return [pltpu.with_memory_space_constraint(array, pltpu.HBM) for array in arrays]


def dot_nn(left, right):
    return lax.dot_general(left, right, (((1,), (0,)), ((), ())), preferred_element_type=f32)


def dot_nt(left, right):
    return lax.dot_general(left, right, (((1,), (1,)), ((), ())), preferred_element_type=f32)


def dot_tn(left, right):
    return lax.dot_general(left, right, (((0,), (0,)), ((), ())), preferred_element_type=f32)


def dot_tt(left, right):
    return lax.dot_general(left, right, (((0,), (1,)), ((), ())), preferred_element_type=f32)


def attend_forward(plan, own, halo, query_class, key_class):
    _, heads, width, n_own = own.shape
    n_halo = halo.shape[-1]
    n_keys = n_own + n_halo
    tile, chunk = FORWARD_TILE, KEY_TILE
    n_tiles = n_own // tile
    block, half = n_own // 2, n_halo // 2

    def body(plan_ref, q_ref, own_k, own_v, halo_k, halo_v, qc_ref, kc_ref, out_ref, lse_ref, keys, values):
        step = pl.program_id(0)

        @pl.when(step == 0)
        def _():
            ones = (lax.broadcasted_iota(jnp.int32, (CLASSES, n_keys), 0) == 0).astype(bf16)
            for head in range(heads):
                for part in range(2):
                    to = pl.ds(pl.multiple_of(plan_ref[n_tiles + part, 0], 128), block)
                    cut = slice(part * block, (part + 1) * block)
                    values[head, :width, to] = own_v[head, :, cut]
                    keys[head, to, :width] = own_k[head, :, cut].T
                    to = pl.ds(pl.multiple_of(plan_ref[n_tiles + part, 1], 128), half)
                    cut = slice(part * half, (part + 1) * half)
                    values[head, :width, to] = halo_v[head, :, cut]
                    keys[head, to, :width] = halo_k[head, :, cut].T
                values[head, width:, :] = ones
                keys[head, :, width:] = kc_ref[...].T

        first = plan_ref[step, 0]
        scale = jnp.asarray(width**-0.5, bf16)
        queries = [jnp.concatenate([q_ref[h] * scale, qc_ref[...]], axis=0) for h in range(heads)]

        def one_chunk(index, carry):
            at = pl.ds(pl.multiple_of(first + index * chunk, 128), chunk)
            scores = [dot_nn(keys[h, at, :], queries[h]) for h in range(heads)]
            result = []
            for h in range(heads):
                top, total = carry[h]
                new_top = jnp.maximum(top, jnp.max(scores[h], axis=0, keepdims=True))
                probs = jnp.exp2((scores[h] - new_top) * LOG2E)
                fade = jnp.exp2((top - new_top) * LOG2E)
                result.append((new_top, total * fade + dot_nn(values[h, :, at], probs.astype(bf16))))
            return tuple(result)

        start = tuple(
            (jnp.full((1, tile), -3e38, f32), jnp.zeros((width + CLASSES, tile), f32)) for _ in range(heads)
        )
        ends = lax.fori_loop(0, plan_ref[step, 1], one_chunk, start)
        for h in range(heads):
            top, total = ends[h]
            row_sum = total[width : width + 1]
            out_ref[h] = (total[:width] / row_sum).astype(bf16)
            lse_ref[h] = top + jnp.log(row_sum)

    whole_own = lambda p: pl.BlockSpec((None, heads, width, n_own), lambda t, r: (p, 0, 0, 0), pipeline_mode=ONCE)
    whole_halo = lambda p: pl.BlockSpec((None, heads, width, n_halo), lambda t, r: (p, 0, 0, 0), pipeline_mode=ONCE)
    tiled = lambda rows: pl.BlockSpec((heads, rows, tile), lambda t, r: (0, 0, t))
    grid = pltpu.PrefetchScalarGridSpec(
        num_scalar_prefetch=1,
        grid=(n_tiles,),
        in_specs=[
            pl.BlockSpec((None, heads, width, tile), lambda t, r: (0, 0, 0, t)),
            whole_own(1),
            whole_own(2),
            whole_halo(0),
            whole_halo(1),
            pl.BlockSpec((CLASSES, tile), lambda t, r: (0, t)),
            pl.BlockSpec((CLASSES, n_keys), lambda t, r: (0, 0), pipeline_mode=ONCE),
        ],
        out_specs=[tiled(width), tiled(1)],
        scratch_shapes=[
            pltpu.VMEM((heads, n_keys, width + CLASSES), bf16),
            pltpu.VMEM((heads, width + CLASSES, n_keys), bf16),
        ],
    )
    return pl.pallas_call(
        body,
        grid_spec=grid,
        out_shape=(
            jax.ShapeDtypeStruct((heads, width, n_own), bf16),
            jax.ShapeDtypeStruct((heads, 1, n_own), f32),
        ),
        compiler_params=pltpu.CompilerParams(dimension_semantics=("arbitrary",), vmem_limit_bytes=20 << 20),
        cost_estimate=pl.CostEstimate(
            flops=8 * heads * n_own * 1152 * 64, transcendentals=heads * n_own * 1152, bytes_accessed=4 << 20
        ),
        name="attend_forward",
    )(plan, own, own, own, halo, halo, query_class, key_class)


def attend_backward(plan, own, halo, query_class, key_class, attended, lse, grad, place=list):
    _, heads, width, n_own = own.shape
    n_halo = halo.shape[-1]
    n_keys = n_own + n_halo
    tile, chunk = BACKWARD_TILE, KEY_TILE
    n_tiles = n_own // tile
    block, half = n_own // 2, n_halo // 2
    scale = width**-0.5

    def body(
        plan_ref, q_ref, own_k, own_v, halo_k, halo_v, qc_ref, kc_ref, att_ref, lse_ref, grad_ref,
        own_out, halo_out, keys, keys_t, values, key_sum, value_sum,
    ):
        step = pl.program_id(0)

        def places(part):
            return (
                pl.ds(pl.multiple_of(plan_ref[n_tiles + part, 0], 128), block),
                slice(part * block, (part + 1) * block),
                pl.ds(pl.multiple_of(plan_ref[n_tiles + part, 1], 128), half),
                slice(part * half, (part + 1) * half),
            )

        @pl.when(step == 0)
        def _():
            for head in range(heads):
                for part in range(2):
                    to, cut, to_halo, cut_halo = places(part)
                    keys_t[head, :, to] = own_k[head, :, cut]
                    keys[head, to, :width] = own_k[head, :, cut].T
                    values[head, to, :] = own_v[head, :, cut].T
                    keys_t[head, :, to_halo] = halo_k[head, :, cut_halo]
                    keys[head, to_halo, :width] = halo_k[head, :, cut_halo].T
                    values[head, to_halo, :] = halo_v[head, :, cut_halo].T
                keys[head, :, width:] = kc_ref[...].T
            key_sum[...] = jnp.zeros_like(key_sum)
            value_sum[...] = jnp.zeros_like(value_sum)

        first = plan_ref[step, 0]
        scaled = [q_ref[h] * jnp.asarray(scale, bf16) for h in range(heads)]
        queries = [jnp.concatenate([scaled[h], qc_ref[...]], axis=0) for h in range(heads)]
        grads = [grad_ref[h] for h in range(heads)]
        logs = [lse_ref[h] * LOG2E for h in range(heads)]
        deltas = [
            jnp.sum(grads[h].astype(f32) * att_ref[h].astype(f32), axis=0, keepdims=True) for h in range(heads)
        ]

        def one_chunk(index, carry):
            at = pl.ds(pl.multiple_of(first + index * chunk, 128), chunk)
            scores = [dot_nn(keys[h, at, :], queries[h]) for h in range(heads)]
            grad_probs = [dot_nn(values[h, at, :], grads[h]) for h in range(heads)]
            result = []
            for h in range(heads):
                probs = jnp.exp2(scores[h] * LOG2E - logs[h])
                grad_scores = (probs * (grad_probs[h] - deltas[h])).astype(bf16)
                value_sum[h, :, at] += dot_nt(grads[h], probs.astype(bf16))
                key_sum[h, :, at] += dot_nt(scaled[h], grad_scores)
                result.append(carry[h] + dot_nn(keys_t[h, :, at], grad_scores))
            return tuple(result)

        start = tuple(jnp.zeros((width, tile), f32) for _ in range(heads))
        ends = lax.fori_loop(0, plan_ref[step, 1], one_chunk, start)
        at_tile = pl.ds(pl.multiple_of(step * tile, 128), tile)
        for h in range(heads):
            own_out[0, h, :, at_tile] = (ends[h] * scale).astype(bf16)

        @pl.when(step == n_tiles - 1)
        def _():
            for head in range(heads):
                for part in range(2):
                    to, cut, to_halo, cut_halo = places(part)
                    own_out[1, head, :, cut] = key_sum[head, :, to].astype(bf16)
                    own_out[2, head, :, cut] = value_sum[head, :, to].astype(bf16)
                    halo_out[0, head, :, cut_halo] = key_sum[head, :, to_halo].astype(bf16)
                    halo_out[1, head, :, cut_halo] = value_sum[head, :, to_halo].astype(bf16)

    whole_own = lambda p: pl.BlockSpec((None, heads, width, n_own), lambda t, r: (p, 0, 0, 0), pipeline_mode=ONCE)
    whole_halo = lambda p: pl.BlockSpec((None, heads, width, n_halo), lambda t, r: (p, 0, 0, 0), pipeline_mode=ONCE)
    tiled = lambda rows: pl.BlockSpec((heads, rows, tile), lambda t, r: (0, 0, t))
    grid = pltpu.PrefetchScalarGridSpec(
        num_scalar_prefetch=1,
        grid=(n_tiles,),
        in_specs=[
            pl.BlockSpec((None, heads, width, tile), lambda t, r: (0, 0, 0, t)),
            whole_own(1),
            whole_own(2),
            whole_halo(0),
            whole_halo(1),
            pl.BlockSpec((CLASSES, tile), lambda t, r: (0, t)),
            pl.BlockSpec((CLASSES, n_keys), lambda t, r: (0, 0), pipeline_mode=ONCE),
            tiled(width),
            tiled(1),
            tiled(width),
        ],
        out_specs=[
            pl.BlockSpec((3, heads, width, n_own), lambda t, r: (0, 0, 0, 0), pipeline_mode=ONCE),
            pl.BlockSpec((2, heads, width, n_halo), lambda t, r: (0, 0, 0, 0), pipeline_mode=ONCE),
        ],
        scratch_shapes=[
            pltpu.VMEM((heads, n_keys, width + CLASSES), bf16),
            pltpu.VMEM((heads, width, n_keys), bf16),
            pltpu.VMEM((heads, n_keys, width), bf16),
            pltpu.VMEM((heads, width, n_keys), f32),
            pltpu.VMEM((heads, width, n_keys), f32),
        ],
    )
    return pl.pallas_call(
        body,
        grid_spec=grid,
        out_shape=(
            pltpu.HBM((3, heads, width, n_own), bf16),
            pltpu.HBM((2, heads, width, n_halo), bf16),
        ),
        compiler_params=pltpu.CompilerParams(dimension_semantics=("arbitrary",), vmem_limit_bytes=20 << 20),
        cost_estimate=pl.CostEstimate(
            flops=20 * heads * n_own * 1152 * 64, transcendentals=heads * n_own * 1152, bytes_accessed=8 << 20
        ),
        name="attend_backward",
    )(plan, *place((own, own, own, halo, halo)), query_class, key_class, *place((attended, lse, grad)))


def attention_plan(item_ids, high, low, n_own, n_halo, tile):
    total = item_ids.shape[0]
    chunk = KEY_TILE
    n_keys = n_own + n_halo
    block, half = n_own // 2, n_halo // 2
    position = jnp.arange(total, dtype=jnp.int32)
    opens = jnp.concatenate([jnp.ones((1,), bool), item_ids[1:] != item_ids[:-1]])
    closes = jnp.concatenate([opens[1:], jnp.ones((1,), bool)])
    key_base = high * (total - n_keys)
    row_base = high * (total - n_own)
    starts = jnp.arange(0, total, tile, dtype=jnp.int32)[:, None]
    tile_first = jnp.max(jnp.where(opens & (position <= starts), position, 0), axis=1)
    tile_last = jnp.min(jnp.where(closes & (position >= starts + tile - 1), position + 1, total), axis=1)
    per_block = block // tile

    def local_tiles(values):
        mine = lax.dynamic_slice_in_dim(values, (row_base + low * block) // tile, per_block)
        other = lax.dynamic_slice_in_dim(values, (row_base + (1 - low) * block) // tile, per_block)
        return jnp.concatenate([mine, other]) - key_base

    begin = local_tiles(tile_first) // 128 * 128
    count = (local_tiles(tile_last) - begin + chunk - 1) // chunk
    begin = jnp.minimum(begin, n_keys - count * chunk)
    own_base = high * (n_keys - n_own)
    halo_base = (1 - high) * n_own
    offsets = jnp.stack(
        [
            jnp.stack([own_base + low * block, halo_base + low * half]),
            jnp.stack([own_base + (1 - low) * block, halo_base + (1 - low) * half]),
        ]
    )
    plan = jnp.concatenate([jnp.stack([begin, count], axis=1), offsets]).astype(jnp.int32)
    classes = jnp.arange(CLASSES, dtype=jnp.int32)[:, None] - 1
    row_ids = jnp.concatenate(
        [
            lax.dynamic_slice_in_dim(item_ids, row_base + low * block, block),
            lax.dynamic_slice_in_dim(item_ids, row_base + (1 - low) * block, block),
        ]
    )
    key_ids = lax.dynamic_slice_in_dim(item_ids, key_base, n_keys)
    query_class = jnp.where(row_ids[None] == classes, 0.0, -MASK_ROOT).astype(bf16)
    key_class = jnp.where(key_ids[None] == classes, MASK_ROOT, 0.0).astype(bf16)
    return plan, query_class, key_class


def layer_norm_parts(values, gain_row, shift_row):
    centre = values - jnp.mean(values, axis=-1, keepdims=True)
    inverse = lax.rsqrt(jnp.mean(centre * centre, axis=-1, keepdims=True) + NORM_EPS)
    unit_rows = centre * inverse
    return (unit_rows * gain_row + shift_row, unit_rows, inverse)


def norm_backward(upstream, unit_rows, inverse, gain_row):
    scaled = upstream * gain_row
    centred = scaled - jnp.mean(scaled, axis=-1, keepdims=True)
    return (centred - unit_rows * jnp.mean(scaled * unit_rows, axis=-1, keepdims=True)) * inverse


def adam_update(weight, gradient, first, second, step_rate):
    first_new = BETA_ONE * first + (1.0 - BETA_ONE) * gradient
    second_new = BETA_TWO * second + (1.0 - BETA_TWO) * gradient * gradient
    first_hat = first_new / (1.0 - BETA_ONE**STEP)
    second_hat = second_new / (1.0 - BETA_TWO**STEP)
    weight_new = weight - step_rate * (first_hat / (jnp.sqrt(second_hat) + ADAM_EPS) + DECAY * weight)
    return (weight_new, first_new, second_new)


def learning_rates():
    return (
        2.0 * D ** (-0.5),
        2.0 * max(D // SHORT, 1) ** (-0.5),
        2.0 * D ** (-0.5),
        2.0 * FF ** (-0.5),
        0.4,
        0.4,
    )


def swap(values, axis, stride=1):
    size = lax.axis_size(axis)
    return lax.ppermute(values, axis, [(i, i ^ stride) for i in range(size)])


def bits(axis):
    size = lax.axis_size(axis)
    return [1 << k for k in range(size.bit_length() - 1)]


def sum_all(values):
    for axis in ("lo", "hi", "dp"):
        for stride in bits(axis):
            values = values + swap(values, axis, stride)
    return values


def gather_rows(values, axis):
    index = lax.axis_index(axis)
    tail = values.shape
    held = values[None]
    for stride in reversed(bits(axis)):
        got = swap(held, axis, stride)
        upper = (index // stride) % 2 == 1
        held = jnp.stack([jnp.where(upper, got, held), jnp.where(upper, held, got)], axis=1)
        held = held.reshape((-1,) + tail)
    return held.reshape((-1,) + tail[1:])


def scatter_halves(held, axis, stride):
    upper = (lax.axis_index(axis) // stride) % 2
    pairs = held.reshape((-1, 2) + held.shape[1:])
    keep = lax.dynamic_index_in_dim(pairs, upper, 1, keepdims=False)
    send = lax.dynamic_index_in_dim(pairs, 1 - upper, 1, keepdims=False)
    return keep, send.astype(bf16)


def head_gradient_specs(down, halo_down, flat, width):
    chunk, near = down.shape[1] // 2, halo_down.shape[1] // 2
    whole = pl.BlockSpec((chunk, width), lambda i, *p: (0, 0), pipeline_mode=ONCE)
    return [
        pl.BlockSpec((down.shape[0], chunk), lambda i, *p: (0, i)),
        pl.BlockSpec((chunk, width), lambda i, *p: (i, 0)),
        pl.BlockSpec((halo_down.shape[0], near), lambda i, *p: (0, i)),
        pl.BlockSpec((near, width), lambda i, *p: (i, 0)),
        pl.BlockSpec((flat.shape[0], chunk), lambda i, *p: (0, i)),
        whole,
        whole,
    ]


def head_gradient_step(down, own_rows, halo_down, halo_rows, flat, mixed_own, mixed_other, total):
    step = pl.program_id(0)
    columns = down.shape[0]
    queries = columns - halo_down.shape[0]
    own = dot_nn(down[...], own_rows[...])
    halo = dot_nn(halo_down[...], halo_rows[...])

    @pl.when(step == 0)
    def _():
        total[:queries] = own[:queries]
        total[queries:columns] = own[queries:] + halo
        total[columns:] = dot_nn(flat[...], mixed_own[...])

    @pl.when(step == 1)
    def _():
        total[:queries] += own[:queries]
        total[queries:columns] += own[queries:] + halo
        total[columns:] += dot_nn(flat[...], mixed_other[...])


def head_gradient_sent(down, own_rows, halo_down, halo_rows, flat, mixed_own, mixed_other):
    width = own_rows.shape[1]
    shape = (down.shape[0] + flat.shape[0], width)

    def body(*refs):
        head_gradient_step(*refs[:7], refs[8])

        @pl.when(pl.program_id(0) == 1)
        def _():
            refs[7][...] = refs[8][...].astype(bf16)

    return pl.pallas_call(
        body,
        grid=(2,),
        in_specs=head_gradient_specs(down, halo_down, flat, width),
        out_specs=pl.BlockSpec(shape, lambda i: (0, 0)),
        out_shape=pltpu.HBM(shape, bf16),
        scratch_shapes=[pltpu.VMEM(shape, f32)],
        compiler_params=pltpu.CompilerParams(dimension_semantics=("arbitrary",), vmem_limit_bytes=24 << 20),
        cost_estimate=NO_COST,
        name="head_gradient_sent",
    )(*far(down), own_rows, *far(halo_down), halo_rows, flat, mixed_own, mixed_other)


def head_gradient_split(upper, n_blocks, operands, received):
    n_columns, width = received.shape
    rows = width // n_blocks
    down, _, halo_down, _, flat, _, _ = operands

    def body(upper_ref, *refs):
        head_gradient_step(*refs[:7], refs[10])

        @pl.when(pl.program_id(0) == 1)
        def _():
            turned = (refs[10][...] + refs[7][...].astype(f32)).T
            is_upper = upper_ref[0] == 1
            for i in range(n_blocks // 2):
                lower_rows = turned[2 * i * rows : (2 * i + 1) * rows]
                upper_rows = turned[(2 * i + 1) * rows : (2 * i + 2) * rows]
                refs[8][i] = jnp.where(is_upper, upper_rows, lower_rows)
                refs[9][i] = jnp.where(is_upper, lower_rows, upper_rows).astype(bf16)

    shape = (n_blocks // 2, rows, n_columns)
    whole = pl.BlockSpec(shape, lambda i, p: (0, 0, 0))
    grid = pltpu.PrefetchScalarGridSpec(
        num_scalar_prefetch=1,
        grid=(2,),
        in_specs=head_gradient_specs(down, halo_down, flat, width)
        + [pl.BlockSpec((n_columns, width), lambda i, p: (0, 0))],
        out_specs=[whole, whole],
        scratch_shapes=[pltpu.VMEM((n_columns, width), f32)],
    )
    return pl.pallas_call(
        body,
        grid_spec=grid,
        out_shape=(pltpu.HBM(shape, f32), pltpu.HBM(shape, bf16)),
        compiler_params=pltpu.CompilerParams(dimension_semantics=("arbitrary",), vmem_limit_bytes=28 << 20),
        cost_estimate=NO_COST,
        name="head_gradient_split",
    )(upper, *far(down), operands[1], *far(halo_down), *operands[3:], received)


def rows_back(at, pairs, received=()):
    n_rows, width = at.stop - at.start, pairs[0][1].shape[0]
    columns = pairs[0][0].shape[0]
    tile = 256
    first = at.start // tile

    def body(*refs):
        total = refs[2 * len(pairs)][...] if received else None
        for k in range(len(pairs)):
            part = dot_nt(refs[2 * k][...].T, refs[2 * k + 1][...])
            total = part if total is None else total + part
        refs[-1][...] = total

    one_pair = [
        pl.BlockSpec((columns, tile), lambda i: (0, first + i)),
        pl.BlockSpec((width, columns), lambda i: (0, 0), pipeline_mode=ONCE),
    ]
    row_tile = pl.BlockSpec((tile, width), lambda i: (i, 0))
    return pl.pallas_call(
        body,
        grid=(n_rows // tile,),
        in_specs=one_pair * len(pairs) + [row_tile] * len(received),
        out_specs=row_tile,
        out_shape=jax.ShapeDtypeStruct((n_rows, width), f32),
        compiler_params=pltpu.CompilerParams(dimension_semantics=("arbitrary",), vmem_limit_bytes=16 << 20),
        cost_estimate=NO_COST,
        name="rows_back",
    )(*far(*(array for pair in pairs for array in pair)), *received)


def feed_rows(place, hidden, rest, extra=()):
    n_rows, n_columns = hidden.shape
    n_ff = n_columns // 2
    width = rest.shape[1]
    tile = 256

    def body(place_ref, hidden_ref, own_ref, peer_ref, *refs):
        total = dot_nt(hidden_ref[:, :n_ff], own_ref[...]) + dot_nt(hidden_ref[:, n_ff:], peer_ref[...])
        if extra:
            total = refs[0][...].astype(f32) + total + refs[1][...] + refs[2][5:6, :]
        refs[-1][...] = total.astype(bf16)

    rows_of = lambda columns: pl.BlockSpec((tile, columns), lambda i, p: (i, 0))
    weight_of = lambda pick: pl.BlockSpec((None, width, n_ff), lambda i, p: (pick(p[0]), 0, 1), pipeline_mode=ONCE)
    extra_specs = [rows_of(width), rows_of(width), pl.BlockSpec((6, width), lambda i, p: (0, 0))] if extra else []
    grid = pltpu.PrefetchScalarGridSpec(
        num_scalar_prefetch=1,
        grid=(n_rows // tile,),
        in_specs=[rows_of(n_columns), weight_of(lambda h: h), weight_of(lambda h: 1 - h)] + extra_specs,
        out_specs=rows_of(width),
    )
    return pl.pallas_call(
        body,
        grid_spec=grid,
        out_shape=jax.ShapeDtypeStruct((n_rows, width), bf16),
        compiler_params=pltpu.CompilerParams(dimension_semantics=("arbitrary",), vmem_limit_bytes=16 << 20),
        cost_estimate=NO_COST,
        name="feed_rows",
    )(place, *far(hidden, rest, rest, *extra))


def first_norm_back(place, mine, other, pair, tokens, grad_mixed, small_params, early_sums):
    rows, width = tokens.shape
    half = mine.shape[0]
    gap = 2 * rows - 2 * half
    step = 128

    def body(place_ref, mine_ref, other_ref, pair_ref, tok_ref, mixed_ref, small_ref, early_ref, grad_ref, sum_ref, order):
        order[0:gap] = jnp.zeros((gap, width), bf16)
        order[gap + 2 * half :] = jnp.zeros((gap, width), bf16)
        first = pl.multiple_of(gap + place_ref[0] * half, 128)
        second = pl.multiple_of(gap + (1 - place_ref[0]) * half, 128)
        order[pl.ds(first, half)] = mine_ref[...]
        order[pl.ds(second, half)] = other_ref[...]
        take = place_ref[1]
        gain_row = small_ref[0:1, :]
        gain_sum = jnp.zeros((1, width), f32)
        shift_sum = jnp.zeros((1, width), f32)
        for k in range(0, rows, step):
            at = slice(k, k + step)
            back = pair_ref[at] + order[pl.ds(pl.multiple_of(take + k, 128), step)].astype(f32)
            _, unit_rows, inverse = layer_norm_parts(tok_ref[at].astype(f32), 1.0, 0.0)
            gain_sum = gain_sum + jnp.sum(back * unit_rows, axis=0, keepdims=True)
            shift_sum = shift_sum + jnp.sum(back, axis=0, keepdims=True)
            grad_ref[at] = mixed_ref[at] + norm_backward(back, unit_rows, inverse, gain_row)
        sum_ref[...] = early_ref[...]
        sum_ref[0:1, :] = gain_sum
        sum_ref[1:2, :] = shift_sum

    return pl.pallas_call(
        body,
        in_specs=[pl.BlockSpec(memory_space=pltpu.SMEM)] + [VMEM] * 7,
        out_specs=[VMEM, VMEM],
        out_shape=(jax.ShapeDtypeStruct((rows, width), f32), jax.ShapeDtypeStruct((16, width), f32)),
        scratch_shapes=[pltpu.VMEM((2 * gap + 2 * half, width), bf16)],
        compiler_params=pltpu.CompilerParams(vmem_limit_bytes=16 << 20),
        cost_estimate=NO_COST,
        name="first_norm_back",
    )(place, mine, other, pair, tokens, grad_mixed, small_params, early_sums)


def gelu_parts(values):
    normal_cdf = 0.5 * (1.0 + lax.erf(values * (0.5**0.5)))
    return values * normal_cdf, normal_cdf + values * (0.3989422804014327 * jnp.exp(-0.5 * values * values))


def feed_forward(place, rows_in, upstream, rest, bias, with_feed):
    n_rows, width = rows_in.shape
    n_ff = bias.shape[2]
    tile = 256

    def body(place_ref, x_ref, u_ref, rest_ref, bias_ref, hid_ref, pre_ref, back_ref, sum_ref, xt_ref, ut_ref, *feed):
        step = pl.program_id(0)
        x = x_ref[...]
        u = u_ref[...]
        xt_ref[...] = x.T
        ut_ref[...] = u.T
        back = fed = None
        for j in range(2):
            s = place_ref[0] if j == 0 else 1 - place_ref[0]
            columns = slice(j * n_ff, (j + 1) * n_ff)
            up = rest_ref[s, :, :n_ff]
            down = rest_ref[s, :, n_ff : 2 * n_ff]
            hidden, slope = gelu_parts(dot_nn(x, up) + bias_ref[s])
            hidden = hidden.astype(bf16)
            hid_ref[:, columns] = hidden
            grad_pre = (dot_nn(u, down) * slope).astype(bf16)
            if with_feed:
                part = dot_nt(hidden, down)
                fed = part if fed is None else fed + part
            pre_ref[:, columns] = grad_pre
            sums = jnp.sum(grad_pre.astype(f32), axis=0, keepdims=True)
            sum_ref[:, columns] = jnp.where(step == 0, sums, sum_ref[:, columns] + sums)
            part = dot_nt(grad_pre, up)
            back = part if back is None else back + part
        back_ref[...] = back
        if with_feed:
            feed[0][...] = fed.astype(bf16)

    by_row = lambda columns: pl.BlockSpec((tile, columns), lambda i, p: (i, 0))
    grid = pltpu.PrefetchScalarGridSpec(
        num_scalar_prefetch=1,
        grid=(n_rows // tile,),
        in_specs=[
            by_row(width),
            by_row(width),
            pl.BlockSpec(rest.shape, lambda i, p: (0, 0, 0), pipeline_mode=ONCE),
            pl.BlockSpec(bias.shape, lambda i, p: (0, 0, 0), pipeline_mode=ONCE),
        ],
        out_specs=[
            by_row(2 * n_ff),
            by_row(2 * n_ff),
            by_row(width),
            pl.BlockSpec((1, 2 * n_ff), lambda i, p: (0, 0)),
            pl.BlockSpec((width, tile), lambda i, p: (0, i)),
            pl.BlockSpec((width, tile), lambda i, p: (0, i)),
        ]
        + [by_row(width)] * with_feed,
    )
    return pl.pallas_call(
        body,
        grid_spec=grid,
        out_shape=(
            pltpu.HBM((n_rows, 2 * n_ff), bf16),
            pltpu.HBM((n_rows, 2 * n_ff), bf16),
            jax.ShapeDtypeStruct((n_rows, width), f32),
            jax.ShapeDtypeStruct((1, 2 * n_ff), f32),
            pltpu.HBM((width, n_rows), bf16),
            pltpu.HBM((width, n_rows), bf16),
        )
        + (jax.ShapeDtypeStruct((n_rows, width), bf16),) * with_feed,
        compiler_params=pltpu.CompilerParams(dimension_semantics=("arbitrary",), vmem_limit_bytes=20 << 20),
        cost_estimate=NO_COST,
        name="feed_forward",
    )(place, rows_in, upstream, *far(rest), bias)


def weight_grads(twos, grad_pres, ups, hiddens):
    width, n_rows = twos[0].shape
    n_ff = hiddens[0].shape[1]
    block = 512
    per = n_ff // block

    def body(x0, x1, p0, p1, u0, u1, h0, h1, out_ref):
        step = pl.program_id(0)

        @pl.when(step < per)
        def _():
            out_ref[...] = (dot_nn(x0[...], p0[...]) + dot_nn(x1[...], p1[...])).astype(bf16)

        @pl.when(step >= per)
        def _():
            out_ref[...] = (dot_nn(u0[...], h0[...]) + dot_nn(u1[...], h1[...])).astype(bf16)

    whole = lambda array: pl.BlockSpec(array.shape, lambda i: (0, 0), pipeline_mode=ONCE)
    early = pl.BlockSpec((n_rows, block), lambda i: (0, jnp.minimum(i, per - 1)))
    late = pl.BlockSpec((n_rows, block), lambda i: (0, jnp.clip(i - per, 0, per - 1)))
    return pl.pallas_call(
        body,
        grid=(2 * per,),
        in_specs=[whole(twos[0])] * 2 + [early] * 2 + [whole(ups[0])] * 2 + [late] * 2,
        out_specs=pl.BlockSpec((width, block), lambda i: (0, i)),
        out_shape=pltpu.HBM((width, 2 * n_ff), bf16),
        compiler_params=pltpu.CompilerParams(dimension_semantics=("arbitrary",), vmem_limit_bytes=16 << 20),
        cost_estimate=NO_COST,
        name="weight_grads",
    )(*twos, *far(*grad_pres), *ups, *far(*hiddens))


def attended_grads(mixed_own, mixed_other, full_out):
    n_rows, width = mixed_own.shape
    columns = full_out.shape[1] // 2

    def body(own_ref, other_ref, out_ref, *grads):
        turned = out_ref[...].T
        for j in range(2):
            part = turned[j * columns : (j + 1) * columns]
            grads[j][:, :n_rows] = dot_nt(part, own_ref[...]).astype(bf16)
            grads[j][:, n_rows:] = dot_nt(part, other_ref[...]).astype(bf16)

    shape = (columns, 2 * n_rows)
    return pl.pallas_call(
        body,
        in_specs=[VMEM] * 3,
        out_specs=[VMEM] * 2,
        out_shape=(jax.ShapeDtypeStruct(shape, bf16),) * 2,
        compiler_params=pltpu.CompilerParams(vmem_limit_bytes=12 << 20),
        cost_estimate=NO_COST,
        name="attended_grads",
    )(mixed_own, mixed_other, full_out)


def second_norm_back(place, pair, received, mixed, upstream_low, small_params, bias_grad):
    rows, width = mixed.shape
    step = 128

    def body(place_ref, pair_ref, got_ref, mixed_ref, up_ref, small_ref, bias_ref, grad_ref, low_ref, sum_ref):
        sums = [jnp.zeros((1, width), f32) for _ in range(4)]
        for k in range(0, rows, step):
            at = slice(k, k + step)
            back = pair_ref[at] + got_ref[at]
            upstream = up_ref[at].astype(f32)
            _, unit_rows, inverse = layer_norm_parts(mixed_ref[at], 1.0, 0.0)
            grad = upstream + norm_backward(back, unit_rows, inverse, small_ref[2:3, :])
            grad_ref[at] = grad
            low_ref[at] = grad.astype(bf16)
            for i, term in enumerate((back * unit_rows, back, grad, upstream)):
                sums[i] = sums[i] + jnp.sum(term, axis=0, keepdims=True)
        sum_ref[...] = jnp.zeros_like(sum_ref)
        for i in range(4):
            sum_ref[i + 2 : i + 3, :] = sums[i]
        for i in range(4):
            own = jnp.where(place_ref[0] == i, bias_ref[0:1, :width], jnp.zeros((1, width), f32))
            peer = jnp.where(place_ref[1] == i, bias_ref[0:1, width:], jnp.zeros((1, width), f32))
            sum_ref[i + 6 : i + 7, :] = own + peer

    return pl.pallas_call(
        body,
        in_specs=[pl.BlockSpec(memory_space=pltpu.SMEM)] + [VMEM] * 6,
        out_specs=[VMEM] * 3,
        out_shape=(
            jax.ShapeDtypeStruct((rows, width), f32),
            jax.ShapeDtypeStruct((rows, width), bf16),
            jax.ShapeDtypeStruct((16, width), f32),
        ),
        compiler_params=pltpu.CompilerParams(vmem_limit_bytes=16 << 20),
        name="second_norm_back",
    )(place, pair, received, mixed, upstream_low, small_params, bias_grad)


def finish_grads(n_data, keep, got, reduced, from_peer, late_sums, n_qkv):
    d_local = reduced.shape[0]
    n_ff = from_peer.shape[1] // 2
    n_out = keep.shape[2] - n_qkv

    def body(keep_ref, got_ref, red_ref, peer_ref, sum_ref, qkv_ref, out_ref, up_ref, down_ref, total_ref):
        heads_grad = keep_ref[0] + got_ref[0].astype(f32)
        qkv_ref[...] = heads_grad[:, :n_qkv]
        out_ref[...] = heads_grad[:, n_qkv:]
        squares = jnp.sum(jnp.square(heads_grad * (1.0 / n_data)), keepdims=True)
        for ref, at, peer_at in ((up_ref, 0, 0), (down_ref, 2 * n_ff, n_ff)):
            grad = red_ref[:, at : at + n_ff].astype(f32) + peer_ref[:, peer_at : peer_at + n_ff].astype(f32)
            ref[...] = grad
            squares = squares + jnp.sum(jnp.square(grad * (1.0 / n_data)), keepdims=True)
        total_ref[...] = sum_ref[...]
        total_ref[10:11, :] = jnp.broadcast_to(squares, (1, sum_ref.shape[1]))

    shapes = [(d_local, n_qkv), (d_local, n_out), (d_local, n_ff), (d_local, n_ff), late_sums.shape]
    return pl.pallas_call(
        body,
        in_specs=[VMEM] * 5,
        out_specs=[VMEM] * 5,
        out_shape=tuple(jax.ShapeDtypeStruct(shape, f32) for shape in shapes),
        compiler_params=pltpu.CompilerParams(vmem_limit_bytes=8 << 20),
        name="finish_grads",
    )(keep, got, reduced, from_peer, late_sums)


def optimizer(n_data, summed, grads, states):
    rates = learning_rates()
    flat = [array for group in states for array in group]
    n_states = len(states)
    heads = grads[0].shape[1] // (3 * HEAD_DIM)

    def body(*refs):
        summed_ref = refs[0]
        grad_refs = refs[1:5]
        state_refs = refs[5 : 5 + 3 * n_states]
        norm_ref = refs[5 + 3 * n_states]
        out_refs = refs[6 + 3 * n_states :]
        small = summed_ref[0:10, :] * (1.0 / n_data)
        total = jnp.sum(small * small, keepdims=True) + summed_ref[10:11, 0:1]
        norm = jnp.sqrt(total)
        norm_ref[...] = norm
        factor = CLIP_NORM / jnp.maximum(norm, CLIP_NORM)

        def update(index, gradient, take=(slice(None), slice(None))):
            w, m, v = (ref[take] for ref in state_refs[3 * index : 3 * index + 3])
            results = adam_update(w, gradient * factor, m, v, rates[index])
            for ref, value in zip(out_refs[3 * index : 3 * index + 3], results):
                ref[take] = value

        for head in range(heads):
            pieces = [
                grad_refs[0][:, (part * heads + head) * HEAD_DIM : (part * heads + head + 1) * HEAD_DIM]
                for part in range(3)
            ]
            at = slice(3 * head * HEAD_DIM, 3 * (head + 1) * HEAD_DIM)
            update(0, jnp.concatenate(pieces, axis=1) * (1.0 / n_data), (slice(None), at))
        update(1, grad_refs[1][...].T * (1.0 / n_data))
        update(2, grad_refs[2][...] * (1.0 / n_data))
        update(3, grad_refs[3][...] * (1.0 / n_data))
        update(4, small[0:6])
        lanes = 128
        bias_grads = [
            small[6 + row : 7 + row, k * lanes : (k + 1) * lanes]
            for row in range(4)
            for k in range(small.shape[1] // lanes)
        ]
        update(5, jnp.concatenate(bias_grads, axis=0))

    whole = lambda array: pl.BlockSpec(array.shape, lambda i: (0,) * len(array.shape))
    return pl.pallas_call(
        body,
        grid=(1,),
        in_specs=[whole(array) for array in (summed, *grads, *flat)],
        out_specs=[pl.BlockSpec((1, 1), lambda i: (0, 0))] + [whole(array) for array in flat],
        out_shape=(
            jax.ShapeDtypeStruct((1, 1), f32),
            *(jax.ShapeDtypeStruct(array.shape, f32) for array in flat),
        ),
        compiler_params=pltpu.CompilerParams(vmem_limit_bytes=16 << 20),
        name="optimizer",
    )(summed, *grads, *flat)


def body(
    tokens,
    cotangent,
    row_item,
    w_qkv,
    w_out,
    w_up,
    w_down,
    small_params,
    up_bias,
    first_qkv,
    first_out,
    first_up,
    first_down,
    first_small,
    first_bias,
    second_qkv,
    second_out,
    second_up,
    second_down,
    second_small,
    second_bias,
):
    rows = tokens.shape[0]
    n_data = lax.axis_size("dp")
    high = lax.axis_index("hi")
    low = lax.axis_index("lo")
    heads_local = w_qkv.shape[1] // (3 * HEAD_DIM)
    head_width = heads_local * HEAD_DIM
    ff_local = w_up.shape[1]
    d_local = w_qkv.shape[0]
    n_own = 2 * rows
    n_halo = LONG - 1
    half = n_halo // 2

    shard_qkv = (
        w_qkv.astype(bf16)
        .reshape(d_local, heads_local, 3, HEAD_DIM)
        .transpose(0, 2, 1, 3)
        .reshape(d_local, 3 * head_width)
    )
    shard_rest = jnp.concatenate([w_up.astype(bf16), w_down.astype(bf16).T, w_out.astype(bf16).T], axis=1)
    qkv_mine = gather_rows(shard_qkv, "dp")
    rest = lax.all_gather(shard_rest, ("hi", "dp"), axis=0, tiled=True).reshape(2, D, -1)
    outs = rest[:, :, 2 * ff_local :]
    full_out = jnp.concatenate(
        [
            lax.dynamic_index_in_dim(outs, high, 0, keepdims=False),
            lax.dynamic_index_in_dim(outs, 1 - high, 0, keepdims=False),
        ],
        axis=1,
    )

    group_row = (2 * high + low) * rows
    own_ids = lax.dynamic_slice_in_dim(row_item, group_row, rows)
    keep_rows = (own_ids >= 0).astype(f32)[:, None]
    residual = tokens.astype(f32)
    normed, _, _ = layer_norm_parts(residual, small_params[0], small_params[1])
    normed = normed.astype(bf16)
    normed_other = swap(normed, "lo")
    send_at = (1 - high) * (512 - 256 * low) + high * low * 1280
    send_rows = lax.dynamic_slice_in_dim(
        jnp.concatenate([normed, normed_other, normed], axis=0), send_at, half, axis=0
    )
    halo_mine = swap(send_rows, "hi")
    halo_other = swap(halo_mine, "lo")
    own_rows = jnp.concatenate([normed, normed_other], axis=0)
    halo_rows = jnp.concatenate([halo_mine, halo_other], axis=0)
    plan, query_class, key_class = attention_plan(row_item, high, low, n_own, n_halo, FORWARD_TILE)
    plan_back, _, _ = attention_plan(row_item, high, low, n_own, n_halo, BACKWARD_TILE)

    upstream = cotangent.astype(f32) * keep_rows
    upstream_low = upstream.astype(bf16)
    upstream_low, qkv_mine = lax.optimization_barrier((upstream_low, qkv_mine))
    upstream_other = swap(upstream_low, "lo")
    own_rows, halo_rows = lax.optimization_barrier((own_rows, halo_rows))
    qkv_theirs = swap(qkv_mine, "hi")

    def project(weight):
        own = dot_tt(weight, own_rows).astype(bf16).reshape(3, heads_local, HEAD_DIM, n_own)
        halo = dot_tt(weight[:, head_width:], halo_rows).astype(bf16).reshape(2, heads_local, HEAD_DIM, n_halo)
        return own, halo

    own_m, halo_m = project(qkv_mine)
    att_m, lse_m = attend_forward(plan, own_m, halo_m, query_class, key_class)
    qkv_theirs, att_m = lax.optimization_barrier((qkv_theirs, att_m))
    own_t, halo_t = project(qkv_theirs)
    att_t, lse_t = attend_forward(plan, own_t, halo_t, query_class, key_class)
    flat = jnp.concatenate([att_m, att_t], axis=0).reshape(2 * head_width, n_own)

    first_half, second_half = slice(0, rows), slice(rows, n_own)

    def reduce_pair(part, kind=f32):
        got = swap(part(second_half).astype(kind), "lo")
        return part(first_half).astype(f32) + got.astype(f32)

    attention_part = reduce_pair(lambda at: dot_tt(flat[:, at], full_out))
    mixed = residual + attention_part + small_params[4]
    normed_two, _, _ = layer_norm_parts(mixed, small_params[2], small_params[3])
    normed_two = normed_two.astype(bf16)
    two_other = swap(normed_two, "lo")
    bias_parts = up_bias.reshape(2, 2, ff_local)
    bias_pair = lax.dynamic_index_in_dim(bias_parts, low, 1, keepdims=False).reshape(2, 1, ff_local)
    half_place = high.astype(jnp.int32).reshape(1)
    hidden_o, pre_o, back_o, bias_o, two_t_o, up_t_o, feed_other = feed_forward(
        half_place, two_other, upstream_other, rest, bias_pair, True
    )
    normed_two, back_o, feed_other = lax.optimization_barrier((normed_two, back_o, feed_other))
    two_got = swap(back_o, "lo")
    feed_got = swap(feed_other, "lo")
    hidden_m, pre_m, two_pair, bias_m, two_t_m, up_t_m = feed_forward(
        half_place, normed_two, upstream_low, rest, bias_pair, False
    )
    bias_grad = bias_m + bias_o
    bias_place = jnp.stack([2 * high + low, 2 * (1 - high) + low]).astype(jnp.int32)
    grad_mixed, mixed_low, early_sums = second_norm_back(
        bias_place, two_pair, two_got, mixed, upstream_low, small_params, bias_grad
    )
    mixed_other = swap(mixed_low, "lo")
    grad_rest = weight_grads((two_t_m, two_t_o), (pre_m, pre_o), (up_t_m, up_t_o), (hidden_m, hidden_o))
    grad_rest, mixed_other = lax.optimization_barrier((grad_rest, mixed_other))
    grad_rest = lax.psum_scatter(grad_rest, "dp", scatter_dimension=0, tiled=True)
    att_grad_m, att_grad_t = attended_grads(mixed_low, mixed_other, full_out)
    att_grad_m = att_grad_m.reshape(heads_local, HEAD_DIM, n_own)
    att_grad_t = att_grad_t.reshape(heads_local, HEAD_DIM, n_own)

    down_t, halo_down_t = attend_backward(
        plan_back, own_t, halo_t, query_class, key_class, att_t, lse_t, att_grad_t
    )
    down_t = down_t.reshape(3 * head_width, n_own)
    halo_down_t = halo_down_t.reshape(2 * head_width, n_halo)

    flat_m, flat_t = flat[:head_width], flat[head_width:]
    qkv_for_peer = head_gradient_sent(
        down_t, own_rows, halo_down_t, halo_rows, flat_t, mixed_low, mixed_other
    )
    qkv_for_peer, att_grad_m = lax.optimization_barrier((qkv_for_peer, att_grad_m))
    qkv_from_peer = swap(qkv_for_peer, "hi")
    down_m, halo_down_m = attend_backward(
        plan_back, own_m, halo_m, query_class, key_class, att_m, lse_m, att_grad_m, lambda arrays: far(*arrays)
    )
    down_m = down_m.reshape(3 * head_width, n_own)
    halo_down_m = halo_down_m.reshape(2 * head_width, n_halo)

    def halo_part(at):
        return dot_tt(halo_down_t[:, at], qkv_theirs[:, head_width:]) + dot_tt(
            halo_down_m[:, at], qkv_mine[:, head_width:]
        )

    strides = bits("dp")
    pairs = ((down_t, qkv_theirs), (down_m, qkv_mine))
    halo_got = swap(halo_part(slice(half, n_halo)), "lo")
    back_sent = rows_back(second_half, pairs)
    back_sent, qkv_from_peer = lax.optimization_barrier((back_sent, qkv_from_peer))
    back_got = swap(back_sent, "lo")
    upper = (lax.axis_index("dp") % 2).astype(jnp.int32).reshape(1)
    operands = (down_m, own_rows, halo_down_m, halo_rows, flat_m, mixed_low, mixed_other)
    keep, send = head_gradient_split(upper, n_data, operands, qkv_from_peer)
    halo_send = (halo_part(slice(0, half)) + halo_got).astype(bf16)
    halo_send, send, down_m, hidden, back_got = lax.optimization_barrier(
        (halo_send, send, down_m, hidden_m, back_got)
    )
    got = swap(send, "dp", strides[0])
    back_mine = swap(halo_send, "hi")
    back_pair = rows_back(first_half, ((down_t, qkv_theirs), (down_m, qkv_mine)), (back_got,))
    output = feed_rows(half_place, hidden, rest, (feed_got, mixed, small_params))
    got, back_pair, output = lax.optimization_barrier((got, back_pair, output))
    keep, send = scatter_halves(keep + got.astype(f32), "dp", strides[1])
    send, back_mine = lax.optimization_barrier((send, back_mine))
    got = swap(send, "dp", strides[1])
    back_other = swap(back_mine, "lo")
    theirs = jnp.concatenate(
        [grad_rest[:, ff_local : 2 * ff_local], grad_rest[:, 3 * ff_local : 4 * ff_local]], axis=1
    )
    back_other, theirs = lax.optimization_barrier((back_other, theirs))
    from_peer = swap(theirs, "hi")
    place = jnp.stack([low, high * (n_own - n_halo) + low * rows]).astype(jnp.int32)
    input_grad, late_sums = first_norm_back(
        place, back_mine, back_other, back_pair, tokens, grad_mixed, small_params, early_sums
    )
    got, late_sums = lax.optimization_barrier((got, late_sums))
    for stride in strides[2:]:
        keep, send = scatter_halves(keep + got.astype(f32), "dp", stride)
        got = swap(send, "dp", stride)
    *grads, summed = finish_grads(n_data, keep, got, grad_rest, from_peer, late_sums, 3 * head_width)
    summed = sum_all(summed)
    norm, *updated = optimizer(
        n_data,
        summed,
        grads,
        (
            (w_qkv, first_qkv, second_qkv),
            (w_out, first_out, second_out),
            (w_up, first_up, second_up),
            (w_down.T, first_down.T, second_down.T),
            (small_params, first_small, second_small),
            tuple(array.reshape(-1, 128) for array in (up_bias, first_bias, second_bias)),
        ),
    )
    updated[9:12] = [array.T for array in updated[9:12]]
    updated[15:18] = [array.reshape(-1) for array in updated[15:18]]
    return (output, input_grad, norm[0, 0], *updated)


def solution(mesh):
    n_data, n_model = mesh.devices.shape
    split = Mesh(mesh.devices.reshape(n_data, 2, n_model // 2), ("dp", "hi", "lo"))
    model = ("hi", "lo")
    rows = P(("dp", "hi", "lo"), None)
    by_row = P("dp", model)
    by_column = P(model, "dp")
    states = (by_row, by_column, by_row, by_column, P(), P())
    in_specs = (rows, rows, P("dp"), *states, *states, *states)
    updated = []
    for spec in states:
        updated.extend([spec, spec, spec])
    out_specs = (rows, rows, P(), *updated)
    return jax.shard_map(body, mesh=split, in_specs=in_specs, out_specs=out_specs, check_vma=False)
```

```python
import jax
import jax.numpy as jnp
from jax import lax
from jax.experimental import pallas as pl
from jax.experimental.pallas import tpu as pltpu
from jax.sharding import Mesh, PartitionSpec as P

HEAD_DIM = 64
FF = 3072
D = 768
SHORT = 257
LONG = 1025
STEP = 5

CLIP_NORM = 1.0
BETA_ONE = 0.9
BETA_TWO = 0.999
ADAM_EPS = 1e-08
DECAY = 0.03
NORM_EPS = 1e-05

LOG2E = 1.4426950408889634
MASK_ROOT = 2.0**20
CLASSES = 16
FORWARD_TILE = 384
BACKWARD_TILE = 256
KEY_TILE = 384

bf16 = jnp.bfloat16
ONCE = pl.Buffered(1)
NO_COST = pl.CostEstimate(flops=0, transcendentals=0, bytes_accessed=0)
VMEM = pl.BlockSpec(memory_space=pltpu.VMEM)
f32 = jnp.float32


def far(*arrays):
    return [pltpu.with_memory_space_constraint(array, pltpu.HBM) for array in arrays]


def dot_nn(left, right):
    return lax.dot_general(left, right, (((1,), (0,)), ((), ())), preferred_element_type=f32)


def dot_nt(left, right):
    return lax.dot_general(left, right, (((1,), (1,)), ((), ())), preferred_element_type=f32)


def dot_tn(left, right):
    return lax.dot_general(left, right, (((0,), (0,)), ((), ())), preferred_element_type=f32)


def dot_tt(left, right):
    return lax.dot_general(left, right, (((0,), (1,)), ((), ())), preferred_element_type=f32)


def attend_forward(plan, own, halo, query_class, key_class):
    _, heads, width, n_own = own.shape
    n_halo = halo.shape[-1]
    n_keys = n_own + n_halo
    tile, chunk = FORWARD_TILE, KEY_TILE
    n_tiles = n_own // tile
    block, half = n_own // 2, n_halo // 2

    def body(plan_ref, q_ref, own_k, own_v, halo_k, halo_v, qc_ref, kc_ref, out_ref, lse_ref, keys, values):
        step = pl.program_id(0)

        @pl.when(step == 0)
        def _():
            ones = (lax.broadcasted_iota(jnp.int32, (CLASSES, n_keys), 0) == 0).astype(bf16)
            for head in range(heads):
                for part in range(2):
                    to = pl.ds(pl.multiple_of(plan_ref[n_tiles + part, 0], 128), block)
                    cut = slice(part * block, (part + 1) * block)
                    values[head, :width, to] = own_v[head, :, cut]
                    keys[head, to, :width] = own_k[head, :, cut].T
                    to = pl.ds(pl.multiple_of(plan_ref[n_tiles + part, 1], 128), half)
                    cut = slice(part * half, (part + 1) * half)
                    values[head, :width, to] = halo_v[head, :, cut]
                    keys[head, to, :width] = halo_k[head, :, cut].T
                values[head, width:, :] = ones
                keys[head, :, width:] = kc_ref[...].T

        first = plan_ref[step, 0]
        scale = jnp.asarray(width**-0.5, bf16)
        queries = [jnp.concatenate([q_ref[h] * scale, qc_ref[...]], axis=0) for h in range(heads)]

        def one_chunk(index, carry):
            at = pl.ds(pl.multiple_of(first + index * chunk, 128), chunk)
            scores = [dot_nn(keys[h, at, :], queries[h]) for h in range(heads)]
            result = []
            for h in range(heads):
                top, total = carry[h]
                new_top = jnp.maximum(top, jnp.max(scores[h], axis=0, keepdims=True))
                probs = jnp.exp2((scores[h] - new_top) * LOG2E)
                fade = jnp.exp2((top - new_top) * LOG2E)
                result.append((new_top, total * fade + dot_nn(values[h, :, at], probs.astype(bf16))))
            return tuple(result)

        start = tuple(
            (jnp.full((1, tile), -3e38, f32), jnp.zeros((width + CLASSES, tile), f32)) for _ in range(heads)
        )
        ends = lax.fori_loop(0, plan_ref[step, 1], one_chunk, start)
        for h in range(heads):
            top, total = ends[h]
            row_sum = total[width : width + 1]
            out_ref[h] = (total[:width] / row_sum).astype(bf16)
            lse_ref[h] = top + jnp.log(row_sum)

    whole_own = lambda p: pl.BlockSpec((None, heads, width, n_own), lambda t, r: (p, 0, 0, 0), pipeline_mode=ONCE)
    whole_halo = lambda p: pl.BlockSpec((None, heads, width, n_halo), lambda t, r: (p, 0, 0, 0), pipeline_mode=ONCE)
    tiled = lambda rows: pl.BlockSpec((heads, rows, tile), lambda t, r: (0, 0, t))
    grid = pltpu.PrefetchScalarGridSpec(
        num_scalar_prefetch=1,
        grid=(n_tiles,),
        in_specs=[
            pl.BlockSpec((None, heads, width, tile), lambda t, r: (0, 0, 0, t)),
            whole_own(1),
            whole_own(2),
            whole_halo(0),
            whole_halo(1),
            pl.BlockSpec((CLASSES, tile), lambda t, r: (0, t)),
            pl.BlockSpec((CLASSES, n_keys), lambda t, r: (0, 0), pipeline_mode=ONCE),
        ],
        out_specs=[tiled(width), tiled(1)],
        scratch_shapes=[
            pltpu.VMEM((heads, n_keys, width + CLASSES), bf16),
            pltpu.VMEM((heads, width + CLASSES, n_keys), bf16),
        ],
    )
    return pl.pallas_call(
        body,
        grid_spec=grid,
        out_shape=(
            jax.ShapeDtypeStruct((heads, width, n_own), bf16),
            jax.ShapeDtypeStruct((heads, 1, n_own), f32),
        ),
        compiler_params=pltpu.CompilerParams(dimension_semantics=("arbitrary",), vmem_limit_bytes=20 << 20),
        cost_estimate=pl.CostEstimate(
            flops=8 * heads * n_own * 1152 * 64, transcendentals=heads * n_own * 1152, bytes_accessed=4 << 20
        ),
        name="attend_forward",
    )(plan, own, own, own, halo, halo, query_class, key_class)


def attend_backward(plan, own, halo, query_class, key_class, attended, lse, grad, place=list):
    _, heads, width, n_own = own.shape
    n_halo = halo.shape[-1]
    n_keys = n_own + n_halo
    tile, chunk = BACKWARD_TILE, KEY_TILE
    n_tiles = n_own // tile
    block, half = n_own // 2, n_halo // 2
    scale = width**-0.5

    def body(
        plan_ref, q_ref, own_k, own_v, halo_k, halo_v, qc_ref, kc_ref, att_ref, lse_ref, grad_ref,
        own_out, halo_out, keys, keys_t, values, key_sum, value_sum,
    ):
        step = pl.program_id(0)

        def places(part):
            return (
                pl.ds(pl.multiple_of(plan_ref[n_tiles + part, 0], 128), block),
                slice(part * block, (part + 1) * block),
                pl.ds(pl.multiple_of(plan_ref[n_tiles + part, 1], 128), half),
                slice(part * half, (part + 1) * half),
            )

        @pl.when(step == 0)
        def _():
            for head in range(heads):
                for part in range(2):
                    to, cut, to_halo, cut_halo = places(part)
                    keys_t[head, :, to] = own_k[head, :, cut]
                    keys[head, to, :width] = own_k[head, :, cut].T
                    values[head, to, :] = own_v[head, :, cut].T
                    keys_t[head, :, to_halo] = halo_k[head, :, cut_halo]
                    keys[head, to_halo, :width] = halo_k[head, :, cut_halo].T
                    values[head, to_halo, :] = halo_v[head, :, cut_halo].T
                keys[head, :, width:] = kc_ref[...].T
            key_sum[...] = jnp.zeros_like(key_sum)
            value_sum[...] = jnp.zeros_like(value_sum)

        first = plan_ref[step, 0]
        scaled = [q_ref[h] * jnp.asarray(scale, bf16) for h in range(heads)]
        queries = [jnp.concatenate([scaled[h], qc_ref[...]], axis=0) for h in range(heads)]
        grads = [grad_ref[h] for h in range(heads)]
        logs = [lse_ref[h] * LOG2E for h in range(heads)]
        deltas = [
            jnp.sum(grads[h].astype(f32) * att_ref[h].astype(f32), axis=0, keepdims=True) for h in range(heads)
        ]

        def one_chunk(index, carry):
            at = pl.ds(pl.multiple_of(first + index * chunk, 128), chunk)
            scores = [dot_nn(keys[h, at, :], queries[h]) for h in range(heads)]
            grad_probs = [dot_nn(values[h, at, :], grads[h]) for h in range(heads)]
            result = []
            for h in range(heads):
                probs = jnp.exp2(scores[h] * LOG2E - logs[h])
                grad_scores = (probs * (grad_probs[h] - deltas[h])).astype(bf16)
                value_sum[h, :, at] += dot_nt(grads[h], probs.astype(bf16))
                key_sum[h, :, at] += dot_nt(scaled[h], grad_scores)
                result.append(carry[h] + dot_nn(keys_t[h, :, at], grad_scores))
            return tuple(result)

        start = tuple(jnp.zeros((width, tile), f32) for _ in range(heads))
        ends = lax.fori_loop(0, plan_ref[step, 1], one_chunk, start)
        at_tile = pl.ds(pl.multiple_of(step * tile, 128), tile)
        for h in range(heads):
            own_out[0, h, :, at_tile] = (ends[h] * scale).astype(bf16)

        @pl.when(step == n_tiles - 1)
        def _():
            for head in range(heads):
                for part in range(2):
                    to, cut, to_halo, cut_halo = places(part)
                    own_out[1, head, :, cut] = key_sum[head, :, to].astype(bf16)
                    own_out[2, head, :, cut] = value_sum[head, :, to].astype(bf16)
                    halo_out[0, head, :, cut_halo] = key_sum[head, :, to_halo].astype(bf16)
                    halo_out[1, head, :, cut_halo] = value_sum[head, :, to_halo].astype(bf16)

    whole_own = lambda p: pl.BlockSpec((None, heads, width, n_own), lambda t, r: (p, 0, 0, 0), pipeline_mode=ONCE)
    whole_halo = lambda p: pl.BlockSpec((None, heads, width, n_halo), lambda t, r: (p, 0, 0, 0), pipeline_mode=ONCE)
    tiled = lambda rows: pl.BlockSpec((heads, rows, tile), lambda t, r: (0, 0, t))
    grid = pltpu.PrefetchScalarGridSpec(
        num_scalar_prefetch=1,
        grid=(n_tiles,),
        in_specs=[
            pl.BlockSpec((None, heads, width, tile), lambda t, r: (0, 0, 0, t)),
            whole_own(1),
            whole_own(2),
            whole_halo(0),
            whole_halo(1),
            pl.BlockSpec((CLASSES, tile), lambda t, r: (0, t)),
            pl.BlockSpec((CLASSES, n_keys), lambda t, r: (0, 0), pipeline_mode=ONCE),
            tiled(width),
            tiled(1),
            tiled(width),
        ],
        out_specs=[
            pl.BlockSpec((3, heads, width, n_own), lambda t, r: (0, 0, 0, 0), pipeline_mode=ONCE),
            pl.BlockSpec((2, heads, width, n_halo), lambda t, r: (0, 0, 0, 0), pipeline_mode=ONCE),
        ],
        scratch_shapes=[
            pltpu.VMEM((heads, n_keys, width + CLASSES), bf16),
            pltpu.VMEM((heads, width, n_keys), bf16),
            pltpu.VMEM((heads, n_keys, width), bf16),
            pltpu.VMEM((heads, width, n_keys), f32),
            pltpu.VMEM((heads, width, n_keys), f32),
        ],
    )
    return pl.pallas_call(
        body,
        grid_spec=grid,
        out_shape=(
            pltpu.HBM((3, heads, width, n_own), bf16),
            pltpu.HBM((2, heads, width, n_halo), bf16),
        ),
        compiler_params=pltpu.CompilerParams(dimension_semantics=("arbitrary",), vmem_limit_bytes=20 << 20),
        cost_estimate=pl.CostEstimate(
            flops=20 * heads * n_own * 1152 * 64, transcendentals=heads * n_own * 1152, bytes_accessed=8 << 20
        ),
        name="attend_backward",
    )(plan, *place((own, own, own, halo, halo)), query_class, key_class, *place((attended, lse, grad)))


def attention_plan(item_ids, high, low, n_own, n_halo, tile):
    total = item_ids.shape[0]
    chunk = KEY_TILE
    n_keys = n_own + n_halo
    block, half = n_own // 2, n_halo // 2
    position = jnp.arange(total, dtype=jnp.int32)
    opens = jnp.concatenate([jnp.ones((1,), bool), item_ids[1:] != item_ids[:-1]])
    closes = jnp.concatenate([opens[1:], jnp.ones((1,), bool)])
    key_base = high * (total - n_keys)
    row_base = high * (total - n_own)
    starts = jnp.arange(0, total, tile, dtype=jnp.int32)[:, None]
    tile_first = jnp.max(jnp.where(opens & (position <= starts), position, 0), axis=1)
    tile_last = jnp.min(jnp.where(closes & (position >= starts + tile - 1), position + 1, total), axis=1)
    per_block = block // tile

    def local_tiles(values):
        mine = lax.dynamic_slice_in_dim(values, (row_base + low * block) // tile, per_block)
        other = lax.dynamic_slice_in_dim(values, (row_base + (1 - low) * block) // tile, per_block)
        return jnp.concatenate([mine, other]) - key_base

    begin = local_tiles(tile_first) // 128 * 128
    count = (local_tiles(tile_last) - begin + chunk - 1) // chunk
    begin = jnp.minimum(begin, n_keys - count * chunk)
    own_base = high * (n_keys - n_own)
    halo_base = (1 - high) * n_own
    offsets = jnp.stack(
        [
            jnp.stack([own_base + low * block, halo_base + low * half]),
            jnp.stack([own_base + (1 - low) * block, halo_base + (1 - low) * half]),
        ]
    )
    plan = jnp.concatenate([jnp.stack([begin, count], axis=1), offsets]).astype(jnp.int32)
    classes = jnp.arange(CLASSES, dtype=jnp.int32)[:, None] - 1
    row_ids = jnp.concatenate(
        [
            lax.dynamic_slice_in_dim(item_ids, row_base + low * block, block),
            lax.dynamic_slice_in_dim(item_ids, row_base + (1 - low) * block, block),
        ]
    )
    key_ids = lax.dynamic_slice_in_dim(item_ids, key_base, n_keys)
    query_class = jnp.where(row_ids[None] == classes, 0.0, -MASK_ROOT).astype(bf16)
    key_class = jnp.where(key_ids[None] == classes, MASK_ROOT, 0.0).astype(bf16)
    return plan, query_class, key_class


def layer_norm_parts(values, gain_row, shift_row):
    centre = values - jnp.mean(values, axis=-1, keepdims=True)
    inverse = lax.rsqrt(jnp.mean(centre * centre, axis=-1, keepdims=True) + NORM_EPS)
    unit_rows = centre * inverse
    return (unit_rows * gain_row + shift_row, unit_rows, inverse)


def norm_backward(upstream, unit_rows, inverse, gain_row):
    scaled = upstream * gain_row
    centred = scaled - jnp.mean(scaled, axis=-1, keepdims=True)
    return (centred - unit_rows * jnp.mean(scaled * unit_rows, axis=-1, keepdims=True)) * inverse


def adam_update(weight, gradient, first, second, step_rate):
    first_new = BETA_ONE * first + (1.0 - BETA_ONE) * gradient
    second_new = BETA_TWO * second + (1.0 - BETA_TWO) * gradient * gradient
    first_hat = first_new / (1.0 - BETA_ONE**STEP)
    second_hat = second_new / (1.0 - BETA_TWO**STEP)
    weight_new = weight - step_rate * (first_hat / (jnp.sqrt(second_hat) + ADAM_EPS) + DECAY * weight)
    return (weight_new, first_new, second_new)


def learning_rates():
    return (
        2.0 * D ** (-0.5),
        2.0 * max(D // SHORT, 1) ** (-0.5),
        2.0 * D ** (-0.5),
        2.0 * FF ** (-0.5),
        0.4,
        0.4,
    )


def swap(values, axis, stride=1):
    size = lax.axis_size(axis)
    return lax.ppermute(values, axis, [(i, i ^ stride) for i in range(size)])


def bits(axis):
    size = lax.axis_size(axis)
    return [1 << k for k in range(size.bit_length() - 1)]


def sum_all(values):
    for axis in ("lo", "hi", "dp"):
        for stride in bits(axis):
            values = values + swap(values, axis, stride)
    return values


def gather_rows(values, axis):
    index = lax.axis_index(axis)
    tail = values.shape
    held = values[None]
    for stride in reversed(bits(axis)):
        got = swap(held, axis, stride)
        upper = (index // stride) % 2 == 1
        held = jnp.stack([jnp.where(upper, got, held), jnp.where(upper, held, got)], axis=1)
        held = held.reshape((-1,) + tail)
    return held.reshape((-1,) + tail[1:])


def scatter_halves(held, axis, stride):
    upper = (lax.axis_index(axis) // stride) % 2
    pairs = held.reshape((-1, 2) + held.shape[1:])
    keep = lax.dynamic_index_in_dim(pairs, upper, 1, keepdims=False)
    send = lax.dynamic_index_in_dim(pairs, 1 - upper, 1, keepdims=False)
    return keep, send.astype(bf16)


def head_gradient_specs(down, halo_down, flat, width):
    chunk, near = down.shape[1] // 2, halo_down.shape[1] // 2
    whole = pl.BlockSpec((chunk, width), lambda i, *p: (0, 0), pipeline_mode=ONCE)
    return [
        pl.BlockSpec((down.shape[0], chunk), lambda i, *p: (0, i)),
        pl.BlockSpec((chunk, width), lambda i, *p: (i, 0)),
        pl.BlockSpec((halo_down.shape[0], near), lambda i, *p: (0, i)),
        pl.BlockSpec((near, width), lambda i, *p: (i, 0)),
        pl.BlockSpec((flat.shape[0], chunk), lambda i, *p: (0, i)),
        whole,
        whole,
    ]


def head_gradient_step(down, own_rows, halo_down, halo_rows, flat, mixed_own, mixed_other, total):
    step = pl.program_id(0)
    columns = down.shape[0]
    queries = columns - halo_down.shape[0]
    own = dot_nn(down[...], own_rows[...])
    halo = dot_nn(halo_down[...], halo_rows[...])

    @pl.when(step == 0)
    def _():
        total[:queries] = own[:queries]
        total[queries:columns] = own[queries:] + halo
        total[columns:] = dot_nn(flat[...], mixed_own[...])

    @pl.when(step == 1)
    def _():
        total[:queries] += own[:queries]
        total[queries:columns] += own[queries:] + halo
        total[columns:] += dot_nn(flat[...], mixed_other[...])


def head_gradient_sent(down, own_rows, halo_down, halo_rows, flat, mixed_own, mixed_other):
    width = own_rows.shape[1]
    shape = (down.shape[0] + flat.shape[0], width)

    def body(*refs):
        head_gradient_step(*refs[:7], refs[8])

        @pl.when(pl.program_id(0) == 1)
        def _():
            refs[7][...] = refs[8][...].astype(bf16)

    return pl.pallas_call(
        body,
        grid=(2,),
        in_specs=head_gradient_specs(down, halo_down, flat, width),
        out_specs=pl.BlockSpec(shape, lambda i: (0, 0)),
        out_shape=pltpu.HBM(shape, bf16),
        scratch_shapes=[pltpu.VMEM(shape, f32)],
        compiler_params=pltpu.CompilerParams(dimension_semantics=("arbitrary",), vmem_limit_bytes=24 << 20),
        cost_estimate=NO_COST,
        name="head_gradient_sent",
    )(*far(down), own_rows, *far(halo_down), halo_rows, flat, mixed_own, mixed_other)


def head_gradient_split(upper, n_blocks, operands, received):
    n_columns, width = received.shape
    rows = width // n_blocks
    down, _, halo_down, _, flat, _, _ = operands

    def body(upper_ref, *refs):
        head_gradient_step(*refs[:7], refs[10])

        @pl.when(pl.program_id(0) == 1)
        def _():
            turned = (refs[10][...] + refs[7][...].astype(f32)).T
            is_upper = upper_ref[0] == 1
            for i in range(n_blocks // 2):
                lower_rows = turned[2 * i * rows : (2 * i + 1) * rows]
                upper_rows = turned[(2 * i + 1) * rows : (2 * i + 2) * rows]
                refs[8][i] = jnp.where(is_upper, upper_rows, lower_rows)
                refs[9][i] = jnp.where(is_upper, lower_rows, upper_rows).astype(bf16)

    shape = (n_blocks // 2, rows, n_columns)
    whole = pl.BlockSpec(shape, lambda i, p: (0, 0, 0))
    grid = pltpu.PrefetchScalarGridSpec(
        num_scalar_prefetch=1,
        grid=(2,),
        in_specs=head_gradient_specs(down, halo_down, flat, width)
        + [pl.BlockSpec((n_columns, width), lambda i, p: (0, 0))],
        out_specs=[whole, whole],
        scratch_shapes=[pltpu.VMEM((n_columns, width), f32)],
    )
    return pl.pallas_call(
        body,
        grid_spec=grid,
        out_shape=(pltpu.HBM(shape, f32), pltpu.HBM(shape, bf16)),
        compiler_params=pltpu.CompilerParams(dimension_semantics=("arbitrary",), vmem_limit_bytes=28 << 20),
        cost_estimate=NO_COST,
        name="head_gradient_split",
    )(upper, *far(down), operands[1], *far(halo_down), *operands[3:], received)


def rows_back(at, pairs, received=()):
    n_rows, width = at.stop - at.start, pairs[0][1].shape[0]
    columns = pairs[0][0].shape[0]
    tile = 256
    first = at.start // tile

    def body(*refs):
        total = refs[2 * len(pairs)][...] if received else None
        for k in range(len(pairs)):
            part = dot_nt(refs[2 * k][...].T, refs[2 * k + 1][...])
            total = part if total is None else total + part
        refs[-1][...] = total

    one_pair = [
        pl.BlockSpec((columns, tile), lambda i: (0, first + i)),
        pl.BlockSpec((width, columns), lambda i: (0, 0), pipeline_mode=ONCE),
    ]
    row_tile = pl.BlockSpec((tile, width), lambda i: (i, 0))
    return pl.pallas_call(
        body,
        grid=(n_rows // tile,),
        in_specs=one_pair * len(pairs) + [row_tile] * len(received),
        out_specs=row_tile,
        out_shape=jax.ShapeDtypeStruct((n_rows, width), f32),
        compiler_params=pltpu.CompilerParams(dimension_semantics=("arbitrary",), vmem_limit_bytes=16 << 20),
        cost_estimate=NO_COST,
        name="rows_back",
    )(*far(*(array for pair in pairs for array in pair)), *received)


def feed_rows(place, hidden, rest, extra=()):
    n_rows, n_columns = hidden.shape
    n_ff = n_columns // 2
    width = rest.shape[1]
    tile = 256

    def body(place_ref, hidden_ref, own_ref, peer_ref, *refs):
        total = dot_nt(hidden_ref[:, :n_ff], own_ref[...]) + dot_nt(hidden_ref[:, n_ff:], peer_ref[...])
        if extra:
            total = refs[0][...].astype(f32) + total + refs[1][...] + refs[2][5:6, :]
        refs[-1][...] = total.astype(bf16)

    rows_of = lambda columns: pl.BlockSpec((tile, columns), lambda i, p: (i, 0))
    weight_of = lambda pick: pl.BlockSpec((None, width, n_ff), lambda i, p: (pick(p[0]), 0, 1), pipeline_mode=ONCE)
    extra_specs = [rows_of(width), rows_of(width), pl.BlockSpec((6, width), lambda i, p: (0, 0))] if extra else []
    grid = pltpu.PrefetchScalarGridSpec(
        num_scalar_prefetch=1,
        grid=(n_rows // tile,),
        in_specs=[rows_of(n_columns), weight_of(lambda h: h), weight_of(lambda h: 1 - h)] + extra_specs,
        out_specs=rows_of(width),
    )
    return pl.pallas_call(
        body,
        grid_spec=grid,
        out_shape=jax.ShapeDtypeStruct((n_rows, width), bf16),
        compiler_params=pltpu.CompilerParams(dimension_semantics=("arbitrary",), vmem_limit_bytes=16 << 20),
        cost_estimate=NO_COST,
        name="feed_rows",
    )(place, *far(hidden, rest, rest, *extra))


def first_norm_back(place, mine, other, pair, tokens, grad_mixed, small_params, early_sums):
    rows, width = tokens.shape
    half = mine.shape[0]
    gap = 2 * rows - 2 * half
    step = 128

    def body(place_ref, mine_ref, other_ref, pair_ref, tok_ref, mixed_ref, small_ref, early_ref, grad_ref, sum_ref, order):
        order[0:gap] = jnp.zeros((gap, width), bf16)
        order[gap + 2 * half :] = jnp.zeros((gap, width), bf16)
        first = pl.multiple_of(gap + place_ref[0] * half, 128)
        second = pl.multiple_of(gap + (1 - place_ref[0]) * half, 128)
        order[pl.ds(first, half)] = mine_ref[...]
        order[pl.ds(second, half)] = other_ref[...]
        take = place_ref[1]
        gain_row = small_ref[0:1, :]
        gain_sum = jnp.zeros((1, width), f32)
        shift_sum = jnp.zeros((1, width), f32)
        for k in range(0, rows, step):
            at = slice(k, k + step)
            back = pair_ref[at] + order[pl.ds(pl.multiple_of(take + k, 128), step)].astype(f32)
            _, unit_rows, inverse = layer_norm_parts(tok_ref[at].astype(f32), 1.0, 0.0)
            gain_sum = gain_sum + jnp.sum(back * unit_rows, axis=0, keepdims=True)
            shift_sum = shift_sum + jnp.sum(back, axis=0, keepdims=True)
            grad_ref[at] = mixed_ref[at] + norm_backward(back, unit_rows, inverse, gain_row)
        sum_ref[...] = early_ref[...]
        sum_ref[0:1, :] = gain_sum
        sum_ref[1:2, :] = shift_sum

    return pl.pallas_call(
        body,
        in_specs=[pl.BlockSpec(memory_space=pltpu.SMEM)] + [VMEM] * 7,
        out_specs=[VMEM, VMEM],
        out_shape=(jax.ShapeDtypeStruct((rows, width), f32), jax.ShapeDtypeStruct((16, width), f32)),
        scratch_shapes=[pltpu.VMEM((2 * gap + 2 * half, width), bf16)],
        compiler_params=pltpu.CompilerParams(vmem_limit_bytes=16 << 20),
        cost_estimate=NO_COST,
        name="first_norm_back",
    )(place, mine, other, pair, tokens, grad_mixed, small_params, early_sums)


def gelu_parts(values):
    normal_cdf = 0.5 * (1.0 + lax.erf(values * (0.5**0.5)))
    return values * normal_cdf, normal_cdf + values * (0.3989422804014327 * jnp.exp(-0.5 * values * values))


def feed_forward(place, rows_in, upstream, rest, bias, with_feed):
    n_rows, width = rows_in.shape
    n_ff = bias.shape[2]
    tile = 256

    def body(place_ref, x_ref, u_ref, rest_ref, bias_ref, hid_ref, pre_ref, back_ref, sum_ref, xt_ref, ut_ref, *feed):
        step = pl.program_id(0)
        x = x_ref[...]
        u = u_ref[...]
        xt_ref[...] = x.T
        ut_ref[...] = u.T
        back = fed = None
        for j in range(2):
            s = place_ref[0] if j == 0 else 1 - place_ref[0]
            columns = slice(j * n_ff, (j + 1) * n_ff)
            up = rest_ref[s, :, :n_ff]
            down = rest_ref[s, :, n_ff : 2 * n_ff]
            hidden, slope = gelu_parts(dot_nn(x, up) + bias_ref[s])
            hidden = hidden.astype(bf16)
            hid_ref[:, columns] = hidden
            grad_pre = (dot_nn(u, down) * slope).astype(bf16)
            if with_feed:
                part = dot_nt(hidden, down)
                fed = part if fed is None else fed + part
            pre_ref[:, columns] = grad_pre
            sums = jnp.sum(grad_pre.astype(f32), axis=0, keepdims=True)
            sum_ref[:, columns] = jnp.where(step == 0, sums, sum_ref[:, columns] + sums)
            part = dot_nt(grad_pre, up)
            back = part if back is None else back + part
        back_ref[...] = back
        if with_feed:
            feed[0][...] = fed.astype(bf16)

    by_row = lambda columns: pl.BlockSpec((tile, columns), lambda i, p: (i, 0))
    grid = pltpu.PrefetchScalarGridSpec(
        num_scalar_prefetch=1,
        grid=(n_rows // tile,),
        in_specs=[
            by_row(width),
            by_row(width),
            pl.BlockSpec(rest.shape, lambda i, p: (0, 0, 0), pipeline_mode=ONCE),
            pl.BlockSpec(bias.shape, lambda i, p: (0, 0, 0), pipeline_mode=ONCE),
        ],
        out_specs=[
            by_row(2 * n_ff),
            by_row(2 * n_ff),
            by_row(width),
            pl.BlockSpec((1, 2 * n_ff), lambda i, p: (0, 0)),
            pl.BlockSpec((width, tile), lambda i, p: (0, i)),
            pl.BlockSpec((width, tile), lambda i, p: (0, i)),
        ]
        + [by_row(width)] * with_feed,
    )
    return pl.pallas_call(
        body,
        grid_spec=grid,
        out_shape=(
            pltpu.HBM((n_rows, 2 * n_ff), bf16),
            pltpu.HBM((n_rows, 2 * n_ff), bf16),
            jax.ShapeDtypeStruct((n_rows, width), f32),
            jax.ShapeDtypeStruct((1, 2 * n_ff), f32),
            pltpu.HBM((width, n_rows), bf16),
            pltpu.HBM((width, n_rows), bf16),
        )
        + (jax.ShapeDtypeStruct((n_rows, width), bf16),) * with_feed,
        compiler_params=pltpu.CompilerParams(dimension_semantics=("arbitrary",), vmem_limit_bytes=20 << 20),
        cost_estimate=NO_COST,
        name="feed_forward",
    )(place, rows_in, upstream, *far(rest), bias)


def weight_grads(twos, grad_pres, ups, hiddens):
    width, n_rows = twos[0].shape
    n_ff = hiddens[0].shape[1]
    block = 512
    per = n_ff // block

    def body(x0, x1, p0, p1, u0, u1, h0, h1, out_ref):
        step = pl.program_id(0)

        @pl.when(step < per)
        def _():
            out_ref[...] = (dot_nn(x0[...], p0[...]) + dot_nn(x1[...], p1[...])).astype(bf16)

        @pl.when(step >= per)
        def _():
            out_ref[...] = (dot_nn(u0[...], h0[...]) + dot_nn(u1[...], h1[...])).astype(bf16)

    whole = lambda array: pl.BlockSpec(array.shape, lambda i: (0, 0), pipeline_mode=ONCE)
    early = pl.BlockSpec((n_rows, block), lambda i: (0, jnp.minimum(i, per - 1)))
    late = pl.BlockSpec((n_rows, block), lambda i: (0, jnp.clip(i - per, 0, per - 1)))
    return pl.pallas_call(
        body,
        grid=(2 * per,),
        in_specs=[whole(twos[0])] * 2 + [early] * 2 + [whole(ups[0])] * 2 + [late] * 2,
        out_specs=pl.BlockSpec((width, block), lambda i: (0, i)),
        out_shape=pltpu.HBM((width, 2 * n_ff), bf16),
        compiler_params=pltpu.CompilerParams(dimension_semantics=("arbitrary",), vmem_limit_bytes=16 << 20),
        cost_estimate=NO_COST,
        name="weight_grads",
    )(*twos, *far(*grad_pres), *ups, *far(*hiddens))


def attended_grads(mixed_own, mixed_other, full_out):
    n_rows, width = mixed_own.shape
    columns = full_out.shape[1] // 2

    def body(own_ref, other_ref, out_ref, *grads):
        turned = out_ref[...].T
        for j in range(2):
            part = turned[j * columns : (j + 1) * columns]
            grads[j][:, :n_rows] = dot_nt(part, own_ref[...]).astype(bf16)
            grads[j][:, n_rows:] = dot_nt(part, other_ref[...]).astype(bf16)

    shape = (columns, 2 * n_rows)
    return pl.pallas_call(
        body,
        in_specs=[VMEM] * 3,
        out_specs=[VMEM] * 2,
        out_shape=(jax.ShapeDtypeStruct(shape, bf16),) * 2,
        compiler_params=pltpu.CompilerParams(vmem_limit_bytes=12 << 20),
        cost_estimate=NO_COST,
        name="attended_grads",
    )(mixed_own, mixed_other, full_out)


def second_norm_back(place, pair, received, mixed, upstream_low, small_params, bias_grad):
    rows, width = mixed.shape
    step = 128

    def body(place_ref, pair_ref, got_ref, mixed_ref, up_ref, small_ref, bias_ref, grad_ref, low_ref, sum_ref):
        sums = [jnp.zeros((1, width), f32) for _ in range(4)]
        for k in range(0, rows, step):
            at = slice(k, k + step)
            back = pair_ref[at] + got_ref[at]
            upstream = up_ref[at].astype(f32)
            _, unit_rows, inverse = layer_norm_parts(mixed_ref[at], 1.0, 0.0)
            grad = upstream + norm_backward(back, unit_rows, inverse, small_ref[2:3, :])
            grad_ref[at] = grad
            low_ref[at] = grad.astype(bf16)
            for i, term in enumerate((back * unit_rows, back, grad, upstream)):
                sums[i] = sums[i] + jnp.sum(term, axis=0, keepdims=True)
        sum_ref[...] = jnp.zeros_like(sum_ref)
        for i in range(4):
            sum_ref[i + 2 : i + 3, :] = sums[i]
        for i in range(4):
            own = jnp.where(place_ref[0] == i, bias_ref[0:1, :width], jnp.zeros((1, width), f32))
            peer = jnp.where(place_ref[1] == i, bias_ref[0:1, width:], jnp.zeros((1, width), f32))
            sum_ref[i + 6 : i + 7, :] = own + peer

    return pl.pallas_call(
        body,
        in_specs=[pl.BlockSpec(memory_space=pltpu.SMEM)] + [VMEM] * 6,
        out_specs=[VMEM] * 3,
        out_shape=(
            jax.ShapeDtypeStruct((rows, width), f32),
            jax.ShapeDtypeStruct((rows, width), bf16),
            jax.ShapeDtypeStruct((16, width), f32),
        ),
        compiler_params=pltpu.CompilerParams(vmem_limit_bytes=16 << 20),
        name="second_norm_back",
    )(place, pair, received, mixed, upstream_low, small_params, bias_grad)


def finish_grads(n_data, keep, got, reduced, from_peer, late_sums, n_qkv):
    d_local = reduced.shape[0]
    n_ff = from_peer.shape[1] // 2
    n_out = keep.shape[2] - n_qkv

    def body(keep_ref, got_ref, red_ref, peer_ref, sum_ref, qkv_ref, out_ref, up_ref, down_ref, total_ref):
        heads_grad = keep_ref[0] + got_ref[0].astype(f32)
        qkv_ref[...] = heads_grad[:, :n_qkv]
        out_ref[...] = heads_grad[:, n_qkv:]
        squares = jnp.sum(jnp.square(heads_grad * (1.0 / n_data)), keepdims=True)
        for ref, at, peer_at in ((up_ref, 0, 0), (down_ref, 2 * n_ff, n_ff)):
            grad = red_ref[:, at : at + n_ff].astype(f32) + peer_ref[:, peer_at : peer_at + n_ff].astype(f32)
            ref[...] = grad
            squares = squares + jnp.sum(jnp.square(grad * (1.0 / n_data)), keepdims=True)
        total_ref[...] = sum_ref[...]
        total_ref[10:11, :] = jnp.broadcast_to(squares, (1, sum_ref.shape[1]))

    shapes = [(d_local, n_qkv), (d_local, n_out), (d_local, n_ff), (d_local, n_ff), late_sums.shape]
    return pl.pallas_call(
        body,
        in_specs=[VMEM] * 5,
        out_specs=[VMEM] * 5,
        out_shape=tuple(jax.ShapeDtypeStruct(shape, f32) for shape in shapes),
        compiler_params=pltpu.CompilerParams(vmem_limit_bytes=8 << 20),
        name="finish_grads",
    )(keep, got, reduced, from_peer, late_sums)


def optimizer(n_data, summed, grads, states):
    rates = learning_rates()
    flat = [array for group in states for array in group]
    n_states = len(states)
    heads = grads[0].shape[1] // (3 * HEAD_DIM)

    def body(*refs):
        summed_ref = refs[0]
        grad_refs = refs[1:5]
        state_refs = refs[5 : 5 + 3 * n_states]
        norm_ref = refs[5 + 3 * n_states]
        out_refs = refs[6 + 3 * n_states :]
        small = summed_ref[0:10, :] * (1.0 / n_data)
        total = jnp.sum(small * small, keepdims=True) + summed_ref[10:11, 0:1]
        norm = jnp.sqrt(total)
        norm_ref[...] = norm
        factor = CLIP_NORM / jnp.maximum(norm, CLIP_NORM)

        def update(index, gradient, take=(slice(None), slice(None))):
            w, m, v = (ref[take] for ref in state_refs[3 * index : 3 * index + 3])
            results = adam_update(w, gradient * factor, m, v, rates[index])
            for ref, value in zip(out_refs[3 * index : 3 * index + 3], results):
                ref[take] = value

        for head in range(heads):
            pieces = [
                grad_refs[0][:, (part * heads + head) * HEAD_DIM : (part * heads + head + 1) * HEAD_DIM]
                for part in range(3)
            ]
            at = slice(3 * head * HEAD_DIM, 3 * (head + 1) * HEAD_DIM)
            update(0, jnp.concatenate(pieces, axis=1) * (1.0 / n_data), (slice(None), at))
        update(1, grad_refs[1][...].T * (1.0 / n_data))
        update(2, grad_refs[2][...] * (1.0 / n_data))
        update(3, grad_refs[3][...] * (1.0 / n_data))
        update(4, small[0:6])
        lanes = 128
        bias_grads = [
            small[6 + row : 7 + row, k * lanes : (k + 1) * lanes]
            for row in range(4)
            for k in range(small.shape[1] // lanes)
        ]
        update(5, jnp.concatenate(bias_grads, axis=0))

    whole = lambda array: pl.BlockSpec(array.shape, lambda i: (0,) * len(array.shape))
    return pl.pallas_call(
        body,
        grid=(1,),
        in_specs=[whole(array) for array in (summed, *grads, *flat)],
        out_specs=[pl.BlockSpec((1, 1), lambda i: (0, 0))] + [whole(array) for array in flat],
        out_shape=(
            jax.ShapeDtypeStruct((1, 1), f32),
            *(jax.ShapeDtypeStruct(array.shape, f32) for array in flat),
        ),
        compiler_params=pltpu.CompilerParams(vmem_limit_bytes=16 << 20),
        name="optimizer",
    )(summed, *grads, *flat)


def body(
    tokens,
    cotangent,
    row_item,
    w_qkv,
    w_out,
    w_up,
    w_down,
    small_params,
    up_bias,
    first_qkv,
    first_out,
    first_up,
    first_down,
    first_small,
    first_bias,
    second_qkv,
    second_out,
    second_up,
    second_down,
    second_small,
    second_bias,
):
    rows = tokens.shape[0]
    n_data = lax.axis_size("dp")
    high = lax.axis_index("hi")
    low = lax.axis_index("lo")
    heads_local = w_qkv.shape[1] // (3 * HEAD_DIM)
    head_width = heads_local * HEAD_DIM
    ff_local = w_up.shape[1]
    d_local = w_qkv.shape[0]
    n_own = 2 * rows
    n_halo = LONG - 1
    half = n_halo // 2

    shard_qkv = (
        w_qkv.astype(bf16)
        .reshape(d_local, heads_local, 3, HEAD_DIM)
        .transpose(0, 2, 1, 3)
        .reshape(d_local, 3 * head_width)
    )
    shard_rest = jnp.concatenate([w_up.astype(bf16), w_down.astype(bf16).T, w_out.astype(bf16).T], axis=1)
    qkv_mine = gather_rows(shard_qkv, "dp")
    rest = lax.all_gather(shard_rest, ("hi", "dp"), axis=0, tiled=True).reshape(2, D, -1)
    outs = rest[:, :, 2 * ff_local :]
    full_out = jnp.concatenate(
        [
            lax.dynamic_index_in_dim(outs, high, 0, keepdims=False),
            lax.dynamic_index_in_dim(outs, 1 - high, 0, keepdims=False),
        ],
        axis=1,
    )

    group_row = (2 * high + low) * rows
    own_ids = lax.dynamic_slice_in_dim(row_item, group_row, rows)
    keep_rows = (own_ids >= 0).astype(f32)[:, None]
    residual = tokens.astype(f32)
    normed, _, _ = layer_norm_parts(residual, small_params[0], small_params[1])
    normed = normed.astype(bf16)
    normed_other = swap(normed, "lo")
    send_at = (1 - high) * (512 - 256 * low) + high * low * 1280
    send_rows = lax.dynamic_slice_in_dim(
        jnp.concatenate([normed, normed_other, normed], axis=0), send_at, half, axis=0
    )
    halo_mine = swap(send_rows, "hi")
    halo_other = swap(halo_mine, "lo")
    own_rows = jnp.concatenate([normed, normed_other], axis=0)
    halo_rows = jnp.concatenate([halo_mine, halo_other], axis=0)
    plan, query_class, key_class = attention_plan(row_item, high, low, n_own, n_halo, FORWARD_TILE)
    plan_back, _, _ = attention_plan(row_item, high, low, n_own, n_halo, BACKWARD_TILE)
    plan, plan_back, query_class, key_class, qkv_mine = lax.optimization_barrier(
        (plan, plan_back, query_class, key_class, qkv_mine)
    )

    upstream = cotangent.astype(f32) * keep_rows
    upstream_low = upstream.astype(bf16)
    upstream_low, qkv_mine = lax.optimization_barrier((upstream_low, qkv_mine))
    qkv_theirs = swap(qkv_mine, "hi")
    upstream_other = swap(upstream_low, "lo")
    own_rows, halo_rows = lax.optimization_barrier((own_rows, halo_rows))

    def project(weight):
        own = dot_tt(weight, own_rows).astype(bf16).reshape(3, heads_local, HEAD_DIM, n_own)
        halo = dot_tt(weight[:, head_width:], halo_rows).astype(bf16).reshape(2, heads_local, HEAD_DIM, n_halo)
        return own, halo

    own_m, halo_m = project(qkv_mine)
    att_m, lse_m = attend_forward(plan, own_m, halo_m, query_class, key_class)
    qkv_theirs, att_m = lax.optimization_barrier((qkv_theirs, att_m))
    own_t, halo_t = project(qkv_theirs)
    att_t, lse_t = attend_forward(plan, own_t, halo_t, query_class, key_class)
    flat = jnp.concatenate([att_m, att_t], axis=0).reshape(2 * head_width, n_own)

    first_half, second_half = slice(0, rows), slice(rows, n_own)

    got = swap(dot_tt(flat[:, second_half], full_out).astype(bf16), "lo")
    attention_part, got = lax.optimization_barrier((dot_tt(flat[:, first_half], full_out), got))
    attention_part = attention_part + got.astype(f32)
    mixed = residual + attention_part + small_params[4]
    normed_two, _, _ = layer_norm_parts(mixed, small_params[2], small_params[3])
    normed_two = normed_two.astype(bf16)
    two_other = swap(normed_two, "lo")
    bias_parts = up_bias.reshape(2, 2, ff_local)
    bias_pair = lax.dynamic_index_in_dim(bias_parts, low, 1, keepdims=False).reshape(2, 1, ff_local)
    half_place = high.astype(jnp.int32).reshape(1)
    hidden_o, pre_o, back_o, bias_o, two_t_o, up_t_o, feed_other = feed_forward(
        half_place, two_other, upstream_other, rest, bias_pair, True
    )
    normed_two, back_o, feed_other = lax.optimization_barrier((normed_two, back_o, feed_other))
    two_got = swap(back_o, "lo")
    feed_got = swap(feed_other, "lo")
    hidden_m, pre_m, two_pair, bias_m, two_t_m, up_t_m = feed_forward(
        half_place, normed_two, upstream_low, rest, bias_pair, False
    )
    bias_grad = bias_m + bias_o
    bias_place = jnp.stack([2 * high + low, 2 * (1 - high) + low]).astype(jnp.int32)
    grad_mixed, mixed_low, early_sums = second_norm_back(
        bias_place, two_pair, two_got, mixed, upstream_low, small_params, bias_grad
    )
    mixed_other = swap(mixed_low, "lo")
    grad_rest = weight_grads((two_t_m, two_t_o), (pre_m, pre_o), (up_t_m, up_t_o), (hidden_m, hidden_o))
    grad_rest, mixed_other = lax.optimization_barrier((grad_rest, mixed_other))
    grad_rest = lax.psum_scatter(grad_rest, "dp", scatter_dimension=0, tiled=True)
    att_grad_m, att_grad_t = attended_grads(mixed_low, mixed_other, full_out)
    att_grad_m = att_grad_m.reshape(heads_local, HEAD_DIM, n_own)
    att_grad_t = att_grad_t.reshape(heads_local, HEAD_DIM, n_own)

    down_t, halo_down_t = attend_backward(
        plan_back, own_t, halo_t, query_class, key_class, att_t, lse_t, att_grad_t
    )
    down_t = down_t.reshape(3 * head_width, n_own)
    halo_down_t = halo_down_t.reshape(2 * head_width, n_halo)

    flat_m, flat_t = flat[:head_width], flat[head_width:]
    qkv_for_peer = head_gradient_sent(
        down_t, own_rows, halo_down_t, halo_rows, flat_t, mixed_low, mixed_other
    )
    qkv_for_peer, att_grad_m = lax.optimization_barrier((qkv_for_peer, att_grad_m))
    qkv_from_peer = swap(qkv_for_peer, "hi")
    down_m, halo_down_m = attend_backward(
        plan_back, own_m, halo_m, query_class, key_class, att_m, lse_m, att_grad_m, lambda arrays: far(*arrays)
    )
    down_m = down_m.reshape(3 * head_width, n_own)
    halo_down_m = halo_down_m.reshape(2 * head_width, n_halo)

    def halo_part(at):
        return dot_tt(halo_down_t[:, at], qkv_theirs[:, head_width:]) + dot_tt(
            halo_down_m[:, at], qkv_mine[:, head_width:]
        )

    strides = bits("dp")
    pairs = ((down_t, qkv_theirs), (down_m, qkv_mine))
    halo_got = swap(halo_part(slice(half, n_halo)), "lo")
    back_sent = rows_back(second_half, pairs)
    back_sent, qkv_from_peer = lax.optimization_barrier((back_sent, qkv_from_peer))
    back_got = swap(back_sent, "lo")
    upper = (lax.axis_index("dp") % 2).astype(jnp.int32).reshape(1)
    operands = (down_m, own_rows, halo_down_m, halo_rows, flat_m, mixed_low, mixed_other)
    keep, send = head_gradient_split(upper, n_data, operands, qkv_from_peer)
    halo_send = (halo_part(slice(0, half)) + halo_got).astype(bf16)
    halo_send, send, down_m, hidden, back_got = lax.optimization_barrier(
        (halo_send, send, down_m, hidden_m, back_got)
    )
    got = swap(send, "dp", strides[0])
    back_mine = swap(halo_send, "hi")
    back_pair = rows_back(first_half, ((down_t, qkv_theirs), (down_m, qkv_mine)), (back_got,))
    output = feed_rows(half_place, hidden, rest, (feed_got, mixed, small_params))
    got, back_pair, output = lax.optimization_barrier((got, back_pair, output))
    keep, send = scatter_halves(keep + got.astype(f32), "dp", strides[1])
    send, back_mine = lax.optimization_barrier((send, back_mine))
    got = swap(send, "dp", strides[1])
    back_other = swap(back_mine, "lo")
    theirs = jnp.concatenate(
        [grad_rest[:, ff_local : 2 * ff_local], grad_rest[:, 3 * ff_local : 4 * ff_local]], axis=1
    )
    got, back_other, theirs = lax.optimization_barrier((got, back_other, theirs))
    from_peer = swap(theirs, "hi")
    keep, send = scatter_halves(keep + got.astype(f32), "dp", strides[2])
    send, back_other = lax.optimization_barrier((send, back_other))
    got = swap(send, "dp", strides[2])
    place = jnp.stack([low, high * (n_own - n_halo) + low * rows]).astype(jnp.int32)
    input_grad, late_sums = first_norm_back(
        place, back_mine, back_other, back_pair, tokens, grad_mixed, small_params, early_sums
    )
    got, late_sums = lax.optimization_barrier((got, late_sums))
    for stride in strides[3:]:
        keep, send = scatter_halves(keep + got.astype(f32), "dp", stride)
        got = swap(send, "dp", stride)
    *grads, summed = finish_grads(n_data, keep, got, grad_rest, from_peer, late_sums, 3 * head_width)
    summed = sum_all(summed)
    norm, *updated = optimizer(
        n_data,
        summed,
        grads,
        (
            (w_qkv, first_qkv, second_qkv),
            (w_out, first_out, second_out),
            (w_up, first_up, second_up),
            (w_down.T, first_down.T, second_down.T),
            (small_params, first_small, second_small),
            tuple(array.reshape(-1, 128) for array in (up_bias, first_bias, second_bias)),
        ),
    )
    updated[9:12] = [array.T for array in updated[9:12]]
    updated[15:18] = [array.reshape(-1) for array in updated[15:18]]
    return (output, input_grad, norm[0, 0], *updated)


def solution(mesh):
    n_data, n_model = mesh.devices.shape
    split = Mesh(mesh.devices.reshape(n_data, 2, n_model // 2), ("dp", "hi", "lo"))
    model = ("hi", "lo")
    rows = P(("dp", "hi", "lo"), None)
    by_row = P("dp", model)
    by_column = P(model, "dp")
    states = (by_row, by_column, by_row, by_column, P(), P())
    in_specs = (rows, rows, P("dp"), *states, *states, *states)
    updated = []
    for spec in states:
        updated.extend([spec, spec, spec])
    out_specs = (rows, rows, P(), *updated)
    return jax.shard_map(body, mesh=split, in_specs=in_specs, out_specs=out_specs, check_vma=False)
```

```python
import jax
import jax.numpy as jnp
from jax import lax
from jax.experimental import pallas as pl
from jax.experimental.pallas import tpu as pltpu
from jax.sharding import Mesh, PartitionSpec as P

HEAD_DIM = 64
FF = 3072
D = 768
SHORT = 257
LONG = 1025
STEP = 5

CLIP_NORM = 1.0
BETA_ONE = 0.9
BETA_TWO = 0.999
ADAM_EPS = 1e-08
DECAY = 0.03
NORM_EPS = 1e-05

LOG2E = 1.4426950408889634
MASK_ROOT = 2.0**20
CLASSES = 16
FORWARD_TILE = 384
BACKWARD_TILE = 256
KEY_TILE = 384

bf16 = jnp.bfloat16
ONCE = pl.Buffered(1)
NO_COST = pl.CostEstimate(flops=0, transcendentals=0, bytes_accessed=0)
VMEM = pl.BlockSpec(memory_space=pltpu.VMEM)
f32 = jnp.float32


def far(*arrays):
    return [pltpu.with_memory_space_constraint(array, pltpu.HBM) for array in arrays]


def dot_nn(left, right):
    return lax.dot_general(left, right, (((1,), (0,)), ((), ())), preferred_element_type=f32)


def dot_nt(left, right):
    return lax.dot_general(left, right, (((1,), (1,)), ((), ())), preferred_element_type=f32)


def dot_tn(left, right):
    return lax.dot_general(left, right, (((0,), (0,)), ((), ())), preferred_element_type=f32)


def dot_tt(left, right):
    return lax.dot_general(left, right, (((0,), (1,)), ((), ())), preferred_element_type=f32)


def attend_forward(plan, own, halo, query_class, key_class):
    _, heads, width, n_own = own.shape
    n_halo = halo.shape[-1]
    n_keys = n_own + n_halo
    tile, chunk = FORWARD_TILE, KEY_TILE
    n_tiles = n_own // tile
    block, half = n_own // 2, n_halo // 2

    def body(plan_ref, q_ref, own_k, own_v, halo_k, halo_v, qc_ref, kc_ref, out_ref, lse_ref, keys, values):
        step = pl.program_id(0)

        @pl.when(step == 0)
        def _():
            ones = (lax.broadcasted_iota(jnp.int32, (CLASSES, n_keys), 0) == 0).astype(bf16)
            for head in range(heads):
                for part in range(2):
                    to = pl.ds(pl.multiple_of(plan_ref[n_tiles + part, 0], 128), block)
                    cut = slice(part * block, (part + 1) * block)
                    values[head, :width, to] = own_v[head, :, cut]
                    keys[head, to, :width] = own_k[head, :, cut].T
                    to = pl.ds(pl.multiple_of(plan_ref[n_tiles + part, 1], 128), half)
                    cut = slice(part * half, (part + 1) * half)
                    values[head, :width, to] = halo_v[head, :, cut]
                    keys[head, to, :width] = halo_k[head, :, cut].T
                values[head, width:, :] = ones
                keys[head, :, width:] = kc_ref[...].T

        first = plan_ref[step, 0]
        scale = jnp.asarray(width**-0.5, bf16)
        queries = [jnp.concatenate([q_ref[h] * scale, qc_ref[...]], axis=0) for h in range(heads)]

        def one_chunk(index, carry):
            at = pl.ds(pl.multiple_of(first + index * chunk, 128), chunk)
            scores = [dot_nn(keys[h, at, :], queries[h]) for h in range(heads)]
            result = []
            for h in range(heads):
                top, total = carry[h]
                new_top = jnp.maximum(top, jnp.max(scores[h], axis=0, keepdims=True))
                probs = jnp.exp2((scores[h] - new_top) * LOG2E)
                fade = jnp.exp2((top - new_top) * LOG2E)
                result.append((new_top, total * fade + dot_nn(values[h, :, at], probs.astype(bf16))))
            return tuple(result)

        start = tuple(
            (jnp.full((1, tile), -3e38, f32), jnp.zeros((width + CLASSES, tile), f32)) for _ in range(heads)
        )
        ends = lax.fori_loop(0, plan_ref[step, 1], one_chunk, start)
        for h in range(heads):
            top, total = ends[h]
            row_sum = total[width : width + 1]
            out_ref[h] = (total[:width] / row_sum).astype(bf16)
            lse_ref[h] = top + jnp.log(row_sum)

    whole_own = lambda p: pl.BlockSpec((None, heads, width, n_own), lambda t, r: (p, 0, 0, 0), pipeline_mode=ONCE)
    whole_halo = lambda p: pl.BlockSpec((None, heads, width, n_halo), lambda t, r: (p, 0, 0, 0), pipeline_mode=ONCE)
    tiled = lambda rows: pl.BlockSpec((heads, rows, tile), lambda t, r: (0, 0, t))
    grid = pltpu.PrefetchScalarGridSpec(
        num_scalar_prefetch=1,
        grid=(n_tiles,),
        in_specs=[
            pl.BlockSpec((None, heads, width, tile), lambda t, r: (0, 0, 0, t)),
            whole_own(1),
            whole_own(2),
            whole_halo(0),
            whole_halo(1),
            pl.BlockSpec((CLASSES, tile), lambda t, r: (0, t)),
            pl.BlockSpec((CLASSES, n_keys), lambda t, r: (0, 0), pipeline_mode=ONCE),
        ],
        out_specs=[tiled(width), tiled(1)],
        scratch_shapes=[
            pltpu.VMEM((heads, n_keys, width + CLASSES), bf16),
            pltpu.VMEM((heads, width + CLASSES, n_keys), bf16),
        ],
    )
    return pl.pallas_call(
        body,
        grid_spec=grid,
        out_shape=(
            jax.ShapeDtypeStruct((heads, width, n_own), bf16),
            jax.ShapeDtypeStruct((heads, 1, n_own), f32),
        ),
        compiler_params=pltpu.CompilerParams(dimension_semantics=("arbitrary",), vmem_limit_bytes=20 << 20),
        cost_estimate=pl.CostEstimate(
            flops=8 * heads * n_own * 1152 * 64, transcendentals=heads * n_own * 1152, bytes_accessed=4 << 20
        ),
        name="attend_forward",
    )(plan, own, own, own, halo, halo, query_class, key_class)


def attend_backward(plan, own, halo, query_class, key_class, attended, lse, grad, place=list):
    _, heads, width, n_own = own.shape
    n_halo = halo.shape[-1]
    n_keys = n_own + n_halo
    tile, chunk = BACKWARD_TILE, KEY_TILE
    n_tiles = n_own // tile
    block, half = n_own // 2, n_halo // 2
    scale = width**-0.5

    def body(
        plan_ref, q_ref, own_k, own_v, halo_k, halo_v, qc_ref, kc_ref, att_ref, lse_ref, grad_ref,
        own_out, halo_out, keys, keys_t, values, key_sum, value_sum,
    ):
        step = pl.program_id(0)

        def places(part):
            return (
                pl.ds(pl.multiple_of(plan_ref[n_tiles + part, 0], 128), block),
                slice(part * block, (part + 1) * block),
                pl.ds(pl.multiple_of(plan_ref[n_tiles + part, 1], 128), half),
                slice(part * half, (part + 1) * half),
            )

        @pl.when(step == 0)
        def _():
            for head in range(heads):
                for part in range(2):
                    to, cut, to_halo, cut_halo = places(part)
                    keys_t[head, :, to] = own_k[head, :, cut]
                    keys[head, to, :width] = own_k[head, :, cut].T
                    values[head, to, :] = own_v[head, :, cut].T
                    keys_t[head, :, to_halo] = halo_k[head, :, cut_halo]
                    keys[head, to_halo, :width] = halo_k[head, :, cut_halo].T
                    values[head, to_halo, :] = halo_v[head, :, cut_halo].T
                keys[head, :, width:] = kc_ref[...].T
            key_sum[...] = jnp.zeros_like(key_sum)
            value_sum[...] = jnp.zeros_like(value_sum)

        first = plan_ref[step, 0]
        scaled = [q_ref[h] * jnp.asarray(scale, bf16) for h in range(heads)]
        queries = [jnp.concatenate([scaled[h], qc_ref[...]], axis=0) for h in range(heads)]
        grads = [grad_ref[h] for h in range(heads)]
        logs = [lse_ref[h] * LOG2E for h in range(heads)]
        deltas = [
            jnp.sum(grads[h].astype(f32) * att_ref[h].astype(f32), axis=0, keepdims=True) for h in range(heads)
        ]

        def one_chunk(index, carry):
            at = pl.ds(pl.multiple_of(first + index * chunk, 128), chunk)
            scores = [dot_nn(keys[h, at, :], queries[h]) for h in range(heads)]
            grad_probs = [dot_nn(values[h, at, :], grads[h]) for h in range(heads)]
            result = []
            for h in range(heads):
                probs = jnp.exp2(scores[h] * LOG2E - logs[h])
                grad_scores = (probs * (grad_probs[h] - deltas[h])).astype(bf16)
                value_sum[h, :, at] += dot_nt(grads[h], probs.astype(bf16))
                key_sum[h, :, at] += dot_nt(scaled[h], grad_scores)
                result.append(carry[h] + dot_nn(keys_t[h, :, at], grad_scores))
            return tuple(result)

        start = tuple(jnp.zeros((width, tile), f32) for _ in range(heads))
        ends = lax.fori_loop(0, plan_ref[step, 1], one_chunk, start)
        at_tile = pl.ds(pl.multiple_of(step * tile, 128), tile)
        for h in range(heads):
            own_out[0, h, :, at_tile] = (ends[h] * scale).astype(bf16)

        @pl.when(step == n_tiles - 1)
        def _():
            for head in range(heads):
                for part in range(2):
                    to, cut, to_halo, cut_halo = places(part)
                    own_out[1, head, :, cut] = key_sum[head, :, to].astype(bf16)
                    own_out[2, head, :, cut] = value_sum[head, :, to].astype(bf16)
                    halo_out[0, head, :, cut_halo] = key_sum[head, :, to_halo].astype(bf16)
                    halo_out[1, head, :, cut_halo] = value_sum[head, :, to_halo].astype(bf16)

    whole_own = lambda p: pl.BlockSpec((None, heads, width, n_own), lambda t, r: (p, 0, 0, 0), pipeline_mode=ONCE)
    whole_halo = lambda p: pl.BlockSpec((None, heads, width, n_halo), lambda t, r: (p, 0, 0, 0), pipeline_mode=ONCE)
    tiled = lambda rows: pl.BlockSpec((heads, rows, tile), lambda t, r: (0, 0, t))
    grid = pltpu.PrefetchScalarGridSpec(
        num_scalar_prefetch=1,
        grid=(n_tiles,),
        in_specs=[
            pl.BlockSpec((None, heads, width, tile), lambda t, r: (0, 0, 0, t)),
            whole_own(1),
            whole_own(2),
            whole_halo(0),
            whole_halo(1),
            pl.BlockSpec((CLASSES, tile), lambda t, r: (0, t)),
            pl.BlockSpec((CLASSES, n_keys), lambda t, r: (0, 0), pipeline_mode=ONCE),
            tiled(width),
            tiled(1),
            tiled(width),
        ],
        out_specs=[
            pl.BlockSpec((3, heads, width, n_own), lambda t, r: (0, 0, 0, 0), pipeline_mode=ONCE),
            pl.BlockSpec((2, heads, width, n_halo), lambda t, r: (0, 0, 0, 0), pipeline_mode=ONCE),
        ],
        scratch_shapes=[
            pltpu.VMEM((heads, n_keys, width + CLASSES), bf16),
            pltpu.VMEM((heads, width, n_keys), bf16),
            pltpu.VMEM((heads, n_keys, width), bf16),
            pltpu.VMEM((heads, width, n_keys), f32),
            pltpu.VMEM((heads, width, n_keys), f32),
        ],
    )
    return pl.pallas_call(
        body,
        grid_spec=grid,
        out_shape=(
            pltpu.HBM((3, heads, width, n_own), bf16),
            pltpu.HBM((2, heads, width, n_halo), bf16),
        ),
        compiler_params=pltpu.CompilerParams(dimension_semantics=("arbitrary",), vmem_limit_bytes=20 << 20),
        cost_estimate=pl.CostEstimate(
            flops=20 * heads * n_own * 1152 * 64, transcendentals=heads * n_own * 1152, bytes_accessed=8 << 20
        ),
        name="attend_backward",
    )(plan, *place((own, own, own, halo, halo)), query_class, key_class, *place((attended, lse, grad)))


def attention_plan(item_ids, high, low, n_own, n_halo, tile):
    total = item_ids.shape[0]
    chunk = KEY_TILE
    n_keys = n_own + n_halo
    block, half = n_own // 2, n_halo // 2
    position = jnp.arange(total, dtype=jnp.int32)
    opens = jnp.concatenate([jnp.ones((1,), bool), item_ids[1:] != item_ids[:-1]])
    closes = jnp.concatenate([opens[1:], jnp.ones((1,), bool)])
    key_base = high * (total - n_keys)
    row_base = high * (total - n_own)
    starts = jnp.arange(0, total, tile, dtype=jnp.int32)[:, None]
    tile_first = jnp.max(jnp.where(opens & (position <= starts), position, 0), axis=1)
    tile_last = jnp.min(jnp.where(closes & (position >= starts + tile - 1), position + 1, total), axis=1)
    per_block = block // tile

    def local_tiles(values):
        mine = lax.dynamic_slice_in_dim(values, (row_base + low * block) // tile, per_block)
        other = lax.dynamic_slice_in_dim(values, (row_base + (1 - low) * block) // tile, per_block)
        return jnp.concatenate([mine, other]) - key_base

    begin = local_tiles(tile_first) // 128 * 128
    count = (local_tiles(tile_last) - begin + chunk - 1) // chunk
    begin = jnp.minimum(begin, n_keys - count * chunk)
    own_base = high * (n_keys - n_own)
    halo_base = (1 - high) * n_own
    offsets = jnp.stack(
        [
            jnp.stack([own_base + low * block, halo_base + low * half]),
            jnp.stack([own_base + (1 - low) * block, halo_base + (1 - low) * half]),
        ]
    )
    plan = jnp.concatenate([jnp.stack([begin, count], axis=1), offsets]).astype(jnp.int32)
    classes = jnp.arange(CLASSES, dtype=jnp.int32)[:, None] - 1
    row_ids = jnp.concatenate(
        [
            lax.dynamic_slice_in_dim(item_ids, row_base + low * block, block),
            lax.dynamic_slice_in_dim(item_ids, row_base + (1 - low) * block, block),
        ]
    )
    key_ids = lax.dynamic_slice_in_dim(item_ids, key_base, n_keys)
    query_class = jnp.where(row_ids[None] == classes, 0.0, -MASK_ROOT).astype(bf16)
    key_class = jnp.where(key_ids[None] == classes, MASK_ROOT, 0.0).astype(bf16)
    return plan, query_class, key_class


def layer_norm_parts(values, gain_row, shift_row):
    centre = values - jnp.mean(values, axis=-1, keepdims=True)
    inverse = lax.rsqrt(jnp.mean(centre * centre, axis=-1, keepdims=True) + NORM_EPS)
    unit_rows = centre * inverse
    return (unit_rows * gain_row + shift_row, unit_rows, inverse)


def norm_backward(upstream, unit_rows, inverse, gain_row):
    scaled = upstream * gain_row
    centred = scaled - jnp.mean(scaled, axis=-1, keepdims=True)
    return (centred - unit_rows * jnp.mean(scaled * unit_rows, axis=-1, keepdims=True)) * inverse


def adam_update(weight, gradient, first, second, step_rate):
    first_new = BETA_ONE * first + (1.0 - BETA_ONE) * gradient
    second_new = BETA_TWO * second + (1.0 - BETA_TWO) * gradient * gradient
    first_hat = first_new / (1.0 - BETA_ONE**STEP)
    second_hat = second_new / (1.0 - BETA_TWO**STEP)
    weight_new = weight - step_rate * (first_hat / (jnp.sqrt(second_hat) + ADAM_EPS) + DECAY * weight)
    return (weight_new, first_new, second_new)


def learning_rates():
    return (
        2.0 * D ** (-0.5),
        2.0 * max(D // SHORT, 1) ** (-0.5),
        2.0 * D ** (-0.5),
        2.0 * FF ** (-0.5),
        0.4,
        0.4,
    )


def swap(values, axis, stride=1):
    size = lax.axis_size(axis)
    return lax.ppermute(values, axis, [(i, i ^ stride) for i in range(size)])


def bits(axis):
    size = lax.axis_size(axis)
    return [1 << k for k in range(size.bit_length() - 1)]


def sum_all(values):
    for axis in ("lo", "hi", "dp"):
        for stride in bits(axis):
            values = values + swap(values, axis, stride)
    return values


def gather_rows(values, axis):
    index = lax.axis_index(axis)
    tail = values.shape
    held = values[None]
    for stride in reversed(bits(axis)):
        got = swap(held, axis, stride)
        upper = (index // stride) % 2 == 1
        held = jnp.stack([jnp.where(upper, got, held), jnp.where(upper, held, got)], axis=1)
        held = held.reshape((-1,) + tail)
    return held.reshape((-1,) + tail[1:])


def fold_halves(keep, got, axis, stride):
    pairs = keep.shape[0] // 2
    upper = ((lax.axis_index(axis) // stride) % 2).astype(jnp.int32).reshape(1)

    def body(upper_ref, keep_ref, got_ref, next_ref, send_ref):
        is_upper = upper_ref[0] == 1
        for i in range(pairs):
            lower_rows = keep_ref[2 * i] + got_ref[2 * i].astype(f32)
            upper_rows = keep_ref[2 * i + 1] + got_ref[2 * i + 1].astype(f32)
            next_ref[i] = jnp.where(is_upper, upper_rows, lower_rows)
            send_ref[i] = jnp.where(is_upper, lower_rows, upper_rows).astype(bf16)

    shape = (pairs,) + keep.shape[1:]
    whole = lambda size: pl.BlockSpec(size, lambda i, p: (0, 0, 0))
    grid = pltpu.PrefetchScalarGridSpec(
        num_scalar_prefetch=1,
        grid=(1,),
        in_specs=[whole(keep.shape), whole(got.shape)],
        out_specs=[whole(shape), whole(shape)],
    )
    return pl.pallas_call(
        body,
        grid_spec=grid,
        out_shape=(jax.ShapeDtypeStruct(shape, f32), jax.ShapeDtypeStruct(shape, bf16)),
        compiler_params=pltpu.CompilerParams(vmem_limit_bytes=12 << 20),
        cost_estimate=NO_COST,
        name="fold_halves",
    )(upper, keep, got)


def head_gradient_specs(down, halo_down, flat, width):
    chunk, near = down.shape[1] // 2, halo_down.shape[1] // 2
    whole = pl.BlockSpec((chunk, width), lambda i, *p: (0, 0), pipeline_mode=ONCE)
    return [
        pl.BlockSpec((down.shape[0], chunk), lambda i, *p: (0, i)),
        pl.BlockSpec((chunk, width), lambda i, *p: (i, 0)),
        pl.BlockSpec((halo_down.shape[0], near), lambda i, *p: (0, i)),
        pl.BlockSpec((near, width), lambda i, *p: (i, 0)),
        pl.BlockSpec((flat.shape[0], chunk), lambda i, *p: (0, i)),
        whole,
        whole,
    ]


def head_gradient_step(down, own_rows, halo_down, halo_rows, flat, mixed_own, mixed_other, total):
    step = pl.program_id(0)
    columns = down.shape[0]
    queries = columns - halo_down.shape[0]
    own = dot_nn(down[...], own_rows[...])
    halo = dot_nn(halo_down[...], halo_rows[...])

    @pl.when(step == 0)
    def _():
        total[:queries] = own[:queries]
        total[queries:columns] = own[queries:] + halo
        total[columns:] = dot_nn(flat[...], mixed_own[...])

    @pl.when(step == 1)
    def _():
        total[:queries] += own[:queries]
        total[queries:columns] += own[queries:] + halo
        total[columns:] += dot_nn(flat[...], mixed_other[...])


def head_gradient_sent(down, own_rows, halo_down, halo_rows, flat, mixed_own, mixed_other):
    width = own_rows.shape[1]
    shape = (down.shape[0] + flat.shape[0], width)

    def body(*refs):
        head_gradient_step(*refs[:7], refs[8])

        @pl.when(pl.program_id(0) == 1)
        def _():
            refs[7][...] = refs[8][...].astype(bf16)

    return pl.pallas_call(
        body,
        grid=(2,),
        in_specs=head_gradient_specs(down, halo_down, flat, width),
        out_specs=pl.BlockSpec(shape, lambda i: (0, 0)),
        out_shape=pltpu.HBM(shape, bf16),
        scratch_shapes=[pltpu.VMEM(shape, f32)],
        compiler_params=pltpu.CompilerParams(dimension_semantics=("arbitrary",), vmem_limit_bytes=24 << 20),
        cost_estimate=NO_COST,
        name="head_gradient_sent",
    )(*far(down), own_rows, *far(halo_down), halo_rows, flat, mixed_own, mixed_other)


def head_gradient_split(upper, n_blocks, operands, received):
    n_columns, width = received.shape
    rows = width // n_blocks
    down, _, halo_down, _, flat, _, _ = operands

    def body(upper_ref, *refs):
        head_gradient_step(*refs[:7], refs[10])

        @pl.when(pl.program_id(0) == 1)
        def _():
            turned = (refs[10][...] + refs[7][...].astype(f32)).T
            is_upper = upper_ref[0] == 1
            for i in range(n_blocks // 2):
                lower_rows = turned[2 * i * rows : (2 * i + 1) * rows]
                upper_rows = turned[(2 * i + 1) * rows : (2 * i + 2) * rows]
                refs[8][i] = jnp.where(is_upper, upper_rows, lower_rows)
                refs[9][i] = jnp.where(is_upper, lower_rows, upper_rows).astype(bf16)

    shape = (n_blocks // 2, rows, n_columns)
    whole = pl.BlockSpec(shape, lambda i, p: (0, 0, 0))
    grid = pltpu.PrefetchScalarGridSpec(
        num_scalar_prefetch=1,
        grid=(2,),
        in_specs=head_gradient_specs(down, halo_down, flat, width)
        + [pl.BlockSpec((n_columns, width), lambda i, p: (0, 0))],
        out_specs=[whole, whole],
        scratch_shapes=[pltpu.VMEM((n_columns, width), f32)],
    )
    return pl.pallas_call(
        body,
        grid_spec=grid,
        out_shape=(pltpu.HBM(shape, f32), pltpu.HBM(shape, bf16)),
        compiler_params=pltpu.CompilerParams(dimension_semantics=("arbitrary",), vmem_limit_bytes=28 << 20),
        cost_estimate=NO_COST,
        name="head_gradient_split",
    )(upper, *far(down), operands[1], *far(halo_down), *operands[3:], received)


def rows_back(at, pairs, received=()):
    n_rows, width = at.stop - at.start, pairs[0][1].shape[0]
    columns = pairs[0][0].shape[0]
    tile = 256
    first = at.start // tile
    kind = f32 if received else bf16

    def body(*refs):
        total = refs[2 * len(pairs)][...].astype(f32) if received else None
        for k in range(len(pairs)):
            part = dot_nt(refs[2 * k][...].T, refs[2 * k + 1][...])
            total = part if total is None else total + part
        refs[-1][...] = total.astype(kind)

    one_pair = [
        pl.BlockSpec((columns, tile), lambda i: (0, first + i)),
        pl.BlockSpec((width, columns), lambda i: (0, 0), pipeline_mode=ONCE),
    ]
    row_tile = pl.BlockSpec((tile, width), lambda i: (i, 0))
    return pl.pallas_call(
        body,
        grid=(n_rows // tile,),
        in_specs=one_pair * len(pairs) + [row_tile] * len(received),
        out_specs=row_tile,
        out_shape=jax.ShapeDtypeStruct((n_rows, width), kind),
        compiler_params=pltpu.CompilerParams(dimension_semantics=("arbitrary",), vmem_limit_bytes=16 << 20),
        cost_estimate=NO_COST,
        name="rows_back",
    )(*far(*(array for pair in pairs for array in pair)), *received)


def feed_rows(place, hidden, rest, extra=()):
    n_rows, n_columns = hidden.shape
    n_ff = n_columns // 2
    width = rest.shape[1]
    tile = 256

    def body(place_ref, hidden_ref, own_ref, peer_ref, *refs):
        total = dot_nt(hidden_ref[:, :n_ff], own_ref[...]) + dot_nt(hidden_ref[:, n_ff:], peer_ref[...])
        if extra:
            total = refs[0][...].astype(f32) + total + refs[1][...] + refs[2][5:6, :]
        refs[-1][...] = total.astype(bf16)

    rows_of = lambda columns: pl.BlockSpec((tile, columns), lambda i, p: (i, 0))
    weight_of = lambda pick: pl.BlockSpec((None, width, n_ff), lambda i, p: (pick(p[0]), 0, 1), pipeline_mode=ONCE)
    extra_specs = [rows_of(width), rows_of(width), pl.BlockSpec((6, width), lambda i, p: (0, 0))] if extra else []
    grid = pltpu.PrefetchScalarGridSpec(
        num_scalar_prefetch=1,
        grid=(n_rows // tile,),
        in_specs=[rows_of(n_columns), weight_of(lambda h: h), weight_of(lambda h: 1 - h)] + extra_specs,
        out_specs=rows_of(width),
    )
    return pl.pallas_call(
        body,
        grid_spec=grid,
        out_shape=jax.ShapeDtypeStruct((n_rows, width), bf16),
        compiler_params=pltpu.CompilerParams(dimension_semantics=("arbitrary",), vmem_limit_bytes=16 << 20),
        cost_estimate=NO_COST,
        name="feed_rows",
    )(place, *far(hidden, rest, rest, *extra))


def first_norm_back(place, mine, other, pair, tokens, grad_mixed, small_params, early_sums):
    rows, width = tokens.shape
    half = mine.shape[0]
    gap = 2 * rows - 2 * half
    step = 128

    def body(place_ref, mine_ref, other_ref, pair_ref, tok_ref, mixed_ref, small_ref, early_ref, grad_ref, sum_ref, order):
        order[0:gap] = jnp.zeros((gap, width), bf16)
        order[gap + 2 * half :] = jnp.zeros((gap, width), bf16)
        first = pl.multiple_of(gap + place_ref[0] * half, 128)
        second = pl.multiple_of(gap + (1 - place_ref[0]) * half, 128)
        order[pl.ds(first, half)] = mine_ref[...]
        order[pl.ds(second, half)] = other_ref[...]
        take = place_ref[1]
        gain_row = small_ref[0:1, :]
        gain_sum = jnp.zeros((1, width), f32)
        shift_sum = jnp.zeros((1, width), f32)
        for k in range(0, rows, step):
            at = slice(k, k + step)
            back = pair_ref[at] + order[pl.ds(pl.multiple_of(take + k, 128), step)].astype(f32)
            _, unit_rows, inverse = layer_norm_parts(tok_ref[at].astype(f32), 1.0, 0.0)
            gain_sum = gain_sum + jnp.sum(back * unit_rows, axis=0, keepdims=True)
            shift_sum = shift_sum + jnp.sum(back, axis=0, keepdims=True)
            grad_ref[at] = mixed_ref[at] + norm_backward(back, unit_rows, inverse, gain_row)
        sum_ref[...] = early_ref[...]
        sum_ref[0:1, :] = gain_sum
        sum_ref[1:2, :] = shift_sum

    return pl.pallas_call(
        body,
        in_specs=[pl.BlockSpec(memory_space=pltpu.SMEM)] + [VMEM] * 7,
        out_specs=[VMEM, VMEM],
        out_shape=(jax.ShapeDtypeStruct((rows, width), f32), jax.ShapeDtypeStruct((16, width), f32)),
        scratch_shapes=[pltpu.VMEM((2 * gap + 2 * half, width), bf16)],
        compiler_params=pltpu.CompilerParams(vmem_limit_bytes=16 << 20),
        cost_estimate=NO_COST,
        name="first_norm_back",
    )(place, mine, other, pair, tokens, grad_mixed, small_params, early_sums)


def gelu_parts(values):
    normal_cdf = 0.5 * (1.0 + lax.erf(values * (0.5**0.5)))
    return values * normal_cdf, normal_cdf + values * (0.3989422804014327 * jnp.exp(-0.5 * values * values))


def feed_forward(place, rows_in, upstream, rest, bias, with_feed):
    n_rows, width = rows_in.shape
    n_ff = bias.shape[2]
    tile = 256

    def body(place_ref, x_ref, u_ref, rest_ref, bias_ref, hid_ref, pre_ref, back_ref, sum_ref, xt_ref, ut_ref, *feed):
        step = pl.program_id(0)
        x = x_ref[...]
        u = u_ref[...]
        xt_ref[...] = x.T
        ut_ref[...] = u.T
        back = fed = None
        for j in range(2):
            s = place_ref[0] if j == 0 else 1 - place_ref[0]
            columns = slice(j * n_ff, (j + 1) * n_ff)
            up = rest_ref[s, :, :n_ff]
            down = rest_ref[s, :, n_ff : 2 * n_ff]
            hidden, slope = gelu_parts(dot_nn(x, up) + bias_ref[s])
            hidden = hidden.astype(bf16)
            hid_ref[:, columns] = hidden
            grad_pre = (dot_nn(u, down) * slope).astype(bf16)
            if with_feed:
                part = dot_nt(hidden, down)
                fed = part if fed is None else fed + part
            pre_ref[:, columns] = grad_pre
            sums = jnp.sum(grad_pre.astype(f32), axis=0, keepdims=True)
            sum_ref[:, columns] = jnp.where(step == 0, sums, sum_ref[:, columns] + sums)
            part = dot_nt(grad_pre, up)
            back = part if back is None else back + part
        back_ref[...] = back.astype(back_ref.dtype)
        if with_feed:
            feed[0][...] = fed.astype(bf16)

    by_row = lambda columns: pl.BlockSpec((tile, columns), lambda i, p: (i, 0))
    grid = pltpu.PrefetchScalarGridSpec(
        num_scalar_prefetch=1,
        grid=(n_rows // tile,),
        in_specs=[
            by_row(width),
            by_row(width),
            pl.BlockSpec(rest.shape, lambda i, p: (0, 0, 0), pipeline_mode=ONCE),
            pl.BlockSpec(bias.shape, lambda i, p: (0, 0, 0), pipeline_mode=ONCE),
        ],
        out_specs=[
            by_row(2 * n_ff),
            by_row(2 * n_ff),
            by_row(width),
            pl.BlockSpec((1, 2 * n_ff), lambda i, p: (0, 0)),
            pl.BlockSpec((width, tile), lambda i, p: (0, i)),
            pl.BlockSpec((width, tile), lambda i, p: (0, i)),
        ]
        + [by_row(width)] * with_feed,
    )
    return pl.pallas_call(
        body,
        grid_spec=grid,
        out_shape=(
            pltpu.HBM((n_rows, 2 * n_ff), bf16),
            pltpu.HBM((n_rows, 2 * n_ff), bf16),
            jax.ShapeDtypeStruct((n_rows, width), bf16 if with_feed else f32),
            jax.ShapeDtypeStruct((1, 2 * n_ff), f32),
            pltpu.HBM((width, n_rows), bf16),
            pltpu.HBM((width, n_rows), bf16),
        )
        + (jax.ShapeDtypeStruct((n_rows, width), bf16),) * with_feed,
        compiler_params=pltpu.CompilerParams(dimension_semantics=("arbitrary",), vmem_limit_bytes=20 << 20),
        cost_estimate=NO_COST,
        name="feed_forward",
    )(place, rows_in, upstream, *far(rest), bias)


def weight_grads(twos, grad_pres, ups, hiddens):
    width, n_rows = twos[0].shape
    n_ff = hiddens[0].shape[1]
    block = 512
    per = n_ff // block

    def body(x0, x1, p0, p1, u0, u1, h0, h1, out_ref):
        step = pl.program_id(0)

        @pl.when(step < per)
        def _():
            out_ref[...] = (dot_nn(x0[...], p0[...]) + dot_nn(x1[...], p1[...])).astype(bf16)

        @pl.when(step >= per)
        def _():
            out_ref[...] = (dot_nn(u0[...], h0[...]) + dot_nn(u1[...], h1[...])).astype(bf16)

    whole = lambda array: pl.BlockSpec(array.shape, lambda i: (0, 0), pipeline_mode=ONCE)
    early = pl.BlockSpec((n_rows, block), lambda i: (0, jnp.minimum(i, per - 1)))
    late = pl.BlockSpec((n_rows, block), lambda i: (0, jnp.clip(i - per, 0, per - 1)))
    return pl.pallas_call(
        body,
        grid=(2 * per,),
        in_specs=[whole(twos[0])] * 2 + [early] * 2 + [whole(ups[0])] * 2 + [late] * 2,
        out_specs=pl.BlockSpec((width, block), lambda i: (0, i)),
        out_shape=pltpu.HBM((width, 2 * n_ff), bf16),
        compiler_params=pltpu.CompilerParams(dimension_semantics=("arbitrary",), vmem_limit_bytes=16 << 20),
        cost_estimate=NO_COST,
        name="weight_grads",
    )(*twos, *far(*grad_pres), *ups, *far(*hiddens))


def attended_grads(mixed_own, mixed_other, full_out):
    n_rows, width = mixed_own.shape
    columns = full_out.shape[1] // 2

    def body(own_ref, other_ref, out_ref, *grads):
        turned = out_ref[...].T
        for j in range(2):
            part = turned[j * columns : (j + 1) * columns]
            grads[j][:, :n_rows] = dot_nt(part, own_ref[...]).astype(bf16)
            grads[j][:, n_rows:] = dot_nt(part, other_ref[...]).astype(bf16)

    shape = (columns, 2 * n_rows)
    return pl.pallas_call(
        body,
        in_specs=[VMEM] * 3,
        out_specs=[VMEM] * 2,
        out_shape=(jax.ShapeDtypeStruct(shape, bf16),) * 2,
        compiler_params=pltpu.CompilerParams(vmem_limit_bytes=12 << 20),
        cost_estimate=NO_COST,
        name="attended_grads",
    )(mixed_own, mixed_other, full_out)


def second_norm_back(place, pair, received, mixed, upstream_low, small_params, bias_grad):
    rows, width = mixed.shape
    step = 128

    def body(place_ref, pair_ref, got_ref, mixed_ref, up_ref, small_ref, bias_ref, grad_ref, low_ref, sum_ref):
        sums = [jnp.zeros((1, width), f32) for _ in range(4)]
        for k in range(0, rows, step):
            at = slice(k, k + step)
            back = pair_ref[at] + got_ref[at].astype(f32)
            upstream = up_ref[at].astype(f32)
            _, unit_rows, inverse = layer_norm_parts(mixed_ref[at], 1.0, 0.0)
            grad = upstream + norm_backward(back, unit_rows, inverse, small_ref[2:3, :])
            grad_ref[at] = grad
            low_ref[at] = grad.astype(bf16)
            for i, term in enumerate((back * unit_rows, back, grad, upstream)):
                sums[i] = sums[i] + jnp.sum(term, axis=0, keepdims=True)
        sum_ref[...] = jnp.zeros_like(sum_ref)
        for i in range(4):
            sum_ref[i + 2 : i + 3, :] = sums[i]
        for i in range(4):
            own = jnp.where(place_ref[0] == i, bias_ref[0:1, :width], jnp.zeros((1, width), f32))
            peer = jnp.where(place_ref[1] == i, bias_ref[0:1, width:], jnp.zeros((1, width), f32))
            sum_ref[i + 6 : i + 7, :] = own + peer

    return pl.pallas_call(
        body,
        in_specs=[pl.BlockSpec(memory_space=pltpu.SMEM)] + [VMEM] * 6,
        out_specs=[VMEM] * 3,
        out_shape=(
            jax.ShapeDtypeStruct((rows, width), f32),
            jax.ShapeDtypeStruct((rows, width), bf16),
            jax.ShapeDtypeStruct((16, width), f32),
        ),
        compiler_params=pltpu.CompilerParams(vmem_limit_bytes=16 << 20),
        name="second_norm_back",
    )(place, pair, received, mixed, upstream_low, small_params, bias_grad)


def finish_grads(n_data, keep, got, reduced, from_peer, late_sums, n_qkv):
    d_local = reduced.shape[0]
    n_ff = from_peer.shape[1] // 2
    n_out = keep.shape[2] - n_qkv

    def body(keep_ref, got_ref, red_ref, peer_ref, sum_ref, qkv_ref, out_ref, up_ref, down_ref, total_ref):
        heads_grad = keep_ref[0] + got_ref[0].astype(f32)
        qkv_ref[...] = heads_grad[:, :n_qkv]
        out_ref[...] = heads_grad[:, n_qkv:]
        squares = jnp.sum(jnp.square(heads_grad * (1.0 / n_data)), keepdims=True)
        for ref, at, peer_at in ((up_ref, 0, 0), (down_ref, 2 * n_ff, n_ff)):
            grad = red_ref[:, at : at + n_ff].astype(f32) + peer_ref[:, peer_at : peer_at + n_ff].astype(f32)
            ref[...] = grad
            squares = squares + jnp.sum(jnp.square(grad * (1.0 / n_data)), keepdims=True)
        total_ref[...] = sum_ref[...]
        total_ref[10:11, :] = jnp.broadcast_to(squares, (1, sum_ref.shape[1]))

    shapes = [(d_local, n_qkv), (d_local, n_out), (d_local, n_ff), (d_local, n_ff), late_sums.shape]
    return pl.pallas_call(
        body,
        in_specs=[VMEM] * 5,
        out_specs=[VMEM] * 5,
        out_shape=tuple(jax.ShapeDtypeStruct(shape, f32) for shape in shapes),
        compiler_params=pltpu.CompilerParams(vmem_limit_bytes=8 << 20),
        name="finish_grads",
    )(keep, got, reduced, from_peer, late_sums)


def optimizer(n_data, summed, grads, states):
    rates = learning_rates()
    flat = [array for group in states for array in group]
    n_states = len(states)
    heads = grads[0].shape[1] // (3 * HEAD_DIM)

    def body(*refs):
        summed_ref = refs[0]
        grad_refs = refs[1:5]
        state_refs = refs[5 : 5 + 3 * n_states]
        norm_ref = refs[5 + 3 * n_states]
        out_refs = refs[6 + 3 * n_states :]
        small = summed_ref[0:10, :] * (1.0 / n_data)
        total = jnp.sum(small * small, keepdims=True) + summed_ref[10:11, 0:1]
        norm = jnp.sqrt(total)
        norm_ref[...] = norm
        factor = CLIP_NORM / jnp.maximum(norm, CLIP_NORM)

        def update(index, gradient, take=(slice(None), slice(None))):
            w, m, v = (ref[take] for ref in state_refs[3 * index : 3 * index + 3])
            results = adam_update(w, gradient * factor, m, v, rates[index])
            for ref, value in zip(out_refs[3 * index : 3 * index + 3], results):
                ref[take] = value

        for head in range(heads):
            pieces = [
                grad_refs[0][:, (part * heads + head) * HEAD_DIM : (part * heads + head + 1) * HEAD_DIM]
                for part in range(3)
            ]
            at = slice(3 * head * HEAD_DIM, 3 * (head + 1) * HEAD_DIM)
            update(0, jnp.concatenate(pieces, axis=1) * (1.0 / n_data), (slice(None), at))
        update(1, grad_refs[1][...].T * (1.0 / n_data))
        update(2, grad_refs[2][...] * (1.0 / n_data))
        update(3, grad_refs[3][...] * (1.0 / n_data))
        update(4, small[0:6])
        lanes = 128
        bias_grads = [
            small[6 + row : 7 + row, k * lanes : (k + 1) * lanes]
            for row in range(4)
            for k in range(small.shape[1] // lanes)
        ]
        update(5, jnp.concatenate(bias_grads, axis=0))

    whole = lambda array: pl.BlockSpec(array.shape, lambda i: (0,) * len(array.shape))
    return pl.pallas_call(
        body,
        grid=(1,),
        in_specs=[whole(array) for array in (summed, *grads, *flat)],
        out_specs=[pl.BlockSpec((1, 1), lambda i: (0, 0))] + [whole(array) for array in flat],
        out_shape=(
            jax.ShapeDtypeStruct((1, 1), f32),
            *(jax.ShapeDtypeStruct(array.shape, f32) for array in flat),
        ),
        compiler_params=pltpu.CompilerParams(vmem_limit_bytes=16 << 20),
        name="optimizer",
    )(summed, *grads, *flat)


def body(
    tokens,
    cotangent,
    row_item,
    w_qkv,
    w_out,
    w_up,
    w_down,
    small_params,
    up_bias,
    first_qkv,
    first_out,
    first_up,
    first_down,
    first_small,
    first_bias,
    second_qkv,
    second_out,
    second_up,
    second_down,
    second_small,
    second_bias,
):
    rows = tokens.shape[0]
    n_data = lax.axis_size("dp")
    high = lax.axis_index("hi")
    low = lax.axis_index("lo")
    heads_local = w_qkv.shape[1] // (3 * HEAD_DIM)
    head_width = heads_local * HEAD_DIM
    ff_local = w_up.shape[1]
    d_local = w_qkv.shape[0]
    n_own = 2 * rows
    n_halo = LONG - 1
    half = n_halo // 2

    shard_qkv = (
        w_qkv.astype(bf16)
        .reshape(d_local, heads_local, 3, HEAD_DIM)
        .transpose(0, 2, 1, 3)
        .reshape(d_local, 3 * head_width)
    )
    shard_rest = jnp.concatenate([w_up.astype(bf16), w_down.astype(bf16).T, w_out.astype(bf16).T], axis=1)
    qkv_mine = gather_rows(shard_qkv, "dp")
    rest = lax.all_gather(shard_rest, ("hi", "dp"), axis=0, tiled=True).reshape(2, D, -1)
    outs = rest[:, :, 2 * ff_local :]
    full_out = jnp.concatenate(
        [
            lax.dynamic_index_in_dim(outs, high, 0, keepdims=False),
            lax.dynamic_index_in_dim(outs, 1 - high, 0, keepdims=False),
        ],
        axis=1,
    )

    group_row = (2 * high + low) * rows
    own_ids = lax.dynamic_slice_in_dim(row_item, group_row, rows)
    keep_rows = (own_ids >= 0).astype(f32)[:, None]
    residual = tokens.astype(f32)
    normed, _, _ = layer_norm_parts(residual, small_params[0], small_params[1])
    normed = normed.astype(bf16)
    normed_other = swap(normed, "lo")
    send_at = (1 - high) * (512 - 256 * low) + high * low * 1280
    send_rows = lax.dynamic_slice_in_dim(
        jnp.concatenate([normed, normed_other, normed], axis=0), send_at, half, axis=0
    )
    halo_mine = swap(send_rows, "hi")
    halo_other = swap(halo_mine, "lo")
    own_rows = jnp.concatenate([normed, normed_other], axis=0)
    halo_rows = jnp.concatenate([halo_mine, halo_other], axis=0)
    plan, query_class, key_class = attention_plan(row_item, high, low, n_own, n_halo, FORWARD_TILE)
    plan_back, _, _ = attention_plan(row_item, high, low, n_own, n_halo, BACKWARD_TILE)
    plan, plan_back, query_class, key_class, qkv_mine = lax.optimization_barrier(
        (plan, plan_back, query_class, key_class, qkv_mine)
    )

    upstream = cotangent.astype(f32) * keep_rows
    upstream_low = upstream.astype(bf16)
    upstream_low, qkv_mine = lax.optimization_barrier((upstream_low, qkv_mine))
    qkv_theirs = swap(qkv_mine, "hi")
    upstream_other = swap(upstream_low, "lo")
    own_rows, halo_rows = lax.optimization_barrier((own_rows, halo_rows))

    def project(weight):
        own = dot_tt(weight, own_rows).astype(bf16).reshape(3, heads_local, HEAD_DIM, n_own)
        halo = dot_tt(weight[:, head_width:], halo_rows).astype(bf16).reshape(2, heads_local, HEAD_DIM, n_halo)
        return own, halo

    own_m, halo_m = project(qkv_mine)
    att_m, lse_m = attend_forward(plan, own_m, halo_m, query_class, key_class)
    qkv_theirs, att_m = lax.optimization_barrier((qkv_theirs, att_m))
    own_t, halo_t = project(qkv_theirs)
    att_t, lse_t = attend_forward(plan, own_t, halo_t, query_class, key_class)
    flat = jnp.concatenate([att_m, att_t], axis=0).reshape(2 * head_width, n_own)

    first_half, second_half = slice(0, rows), slice(rows, n_own)

    got = swap(dot_tt(flat[:, second_half], full_out).astype(bf16), "lo")
    attention_part, got = lax.optimization_barrier((dot_tt(flat[:, first_half], full_out), got))
    attention_part = attention_part + got.astype(f32)
    mixed = residual + attention_part + small_params[4]
    normed_two, _, _ = layer_norm_parts(mixed, small_params[2], small_params[3])
    normed_two = normed_two.astype(bf16)
    two_other = swap(normed_two, "lo")
    bias_parts = up_bias.reshape(2, 2, ff_local)
    bias_pair = lax.dynamic_index_in_dim(bias_parts, low, 1, keepdims=False).reshape(2, 1, ff_local)
    half_place = high.astype(jnp.int32).reshape(1)
    hidden_o, pre_o, back_o, bias_o, two_t_o, up_t_o, feed_other = feed_forward(
        half_place, two_other, upstream_other, rest, bias_pair, True
    )
    normed_two, back_o, feed_other = lax.optimization_barrier((normed_two, back_o, feed_other))
    two_got = swap(back_o, "lo")
    feed_got = swap(feed_other, "lo")
    hidden_m, pre_m, two_pair, bias_m, two_t_m, up_t_m = feed_forward(
        half_place, normed_two, upstream_low, rest, bias_pair, False
    )
    bias_grad = bias_m + bias_o
    bias_place = jnp.stack([2 * high + low, 2 * (1 - high) + low]).astype(jnp.int32)
    grad_mixed, mixed_low, early_sums = second_norm_back(
        bias_place, two_pair, two_got, mixed, upstream_low, small_params, bias_grad
    )
    mixed_other = swap(mixed_low, "lo")
    grad_rest = weight_grads((two_t_m, two_t_o), (pre_m, pre_o), (up_t_m, up_t_o), (hidden_m, hidden_o))
    grad_rest, mixed_other = lax.optimization_barrier((grad_rest, mixed_other))
    grad_rest = lax.psum_scatter(grad_rest, "dp", scatter_dimension=0, tiled=True)
    att_grad_m, att_grad_t = attended_grads(mixed_low, mixed_other, full_out)
    att_grad_m = att_grad_m.reshape(heads_local, HEAD_DIM, n_own)
    att_grad_t = att_grad_t.reshape(heads_local, HEAD_DIM, n_own)

    down_t, halo_down_t = attend_backward(
        plan_back, own_t, halo_t, query_class, key_class, att_t, lse_t, att_grad_t
    )
    down_t = down_t.reshape(3 * head_width, n_own)
    halo_down_t = halo_down_t.reshape(2 * head_width, n_halo)

    flat_m, flat_t = flat[:head_width], flat[head_width:]
    qkv_for_peer = head_gradient_sent(
        down_t, own_rows, halo_down_t, halo_rows, flat_t, mixed_low, mixed_other
    )
    qkv_for_peer, att_grad_m = lax.optimization_barrier((qkv_for_peer, att_grad_m))
    qkv_from_peer = swap(qkv_for_peer, "hi")
    down_m, halo_down_m = attend_backward(
        plan_back, own_m, halo_m, query_class, key_class, att_m, lse_m, att_grad_m, lambda arrays: far(*arrays)
    )
    down_m = down_m.reshape(3 * head_width, n_own)
    halo_down_m = halo_down_m.reshape(2 * head_width, n_halo)

    def halo_part(at):
        return dot_tt(halo_down_t[:, at], qkv_theirs[:, head_width:]) + dot_tt(
            halo_down_m[:, at], qkv_mine[:, head_width:]
        )

    strides = bits("dp")
    pairs = ((down_t, qkv_theirs), (down_m, qkv_mine))
    halo_got = swap(halo_part(slice(half, n_halo)).astype(bf16), "lo").astype(f32)
    back_sent = rows_back(second_half, pairs)
    back_sent, qkv_from_peer = lax.optimization_barrier((back_sent, qkv_from_peer))
    back_got = swap(back_sent, "lo")
    upper = (lax.axis_index("dp") % 2).astype(jnp.int32).reshape(1)
    operands = (down_m, own_rows, halo_down_m, halo_rows, flat_m, mixed_low, mixed_other)
    keep, send = head_gradient_split(upper, n_data, operands, qkv_from_peer)
    halo_send = (halo_part(slice(0, half)) + halo_got).astype(bf16)
    send, down_m, hidden, back_got = lax.optimization_barrier((send, down_m, hidden_m, back_got))
    got = swap(send, "dp", strides[0])
    back_mine = swap(halo_send, "hi")
    back_pair = rows_back(first_half, ((down_t, qkv_theirs), (down_m, qkv_mine)), (back_got,))
    output = feed_rows(half_place, hidden, rest, (feed_got, mixed, small_params))
    got, back_mine, back_pair, output = lax.optimization_barrier((got, back_mine, back_pair, output))
    keep, send = fold_halves(keep, got, "dp", strides[1])
    got = swap(send, "dp", strides[1])
    back_other = swap(back_mine, "lo")
    theirs = jnp.concatenate(
        [grad_rest[:, ff_local : 2 * ff_local], grad_rest[:, 3 * ff_local : 4 * ff_local]], axis=1
    )
    got, back_other, theirs = lax.optimization_barrier((got, back_other, theirs))
    from_peer = swap(theirs, "hi")
    keep, send = fold_halves(keep, got, "dp", strides[2])
    send, back_other = lax.optimization_barrier((send, back_other))
    got = swap(send, "dp", strides[2])
    place = jnp.stack([low, high * (n_own - n_halo) + low * rows]).astype(jnp.int32)
    input_grad, late_sums = first_norm_back(
        place, back_mine, back_other, back_pair, tokens, grad_mixed, small_params, early_sums
    )
    got, late_sums = lax.optimization_barrier((got, late_sums))
    for stride in strides[3:]:
        keep, send = fold_halves(keep, got, "dp", stride)
        got = swap(send, "dp", stride)
    *grads, summed = finish_grads(n_data, keep, got, grad_rest, from_peer, late_sums, 3 * head_width)
    summed = sum_all(summed)
    norm, *updated = optimizer(
        n_data,
        summed,
        grads,
        (
            (w_qkv, first_qkv, second_qkv),
            (w_out, first_out, second_out),
            (w_up, first_up, second_up),
            (w_down.T, first_down.T, second_down.T),
            (small_params, first_small, second_small),
            tuple(array.reshape(-1, 128) for array in (up_bias, first_bias, second_bias)),
        ),
    )
    updated[9:12] = [array.T for array in updated[9:12]]
    updated[15:18] = [array.reshape(-1) for array in updated[15:18]]
    return (output, input_grad, norm[0, 0], *updated)


def solution(mesh):
    n_data, n_model = mesh.devices.shape
    split = Mesh(mesh.devices.reshape(n_data, 2, n_model // 2), ("dp", "hi", "lo"))
    model = ("hi", "lo")
    rows = P(("dp", "hi", "lo"), None)
    by_row = P("dp", model)
    by_column = P(model, "dp")
    states = (by_row, by_column, by_row, by_column, P(), P())
    in_specs = (rows, rows, P("dp"), *states, *states, *states)
    updated = []
    for spec in states:
        updated.extend([spec, spec, spec])
    out_specs = (rows, rows, P(), *updated)
    return jax.shard_map(body, mesh=split, in_specs=in_specs, out_specs=out_specs, check_vma=False)
```

```python
import jax
import jax.numpy as jnp
from jax import lax
from jax.experimental import pallas as pl
from jax.experimental.pallas import tpu as pltpu
from jax.sharding import Mesh, PartitionSpec as P

HEAD_DIM = 64
FF = 3072
D = 768
SHORT = 257
LONG = 1025
STEP = 5

CLIP_NORM = 1.0
BETA_ONE = 0.9
BETA_TWO = 0.999
ADAM_EPS = 1e-08
DECAY = 0.03
NORM_EPS = 1e-05

LOG2E = 1.4426950408889634
MASK_ROOT = 2.0**20
CLASSES = 16
FORWARD_TILE = 384
BACKWARD_TILE = 256
KEY_TILE = 384

bf16 = jnp.bfloat16
ONCE = pl.Buffered(1)
NO_COST = pl.CostEstimate(flops=0, transcendentals=0, bytes_accessed=0)
VMEM = pl.BlockSpec(memory_space=pltpu.VMEM)
f32 = jnp.float32


def far(*arrays):
    return [pltpu.with_memory_space_constraint(array, pltpu.HBM) for array in arrays]


def dot_nn(left, right):
    return lax.dot_general(left, right, (((1,), (0,)), ((), ())), preferred_element_type=f32)


def dot_nt(left, right):
    return lax.dot_general(left, right, (((1,), (1,)), ((), ())), preferred_element_type=f32)


def dot_tn(left, right):
    return lax.dot_general(left, right, (((0,), (0,)), ((), ())), preferred_element_type=f32)


def dot_tt(left, right):
    return lax.dot_general(left, right, (((0,), (1,)), ((), ())), preferred_element_type=f32)


def attend_forward(plan, own, halo, query_class, key_class):
    _, heads, width, n_own = own.shape
    n_halo = halo.shape[-1]
    n_keys = n_own + n_halo
    tile, chunk = FORWARD_TILE, KEY_TILE
    n_tiles = n_own // tile
    block, half = n_own // 2, n_halo // 2

    def body(plan_ref, q_ref, own_k, own_v, halo_k, halo_v, qc_ref, kc_ref, out_ref, lse_ref, keys, values):
        step = pl.program_id(0)

        @pl.when(step == 0)
        def _():
            ones = (lax.broadcasted_iota(jnp.int32, (CLASSES, n_keys), 0) == 0).astype(bf16)
            for head in range(heads):
                for part in range(2):
                    to = pl.ds(pl.multiple_of(plan_ref[n_tiles + part, 0], 128), block)
                    cut = slice(part * block, (part + 1) * block)
                    values[head, :width, to] = own_v[head, :, cut]
                    keys[head, to, :width] = own_k[head, :, cut].T
                    to = pl.ds(pl.multiple_of(plan_ref[n_tiles + part, 1], 128), half)
                    cut = slice(part * half, (part + 1) * half)
                    values[head, :width, to] = halo_v[head, :, cut]
                    keys[head, to, :width] = halo_k[head, :, cut].T
                values[head, width:, :] = ones
                keys[head, :, width:] = kc_ref[...].T

        first = plan_ref[step, 0]
        scale = jnp.asarray(width**-0.5, bf16)
        queries = [jnp.concatenate([q_ref[h] * scale, qc_ref[...]], axis=0) for h in range(heads)]

        def one_chunk(index, carry):
            at = pl.ds(pl.multiple_of(first + index * chunk, 128), chunk)
            scores = [dot_nn(keys[h, at, :], queries[h]) for h in range(heads)]
            result = []
            for h in range(heads):
                top, total = carry[h]
                new_top = jnp.maximum(top, jnp.max(scores[h], axis=0, keepdims=True))
                probs = jnp.exp2((scores[h] - new_top) * LOG2E)
                fade = jnp.exp2((top - new_top) * LOG2E)
                result.append((new_top, total * fade + dot_nn(values[h, :, at], probs.astype(bf16))))
            return tuple(result)

        start = tuple(
            (jnp.full((1, tile), -3e38, f32), jnp.zeros((width + CLASSES, tile), f32)) for _ in range(heads)
        )
        ends = lax.fori_loop(0, plan_ref[step, 1], one_chunk, start)
        for h in range(heads):
            top, total = ends[h]
            row_sum = total[width : width + 1]
            out_ref[h] = (total[:width] / row_sum).astype(bf16)
            lse_ref[h] = top + jnp.log(row_sum)

    whole_own = lambda p: pl.BlockSpec((None, heads, width, n_own), lambda t, r: (p, 0, 0, 0), pipeline_mode=ONCE)
    whole_halo = lambda p: pl.BlockSpec((None, heads, width, n_halo), lambda t, r: (p, 0, 0, 0), pipeline_mode=ONCE)
    tiled = lambda rows: pl.BlockSpec((heads, rows, tile), lambda t, r: (0, 0, t))
    grid = pltpu.PrefetchScalarGridSpec(
        num_scalar_prefetch=1,
        grid=(n_tiles,),
        in_specs=[
            pl.BlockSpec((None, heads, width, tile), lambda t, r: (0, 0, 0, t)),
            whole_own(1),
            whole_own(2),
            whole_halo(0),
            whole_halo(1),
            pl.BlockSpec((CLASSES, tile), lambda t, r: (0, t)),
            pl.BlockSpec((CLASSES, n_keys), lambda t, r: (0, 0), pipeline_mode=ONCE),
        ],
        out_specs=[tiled(width), tiled(1)],
        scratch_shapes=[
            pltpu.VMEM((heads, n_keys, width + CLASSES), bf16),
            pltpu.VMEM((heads, width + CLASSES, n_keys), bf16),
        ],
    )
    return pl.pallas_call(
        body,
        grid_spec=grid,
        out_shape=(
            jax.ShapeDtypeStruct((heads, width, n_own), bf16),
            jax.ShapeDtypeStruct((heads, 1, n_own), f32),
        ),
        compiler_params=pltpu.CompilerParams(dimension_semantics=("arbitrary",), vmem_limit_bytes=20 << 20),
        cost_estimate=pl.CostEstimate(
            flops=8 * heads * n_own * 1152 * 64, transcendentals=heads * n_own * 1152, bytes_accessed=4 << 20
        ),
        name="attend_forward",
    )(plan, own, own, own, halo, halo, query_class, key_class)


def attend_backward(plan, own, halo, query_class, key_class, attended, lse, grad, place=list):
    _, heads, width, n_own = own.shape
    n_halo = halo.shape[-1]
    n_keys = n_own + n_halo
    tile, chunk = BACKWARD_TILE, KEY_TILE
    n_tiles = n_own // tile
    block, half = n_own // 2, n_halo // 2
    scale = width**-0.5

    def body(
        plan_ref, q_ref, own_k, own_v, halo_k, halo_v, qc_ref, kc_ref, att_ref, lse_ref, grad_ref,
        own_out, halo_out, keys, keys_t, values, key_sum, value_sum,
    ):
        step = pl.program_id(0)

        def places(part):
            return (
                pl.ds(pl.multiple_of(plan_ref[n_tiles + part, 0], 128), block),
                slice(part * block, (part + 1) * block),
                pl.ds(pl.multiple_of(plan_ref[n_tiles + part, 1], 128), half),
                slice(part * half, (part + 1) * half),
            )

        @pl.when(step == 0)
        def _():
            for head in range(heads):
                for part in range(2):
                    to, cut, to_halo, cut_halo = places(part)
                    keys_t[head, :, to] = own_k[head, :, cut]
                    keys[head, to, :width] = own_k[head, :, cut].T
                    values[head, to, :] = own_v[head, :, cut].T
                    keys_t[head, :, to_halo] = halo_k[head, :, cut_halo]
                    keys[head, to_halo, :width] = halo_k[head, :, cut_halo].T
                    values[head, to_halo, :] = halo_v[head, :, cut_halo].T
                keys[head, :, width:] = kc_ref[...].T
            key_sum[...] = jnp.zeros_like(key_sum)
            value_sum[...] = jnp.zeros_like(value_sum)

        first = plan_ref[step, 0]
        scaled = [q_ref[h] * jnp.asarray(scale, bf16) for h in range(heads)]
        queries = [jnp.concatenate([scaled[h], qc_ref[...]], axis=0) for h in range(heads)]
        grads = [grad_ref[h] for h in range(heads)]
        logs = [lse_ref[h] * LOG2E for h in range(heads)]
        deltas = [
            jnp.sum(grads[h].astype(f32) * att_ref[h].astype(f32), axis=0, keepdims=True) for h in range(heads)
        ]

        def one_chunk(index, carry):
            at = pl.ds(pl.multiple_of(first + index * chunk, 128), chunk)
            scores = [dot_nn(keys[h, at, :], queries[h]) for h in range(heads)]
            grad_probs = [dot_nn(values[h, at, :], grads[h]) for h in range(heads)]
            result = []
            for h in range(heads):
                probs = jnp.exp2(scores[h] * LOG2E - logs[h])
                grad_scores = (probs * (grad_probs[h] - deltas[h])).astype(bf16)
                value_sum[h, :, at] += dot_nt(grads[h], probs.astype(bf16))
                key_sum[h, :, at] += dot_nt(scaled[h], grad_scores)
                result.append(carry[h] + dot_nn(keys_t[h, :, at], grad_scores))
            return tuple(result)

        start = tuple(jnp.zeros((width, tile), f32) for _ in range(heads))
        ends = lax.fori_loop(0, plan_ref[step, 1], one_chunk, start)
        at_tile = pl.ds(pl.multiple_of(step * tile, 128), tile)
        for h in range(heads):
            own_out[0, h, :, at_tile] = (ends[h] * scale).astype(bf16)

        @pl.when(step == n_tiles - 1)
        def _():
            for head in range(heads):
                for part in range(2):
                    to, cut, to_halo, cut_halo = places(part)
                    own_out[1, head, :, cut] = key_sum[head, :, to].astype(bf16)
                    own_out[2, head, :, cut] = value_sum[head, :, to].astype(bf16)
                    halo_out[0, head, :, cut_halo] = key_sum[head, :, to_halo].astype(bf16)
                    halo_out[1, head, :, cut_halo] = value_sum[head, :, to_halo].astype(bf16)

    whole_own = lambda p: pl.BlockSpec((None, heads, width, n_own), lambda t, r: (p, 0, 0, 0), pipeline_mode=ONCE)
    whole_halo = lambda p: pl.BlockSpec((None, heads, width, n_halo), lambda t, r: (p, 0, 0, 0), pipeline_mode=ONCE)
    tiled = lambda rows: pl.BlockSpec((heads, rows, tile), lambda t, r: (0, 0, t))
    grid = pltpu.PrefetchScalarGridSpec(
        num_scalar_prefetch=1,
        grid=(n_tiles,),
        in_specs=[
            pl.BlockSpec((None, heads, width, tile), lambda t, r: (0, 0, 0, t)),
            whole_own(1),
            whole_own(2),
            whole_halo(0),
            whole_halo(1),
            pl.BlockSpec((CLASSES, tile), lambda t, r: (0, t)),
            pl.BlockSpec((CLASSES, n_keys), lambda t, r: (0, 0), pipeline_mode=ONCE),
            tiled(width),
            tiled(1),
            tiled(width),
        ],
        out_specs=[
            pl.BlockSpec((3, heads, width, n_own), lambda t, r: (0, 0, 0, 0), pipeline_mode=ONCE),
            pl.BlockSpec((2, heads, width, n_halo), lambda t, r: (0, 0, 0, 0), pipeline_mode=ONCE),
        ],
        scratch_shapes=[
            pltpu.VMEM((heads, n_keys, width + CLASSES), bf16),
            pltpu.VMEM((heads, width, n_keys), bf16),
            pltpu.VMEM((heads, n_keys, width), bf16),
            pltpu.VMEM((heads, width, n_keys), f32),
            pltpu.VMEM((heads, width, n_keys), f32),
        ],
    )
    return pl.pallas_call(
        body,
        grid_spec=grid,
        out_shape=(
            pltpu.HBM((3, heads, width, n_own), bf16),
            pltpu.HBM((2, heads, width, n_halo), bf16),
        ),
        compiler_params=pltpu.CompilerParams(dimension_semantics=("arbitrary",), vmem_limit_bytes=20 << 20),
        cost_estimate=pl.CostEstimate(
            flops=20 * heads * n_own * 1152 * 64, transcendentals=heads * n_own * 1152, bytes_accessed=8 << 20
        ),
        name="attend_backward",
    )(plan, *place((own, own, own, halo, halo)), query_class, key_class, *place((attended, lse, grad)))


def attention_plan(item_ids, high, low, n_own, n_halo, tile):
    total = item_ids.shape[0]
    chunk = KEY_TILE
    n_keys = n_own + n_halo
    block, half = n_own // 2, n_halo // 2
    position = jnp.arange(total, dtype=jnp.int32)
    opens = jnp.concatenate([jnp.ones((1,), bool), item_ids[1:] != item_ids[:-1]])
    closes = jnp.concatenate([opens[1:], jnp.ones((1,), bool)])
    key_base = high * (total - n_keys)
    row_base = high * (total - n_own)
    starts = jnp.arange(0, total, tile, dtype=jnp.int32)[:, None]
    tile_first = jnp.max(jnp.where(opens & (position <= starts), position, 0), axis=1)
    tile_last = jnp.min(jnp.where(closes & (position >= starts + tile - 1), position + 1, total), axis=1)
    per_block = block // tile

    def local_tiles(values):
        mine = lax.dynamic_slice_in_dim(values, (row_base + low * block) // tile, per_block)
        other = lax.dynamic_slice_in_dim(values, (row_base + (1 - low) * block) // tile, per_block)
        return jnp.concatenate([mine, other]) - key_base

    begin = local_tiles(tile_first) // 128 * 128
    count = (local_tiles(tile_last) - begin + chunk - 1) // chunk
    begin = jnp.minimum(begin, n_keys - count * chunk)
    own_base = high * (n_keys - n_own)
    halo_base = (1 - high) * n_own
    offsets = jnp.stack(
        [
            jnp.stack([own_base + low * block, halo_base + low * half]),
            jnp.stack([own_base + (1 - low) * block, halo_base + (1 - low) * half]),
        ]
    )
    plan = jnp.concatenate([jnp.stack([begin, count], axis=1), offsets]).astype(jnp.int32)
    classes = jnp.arange(CLASSES, dtype=jnp.int32)[:, None] - 1
    row_ids = jnp.concatenate(
        [
            lax.dynamic_slice_in_dim(item_ids, row_base + low * block, block),
            lax.dynamic_slice_in_dim(item_ids, row_base + (1 - low) * block, block),
        ]
    )
    key_ids = lax.dynamic_slice_in_dim(item_ids, key_base, n_keys)
    query_class = jnp.where(row_ids[None] == classes, 0.0, -MASK_ROOT).astype(bf16)
    key_class = jnp.where(key_ids[None] == classes, MASK_ROOT, 0.0).astype(bf16)
    return plan, query_class, key_class


def layer_norm_parts(values, gain_row, shift_row):
    centre = values - jnp.mean(values, axis=-1, keepdims=True)
    inverse = lax.rsqrt(jnp.mean(centre * centre, axis=-1, keepdims=True) + NORM_EPS)
    unit_rows = centre * inverse
    return (unit_rows * gain_row + shift_row, unit_rows, inverse)


def norm_backward(upstream, unit_rows, inverse, gain_row):
    scaled = upstream * gain_row
    centred = scaled - jnp.mean(scaled, axis=-1, keepdims=True)
    return (centred - unit_rows * jnp.mean(scaled * unit_rows, axis=-1, keepdims=True)) * inverse


def adam_update(weight, gradient, first, second, step_rate):
    first_new = BETA_ONE * first + (1.0 - BETA_ONE) * gradient
    second_new = BETA_TWO * second + (1.0 - BETA_TWO) * gradient * gradient
    first_hat = first_new / (1.0 - BETA_ONE**STEP)
    second_hat = second_new / (1.0 - BETA_TWO**STEP)
    weight_new = weight - step_rate * (first_hat / (jnp.sqrt(second_hat) + ADAM_EPS) + DECAY * weight)
    return (weight_new, first_new, second_new)


def learning_rates():
    return (
        2.0 * D ** (-0.5),
        2.0 * max(D // SHORT, 1) ** (-0.5),
        2.0 * D ** (-0.5),
        2.0 * FF ** (-0.5),
        0.4,
        0.4,
    )


def swap(values, axis, stride=1):
    size = lax.axis_size(axis)
    return lax.ppermute(values, axis, [(i, i ^ stride) for i in range(size)])


def bits(axis):
    size = lax.axis_size(axis)
    return [1 << k for k in range(size.bit_length() - 1)]


def sum_all(values):
    for axis in ("lo", "hi", "dp"):
        for stride in bits(axis):
            values = values + swap(values, axis, stride)
    return values


def gather_rows(values, axis):
    index = lax.axis_index(axis)
    tail = values.shape
    held = values[None]
    for stride in reversed(bits(axis)):
        got = swap(held, axis, stride)
        upper = (index // stride) % 2 == 1
        held = jnp.stack([jnp.where(upper, got, held), jnp.where(upper, held, got)], axis=1)
        held = held.reshape((-1,) + tail)
    return held.reshape((-1,) + tail[1:])


def rest_shard(up, down, out):
    rows, n_ff = up.shape
    n_out = out.shape[0]

    def body(up_ref, down_ref, out_ref, rest_ref):
        rest_ref[:, :n_ff] = up_ref[...].astype(bf16)
        rest_ref[:, n_ff : 2 * n_ff] = down_ref[...].astype(bf16)
        rest_ref[:, 2 * n_ff :] = out_ref[...].T.astype(bf16)

    whole = lambda array: pl.BlockSpec(array.shape, lambda i: (0, 0))
    shape = (rows, 2 * n_ff + n_out)
    return pl.pallas_call(
        body,
        grid=(1,),
        in_specs=[whole(up), whole(down), whole(out)],
        out_specs=pl.BlockSpec(shape, lambda i: (0, 0)),
        out_shape=pltpu.HBM(shape, bf16),
        compiler_params=pltpu.CompilerParams(vmem_limit_bytes=8 << 20),
        cost_estimate=NO_COST,
        name="rest_shard",
    )(*far(up, down, out))


def fold_halves(keep, got, axis, stride):
    pairs = keep.shape[0] // 2
    upper = ((lax.axis_index(axis) // stride) % 2).astype(jnp.int32).reshape(1)

    def body(upper_ref, keep_ref, got_ref, next_ref, send_ref):
        is_upper = upper_ref[0] == 1
        for i in range(pairs):
            lower_rows = keep_ref[2 * i] + got_ref[2 * i].astype(f32)
            upper_rows = keep_ref[2 * i + 1] + got_ref[2 * i + 1].astype(f32)
            next_ref[i] = jnp.where(is_upper, upper_rows, lower_rows)
            send_ref[i] = jnp.where(is_upper, lower_rows, upper_rows).astype(bf16)

    shape = (pairs,) + keep.shape[1:]
    whole = lambda size: pl.BlockSpec(size, lambda i, p: (0, 0, 0))
    grid = pltpu.PrefetchScalarGridSpec(
        num_scalar_prefetch=1,
        grid=(1,),
        in_specs=[whole(keep.shape), whole(got.shape)],
        out_specs=[whole(shape), whole(shape)],
    )
    return pl.pallas_call(
        body,
        grid_spec=grid,
        out_shape=(jax.ShapeDtypeStruct(shape, f32), jax.ShapeDtypeStruct(shape, bf16)),
        compiler_params=pltpu.CompilerParams(vmem_limit_bytes=12 << 20),
        cost_estimate=NO_COST,
        name="fold_halves",
    )(upper, keep, got)


def head_gradient_specs(down, halo_down, flat, width):
    chunk, near = down.shape[1] // 2, halo_down.shape[1] // 2
    whole = pl.BlockSpec((chunk, width), lambda i, *p: (0, 0), pipeline_mode=ONCE)
    return [
        pl.BlockSpec((down.shape[0], chunk), lambda i, *p: (0, i)),
        pl.BlockSpec((chunk, width), lambda i, *p: (i, 0)),
        pl.BlockSpec((halo_down.shape[0], near), lambda i, *p: (0, i)),
        pl.BlockSpec((near, width), lambda i, *p: (i, 0)),
        pl.BlockSpec((flat.shape[0], chunk), lambda i, *p: (0, i)),
        whole,
        whole,
    ]


def head_gradient_step(down, own_rows, halo_down, halo_rows, flat, mixed_own, mixed_other, total):
    step = pl.program_id(0)
    columns = down.shape[0]
    queries = columns - halo_down.shape[0]
    own = dot_nn(down[...], own_rows[...])
    halo = dot_nn(halo_down[...], halo_rows[...])

    @pl.when(step == 0)
    def _():
        total[:queries] = own[:queries]
        total[queries:columns] = own[queries:] + halo
        total[columns:] = dot_nn(flat[...], mixed_own[...])

    @pl.when(step == 1)
    def _():
        total[:queries] += own[:queries]
        total[queries:columns] += own[queries:] + halo
        total[columns:] += dot_nn(flat[...], mixed_other[...])


def head_gradient_sent(down, own_rows, halo_down, halo_rows, flat, mixed_own, mixed_other):
    width = own_rows.shape[1]
    shape = (down.shape[0] + flat.shape[0], width)

    def body(*refs):
        head_gradient_step(*refs[:7], refs[8])

        @pl.when(pl.program_id(0) == 1)
        def _():
            refs[7][...] = refs[8][...].astype(bf16)

    return pl.pallas_call(
        body,
        grid=(2,),
        in_specs=head_gradient_specs(down, halo_down, flat, width),
        out_specs=pl.BlockSpec(shape, lambda i: (0, 0)),
        out_shape=pltpu.HBM(shape, bf16),
        scratch_shapes=[pltpu.VMEM(shape, f32)],
        compiler_params=pltpu.CompilerParams(dimension_semantics=("arbitrary",), vmem_limit_bytes=24 << 20),
        cost_estimate=NO_COST,
        name="head_gradient_sent",
    )(*far(down), own_rows, *far(halo_down), halo_rows, flat, mixed_own, mixed_other)


def head_gradient_split(upper, n_blocks, operands, received):
    n_columns, width = received.shape
    rows = width // n_blocks
    down, _, halo_down, _, flat, _, _ = operands

    def body(upper_ref, *refs):
        head_gradient_step(*refs[:7], refs[10])

        @pl.when(pl.program_id(0) == 1)
        def _():
            turned = (refs[10][...] + refs[7][...].astype(f32)).T
            is_upper = upper_ref[0] == 1
            for i in range(n_blocks // 2):
                lower_rows = turned[2 * i * rows : (2 * i + 1) * rows]
                upper_rows = turned[(2 * i + 1) * rows : (2 * i + 2) * rows]
                refs[8][i] = jnp.where(is_upper, upper_rows, lower_rows)
                refs[9][i] = jnp.where(is_upper, lower_rows, upper_rows).astype(bf16)

    shape = (n_blocks // 2, rows, n_columns)
    whole = pl.BlockSpec(shape, lambda i, p: (0, 0, 0))
    grid = pltpu.PrefetchScalarGridSpec(
        num_scalar_prefetch=1,
        grid=(2,),
        in_specs=head_gradient_specs(down, halo_down, flat, width)
        + [pl.BlockSpec((n_columns, width), lambda i, p: (0, 0))],
        out_specs=[whole, whole],
        scratch_shapes=[pltpu.VMEM((n_columns, width), f32)],
    )
    return pl.pallas_call(
        body,
        grid_spec=grid,
        out_shape=(pltpu.HBM(shape, f32), pltpu.HBM(shape, bf16)),
        compiler_params=pltpu.CompilerParams(dimension_semantics=("arbitrary",), vmem_limit_bytes=28 << 20),
        cost_estimate=NO_COST,
        name="head_gradient_split",
    )(upper, *far(down), operands[1], *far(halo_down), *operands[3:], received)


def rows_back(at, pairs, received=()):
    n_rows, width = at.stop - at.start, pairs[0][1].shape[0]
    pairs = [(down, weight.T) for down, weight in pairs]
    columns = pairs[0][0].shape[0]
    tile = 256
    first = at.start // tile
    kind = f32 if received else bf16

    def body(*refs):
        total = refs[2 * len(pairs)][...].astype(f32) if received else None
        for k in range(len(pairs)):
            part = dot_nn(refs[2 * k][...].T, refs[2 * k + 1][...])
            total = part if total is None else total + part
        refs[-1][...] = total.astype(kind)

    one_pair = [
        pl.BlockSpec((columns, tile), lambda i: (0, first + i)),
        pl.BlockSpec((columns, width), lambda i: (0, 0), pipeline_mode=ONCE),
    ]
    row_tile = pl.BlockSpec((tile, width), lambda i: (i, 0))
    return pl.pallas_call(
        body,
        grid=(n_rows // tile,),
        in_specs=one_pair * len(pairs) + [row_tile] * len(received),
        out_specs=row_tile,
        out_shape=jax.ShapeDtypeStruct((n_rows, width), kind),
        compiler_params=pltpu.CompilerParams(dimension_semantics=("arbitrary",), vmem_limit_bytes=16 << 20),
        cost_estimate=NO_COST,
        name="rows_back",
    )(*far(*(array for pair in pairs for array in pair)), *received)


def feed_rows(place, hidden, rest, extra=()):
    n_rows, n_columns = hidden.shape
    n_ff = n_columns // 2
    width = rest.shape[1]
    tile = 256

    def body(place_ref, hidden_ref, own_ref, peer_ref, *refs):
        total = dot_nt(hidden_ref[:, :n_ff], own_ref[...]) + dot_nt(hidden_ref[:, n_ff:], peer_ref[...])
        if extra:
            total = refs[0][...].astype(f32) + total + refs[1][...] + refs[2][5:6, :]
        refs[-1][...] = total.astype(bf16)

    rows_of = lambda columns: pl.BlockSpec((tile, columns), lambda i, p: (i, 0))
    weight_of = lambda pick: pl.BlockSpec((None, width, n_ff), lambda i, p: (pick(p[0]), 0, 1), pipeline_mode=ONCE)
    extra_specs = [rows_of(width), rows_of(width), pl.BlockSpec((6, width), lambda i, p: (0, 0))] if extra else []
    grid = pltpu.PrefetchScalarGridSpec(
        num_scalar_prefetch=1,
        grid=(n_rows // tile,),
        in_specs=[rows_of(n_columns), weight_of(lambda h: h), weight_of(lambda h: 1 - h)] + extra_specs,
        out_specs=rows_of(width),
    )
    return pl.pallas_call(
        body,
        grid_spec=grid,
        out_shape=jax.ShapeDtypeStruct((n_rows, width), bf16),
        compiler_params=pltpu.CompilerParams(dimension_semantics=("arbitrary",), vmem_limit_bytes=16 << 20),
        cost_estimate=NO_COST,
        name="feed_rows",
    )(place, *far(hidden, rest, rest, *extra))


def first_norm_back(place, mine, other, pair, tokens, grad_mixed, small_params, early_sums):
    rows, width = tokens.shape
    half = mine.shape[0]
    gap = 2 * rows - 2 * half
    step = 128

    def body(place_ref, mine_ref, other_ref, pair_ref, tok_ref, mixed_ref, small_ref, early_ref, grad_ref, sum_ref, order):
        order[0:gap] = jnp.zeros((gap, width), bf16)
        order[gap + 2 * half :] = jnp.zeros((gap, width), bf16)
        first = pl.multiple_of(gap + place_ref[0] * half, 128)
        second = pl.multiple_of(gap + (1 - place_ref[0]) * half, 128)
        order[pl.ds(first, half)] = mine_ref[...]
        order[pl.ds(second, half)] = other_ref[...]
        take = place_ref[1]
        gain_row = small_ref[0:1, :]
        gain_sum = jnp.zeros((1, width), f32)
        shift_sum = jnp.zeros((1, width), f32)
        for k in range(0, rows, step):
            at = slice(k, k + step)
            back = pair_ref[at] + order[pl.ds(pl.multiple_of(take + k, 128), step)].astype(f32)
            _, unit_rows, inverse = layer_norm_parts(tok_ref[at].astype(f32), 1.0, 0.0)
            gain_sum = gain_sum + jnp.sum(back * unit_rows, axis=0, keepdims=True)
            shift_sum = shift_sum + jnp.sum(back, axis=0, keepdims=True)
            grad_ref[at] = mixed_ref[at] + norm_backward(back, unit_rows, inverse, gain_row)
        sum_ref[...] = early_ref[...]
        sum_ref[0:1, :] = gain_sum
        sum_ref[1:2, :] = shift_sum

    return pl.pallas_call(
        body,
        in_specs=[pl.BlockSpec(memory_space=pltpu.SMEM)] + [VMEM] * 7,
        out_specs=[VMEM, VMEM],
        out_shape=(jax.ShapeDtypeStruct((rows, width), f32), jax.ShapeDtypeStruct((16, width), f32)),
        scratch_shapes=[pltpu.VMEM((2 * gap + 2 * half, width), bf16)],
        compiler_params=pltpu.CompilerParams(vmem_limit_bytes=16 << 20),
        cost_estimate=NO_COST,
        name="first_norm_back",
    )(place, mine, other, pair, tokens, grad_mixed, small_params, early_sums)


def gelu_parts(values):
    normal_cdf = 0.5 * (1.0 + lax.erf(values * (0.5**0.5)))
    return values * normal_cdf, normal_cdf + values * (0.3989422804014327 * jnp.exp(-0.5 * values * values))


def feed_forward(place, rows_in, upstream, rest, bias, with_feed):
    n_rows, width = rows_in.shape
    n_ff = bias.shape[2]
    tile = 256

    def body(place_ref, x_ref, u_ref, rest_ref, bias_ref, hid_ref, pre_ref, back_ref, sum_ref, xt_ref, ut_ref, *feed):
        step = pl.program_id(0)
        x = x_ref[...]
        u = u_ref[...]
        xt_ref[...] = x.T
        ut_ref[...] = u.T
        back = fed = None
        for j in range(2):
            s = place_ref[0] if j == 0 else 1 - place_ref[0]
            columns = slice(j * n_ff, (j + 1) * n_ff)
            up = rest_ref[s, :, :n_ff]
            down = rest_ref[s, :, n_ff : 2 * n_ff]
            hidden, slope = gelu_parts(dot_nn(x, up) + bias_ref[s])
            hidden = hidden.astype(bf16)
            hid_ref[:, columns] = hidden
            grad_pre = (dot_nn(u, down) * slope).astype(bf16)
            if with_feed:
                part = dot_nt(hidden, down)
                fed = part if fed is None else fed + part
            pre_ref[:, columns] = grad_pre
            sums = jnp.sum(grad_pre.astype(f32), axis=0, keepdims=True)
            sum_ref[:, columns] = jnp.where(step == 0, sums, sum_ref[:, columns] + sums)
            part = dot_nt(grad_pre, up)
            back = part if back is None else back + part
        back_ref[...] = back.astype(back_ref.dtype)
        if with_feed:
            feed[0][...] = fed.astype(bf16)

    by_row = lambda columns: pl.BlockSpec((tile, columns), lambda i, p: (i, 0))
    grid = pltpu.PrefetchScalarGridSpec(
        num_scalar_prefetch=1,
        grid=(n_rows // tile,),
        in_specs=[
            by_row(width),
            by_row(width),
            pl.BlockSpec(rest.shape, lambda i, p: (0, 0, 0), pipeline_mode=ONCE),
            pl.BlockSpec(bias.shape, lambda i, p: (0, 0, 0), pipeline_mode=ONCE),
        ],
        out_specs=[
            by_row(2 * n_ff),
            by_row(2 * n_ff),
            by_row(width),
            pl.BlockSpec((1, 2 * n_ff), lambda i, p: (0, 0)),
            pl.BlockSpec((width, tile), lambda i, p: (0, i)),
            pl.BlockSpec((width, tile), lambda i, p: (0, i)),
        ]
        + [by_row(width)] * with_feed,
    )
    return pl.pallas_call(
        body,
        grid_spec=grid,
        out_shape=(
            pltpu.HBM((n_rows, 2 * n_ff), bf16),
            pltpu.HBM((n_rows, 2 * n_ff), bf16),
            jax.ShapeDtypeStruct((n_rows, width), bf16 if with_feed else f32),
            jax.ShapeDtypeStruct((1, 2 * n_ff), f32),
            pltpu.HBM((width, n_rows), bf16),
            pltpu.HBM((width, n_rows), bf16),
        )
        + (jax.ShapeDtypeStruct((n_rows, width), bf16),) * with_feed,
        compiler_params=pltpu.CompilerParams(dimension_semantics=("arbitrary",), vmem_limit_bytes=20 << 20),
        cost_estimate=NO_COST,
        name="feed_forward",
    )(place, rows_in, upstream, *far(rest), bias)


def weight_grads(twos, grad_pres, ups, hiddens):
    width, n_rows = twos[0].shape
    n_ff = hiddens[0].shape[1]
    block = 512
    per = n_ff // block

    def body(x0, x1, p0, p1, u0, u1, h0, h1, out_ref):
        step = pl.program_id(0)

        @pl.when(step < per)
        def _():
            out_ref[...] = (dot_nn(x0[...], p0[...]) + dot_nn(x1[...], p1[...])).astype(bf16)

        @pl.when(step >= per)
        def _():
            out_ref[...] = (dot_nn(u0[...], h0[...]) + dot_nn(u1[...], h1[...])).astype(bf16)

    whole = lambda array: pl.BlockSpec(array.shape, lambda i: (0, 0), pipeline_mode=ONCE)
    early = pl.BlockSpec((n_rows, block), lambda i: (0, jnp.minimum(i, per - 1)))
    late = pl.BlockSpec((n_rows, block), lambda i: (0, jnp.clip(i - per, 0, per - 1)))
    return pl.pallas_call(
        body,
        grid=(2 * per,),
        in_specs=[whole(twos[0])] * 2 + [early] * 2 + [whole(ups[0])] * 2 + [late] * 2,
        out_specs=pl.BlockSpec((width, block), lambda i: (0, i)),
        out_shape=pltpu.HBM((width, 2 * n_ff), bf16),
        compiler_params=pltpu.CompilerParams(dimension_semantics=("arbitrary",), vmem_limit_bytes=16 << 20),
        cost_estimate=NO_COST,
        name="weight_grads",
    )(*twos, *far(*grad_pres), *ups, *far(*hiddens))


def attended_grads(mixed_own, mixed_other, full_out):
    n_rows, width = mixed_own.shape
    columns = full_out.shape[1] // 2

    def body(own_ref, other_ref, out_ref, *grads):
        turned = out_ref[...].T
        for j in range(2):
            part = turned[j * columns : (j + 1) * columns]
            grads[j][:, :n_rows] = dot_nt(part, own_ref[...]).astype(bf16)
            grads[j][:, n_rows:] = dot_nt(part, other_ref[...]).astype(bf16)

    shape = (columns, 2 * n_rows)
    return pl.pallas_call(
        body,
        in_specs=[VMEM] * 3,
        out_specs=[VMEM] * 2,
        out_shape=(jax.ShapeDtypeStruct(shape, bf16),) * 2,
        compiler_params=pltpu.CompilerParams(vmem_limit_bytes=12 << 20),
        cost_estimate=NO_COST,
        name="attended_grads",
    )(mixed_own, mixed_other, full_out)


def second_norm_back(place, pair, received, mixed, upstream_low, small_params, bias_grad):
    rows, width = mixed.shape
    step = 128

    def body(place_ref, pair_ref, got_ref, mixed_ref, up_ref, small_ref, bias_ref, grad_ref, low_ref, sum_ref):
        sums = [jnp.zeros((1, width), f32) for _ in range(4)]
        for k in range(0, rows, step):
            at = slice(k, k + step)
            back = pair_ref[at] + got_ref[at].astype(f32)
            upstream = up_ref[at].astype(f32)
            _, unit_rows, inverse = layer_norm_parts(mixed_ref[at], 1.0, 0.0)
            grad = upstream + norm_backward(back, unit_rows, inverse, small_ref[2:3, :])
            grad_ref[at] = grad
            low_ref[at] = grad.astype(bf16)
            for i, term in enumerate((back * unit_rows, back, grad, upstream)):
                sums[i] = sums[i] + jnp.sum(term, axis=0, keepdims=True)
        sum_ref[...] = jnp.zeros_like(sum_ref)
        for i in range(4):
            sum_ref[i + 2 : i + 3, :] = sums[i]
        for i in range(4):
            own = jnp.where(place_ref[0] == i, bias_ref[0:1, :width], jnp.zeros((1, width), f32))
            peer = jnp.where(place_ref[1] == i, bias_ref[0:1, width:], jnp.zeros((1, width), f32))
            sum_ref[i + 6 : i + 7, :] = own + peer

    return pl.pallas_call(
        body,
        in_specs=[pl.BlockSpec(memory_space=pltpu.SMEM)] + [VMEM] * 6,
        out_specs=[VMEM] * 3,
        out_shape=(
            jax.ShapeDtypeStruct((rows, width), f32),
            jax.ShapeDtypeStruct((rows, width), bf16),
            jax.ShapeDtypeStruct((16, width), f32),
        ),
        compiler_params=pltpu.CompilerParams(vmem_limit_bytes=16 << 20),
        name="second_norm_back",
    )(place, pair, received, mixed, upstream_low, small_params, bias_grad)


def finish_grads(n_data, keep, got, reduced, from_peer, late_sums, n_qkv):
    d_local = reduced.shape[0]
    n_ff = from_peer.shape[1] // 2
    n_out = keep.shape[2] - n_qkv

    def body(keep_ref, got_ref, red_ref, peer_ref, sum_ref, qkv_ref, out_ref, up_ref, down_ref, total_ref):
        heads_grad = keep_ref[0] + got_ref[0].astype(f32)
        qkv_ref[...] = heads_grad[:, :n_qkv]
        out_ref[...] = heads_grad[:, n_qkv:]
        squares = jnp.sum(jnp.square(heads_grad * (1.0 / n_data)), keepdims=True)
        for ref, at, peer_at in ((up_ref, 0, 0), (down_ref, 2 * n_ff, n_ff)):
            grad = red_ref[:, at : at + n_ff].astype(f32) + peer_ref[:, peer_at : peer_at + n_ff].astype(f32)
            ref[...] = grad
            squares = squares + jnp.sum(jnp.square(grad * (1.0 / n_data)), keepdims=True)
        total_ref[...] = sum_ref[...]
        total_ref[10:11, :] = jnp.broadcast_to(squares, (1, sum_ref.shape[1]))

    shapes = [(d_local, n_qkv), (d_local, n_out), (d_local, n_ff), (d_local, n_ff), late_sums.shape]
    return pl.pallas_call(
        body,
        in_specs=[VMEM] * 5,
        out_specs=[VMEM] * 5,
        out_shape=tuple(jax.ShapeDtypeStruct(shape, f32) for shape in shapes),
        compiler_params=pltpu.CompilerParams(vmem_limit_bytes=8 << 20),
        name="finish_grads",
    )(keep, got, reduced, from_peer, late_sums)


def optimizer(n_data, summed, grads, states):
    rates = learning_rates()
    flat = [array for group in states for array in group]
    n_states = len(states)
    heads = grads[0].shape[1] // (3 * HEAD_DIM)

    def body(*refs):
        summed_ref = refs[0]
        grad_refs = refs[1:5]
        state_refs = refs[5 : 5 + 3 * n_states]
        norm_ref = refs[5 + 3 * n_states]
        out_refs = refs[6 + 3 * n_states :]
        small = summed_ref[0:10, :] * (1.0 / n_data)
        total = jnp.sum(small * small, keepdims=True) + summed_ref[10:11, 0:1]
        norm = jnp.sqrt(total)
        norm_ref[...] = norm
        factor = CLIP_NORM / jnp.maximum(norm, CLIP_NORM)

        def update(index, gradient, take=(slice(None), slice(None))):
            w, m, v = (ref[take] for ref in state_refs[3 * index : 3 * index + 3])
            results = adam_update(w, gradient * factor, m, v, rates[index])
            for ref, value in zip(out_refs[3 * index : 3 * index + 3], results):
                ref[take] = value

        for head in range(heads):
            pieces = [
                grad_refs[0][:, (part * heads + head) * HEAD_DIM : (part * heads + head + 1) * HEAD_DIM]
                for part in range(3)
            ]
            at = slice(3 * head * HEAD_DIM, 3 * (head + 1) * HEAD_DIM)
            update(0, jnp.concatenate(pieces, axis=1) * (1.0 / n_data), (slice(None), at))
        update(1, grad_refs[1][...].T * (1.0 / n_data))
        update(2, grad_refs[2][...] * (1.0 / n_data))
        update(3, grad_refs[3][...] * (1.0 / n_data))
        update(4, small[0:6])
        lanes = 128
        bias_grads = [
            small[6 + row : 7 + row, k * lanes : (k + 1) * lanes]
            for row in range(4)
            for k in range(small.shape[1] // lanes)
        ]
        update(5, jnp.concatenate(bias_grads, axis=0))

    whole = lambda array: pl.BlockSpec(array.shape, lambda i: (0,) * len(array.shape))
    return pl.pallas_call(
        body,
        grid=(1,),
        in_specs=[whole(array) for array in (summed, *grads, *flat)],
        out_specs=[pl.BlockSpec((1, 1), lambda i: (0, 0))] + [whole(array) for array in flat],
        out_shape=(
            jax.ShapeDtypeStruct((1, 1), f32),
            *(jax.ShapeDtypeStruct(array.shape, f32) for array in flat),
        ),
        compiler_params=pltpu.CompilerParams(vmem_limit_bytes=16 << 20),
        name="optimizer",
    )(summed, *grads, *flat)


def body(
    tokens,
    cotangent,
    row_item,
    w_qkv,
    w_out,
    w_up,
    w_down,
    small_params,
    up_bias,
    first_qkv,
    first_out,
    first_up,
    first_down,
    first_small,
    first_bias,
    second_qkv,
    second_out,
    second_up,
    second_down,
    second_small,
    second_bias,
):
    rows = tokens.shape[0]
    n_data = lax.axis_size("dp")
    high = lax.axis_index("hi")
    low = lax.axis_index("lo")
    heads_local = w_qkv.shape[1] // (3 * HEAD_DIM)
    head_width = heads_local * HEAD_DIM
    ff_local = w_up.shape[1]
    d_local = w_qkv.shape[0]
    n_own = 2 * rows
    n_halo = LONG - 1
    half = n_halo // 2

    shard_qkv = (
        w_qkv.astype(bf16)
        .reshape(d_local, heads_local, 3, HEAD_DIM)
        .transpose(0, 2, 1, 3)
        .reshape(d_local, 3 * head_width)
    )
    shard_rest = rest_shard(w_up, w_down.T, w_out)
    qkv_mine = gather_rows(shard_qkv, "dp")
    rest = lax.all_gather(shard_rest, ("hi", "dp"), axis=0, tiled=True).reshape(2, D, -1)
    outs = rest[:, :, 2 * ff_local :]
    full_out = jnp.concatenate(
        [
            lax.dynamic_index_in_dim(outs, high, 0, keepdims=False),
            lax.dynamic_index_in_dim(outs, 1 - high, 0, keepdims=False),
        ],
        axis=1,
    )

    group_row = (2 * high + low) * rows
    own_ids = lax.dynamic_slice_in_dim(row_item, group_row, rows)
    keep_rows = (own_ids >= 0).astype(f32)[:, None]
    residual = tokens.astype(f32)
    normed, _, _ = layer_norm_parts(residual, small_params[0], small_params[1])
    normed = normed.astype(bf16)
    normed_other = swap(normed, "lo")
    send_at = (1 - high) * (512 - 256 * low) + high * low * 1280
    send_rows = lax.dynamic_slice_in_dim(
        jnp.concatenate([normed, normed_other, normed], axis=0), send_at, half, axis=0
    )
    halo_mine = swap(send_rows, "hi")
    halo_other = swap(halo_mine, "lo")
    own_rows = jnp.concatenate([normed, normed_other], axis=0)
    halo_rows = jnp.concatenate([halo_mine, halo_other], axis=0)
    plan, query_class, key_class = attention_plan(row_item, high, low, n_own, n_halo, FORWARD_TILE)
    plan_back, _, _ = attention_plan(row_item, high, low, n_own, n_halo, BACKWARD_TILE)
    plan, plan_back, query_class, key_class, qkv_mine = lax.optimization_barrier(
        (plan, plan_back, query_class, key_class, qkv_mine)
    )

    upstream = cotangent.astype(f32) * keep_rows
    upstream_low = upstream.astype(bf16)
    upstream_low, qkv_mine = lax.optimization_barrier((upstream_low, qkv_mine))
    qkv_theirs = swap(qkv_mine, "hi")
    upstream_other = swap(upstream_low, "lo")
    own_rows, halo_rows = lax.optimization_barrier((own_rows, halo_rows))

    def project(weight):
        own = dot_tt(weight, own_rows).astype(bf16).reshape(3, heads_local, HEAD_DIM, n_own)
        halo = dot_tt(weight[:, head_width:], halo_rows).astype(bf16).reshape(2, heads_local, HEAD_DIM, n_halo)
        return own, halo

    own_m, halo_m = project(qkv_mine)
    att_m, lse_m = attend_forward(plan, own_m, halo_m, query_class, key_class)
    qkv_theirs, att_m = lax.optimization_barrier((qkv_theirs, att_m))
    own_t, halo_t = project(qkv_theirs)
    att_t, lse_t = attend_forward(plan, own_t, halo_t, query_class, key_class)
    flat = jnp.concatenate([att_m, att_t], axis=0).reshape(2 * head_width, n_own)

    first_half, second_half = slice(0, rows), slice(rows, n_own)

    got = swap(dot_tt(flat[:, second_half], full_out).astype(bf16), "lo")
    attention_part, got = lax.optimization_barrier((dot_tt(flat[:, first_half], full_out), got))
    attention_part = attention_part + got.astype(f32)
    mixed = residual + attention_part + small_params[4]
    normed_two, _, _ = layer_norm_parts(mixed, small_params[2], small_params[3])
    normed_two = normed_two.astype(bf16)
    two_other = swap(normed_two, "lo")
    bias_parts = up_bias.reshape(2, 2, ff_local)
    bias_pair = lax.dynamic_index_in_dim(bias_parts, low, 1, keepdims=False).reshape(2, 1, ff_local)
    half_place = high.astype(jnp.int32).reshape(1)
    hidden_o, pre_o, back_o, bias_o, two_t_o, up_t_o, feed_other = feed_forward(
        half_place, two_other, upstream_other, rest, bias_pair, True
    )
    normed_two, back_o, feed_other = lax.optimization_barrier((normed_two, back_o, feed_other))
    two_got = swap(back_o, "lo")
    feed_got = swap(feed_other, "lo")
    hidden_m, pre_m, two_pair, bias_m, two_t_m, up_t_m = feed_forward(
        half_place, normed_two, upstream_low, rest, bias_pair, False
    )
    bias_grad = bias_m + bias_o
    bias_place = jnp.stack([2 * high + low, 2 * (1 - high) + low]).astype(jnp.int32)
    grad_mixed, mixed_low, early_sums = second_norm_back(
        bias_place, two_pair, two_got, mixed, upstream_low, small_params, bias_grad
    )
    mixed_other = swap(mixed_low, "lo")
    grad_rest = weight_grads((two_t_m, two_t_o), (pre_m, pre_o), (up_t_m, up_t_o), (hidden_m, hidden_o))
    grad_rest, mixed_other = lax.optimization_barrier((grad_rest, mixed_other))
    grad_rest = lax.psum_scatter(grad_rest, "dp", scatter_dimension=0, tiled=True)
    att_grad_m, att_grad_t = attended_grads(mixed_low, mixed_other, full_out)
    att_grad_m = att_grad_m.reshape(heads_local, HEAD_DIM, n_own)
    att_grad_t = att_grad_t.reshape(heads_local, HEAD_DIM, n_own)

    down_t, halo_down_t = attend_backward(
        plan_back, own_t, halo_t, query_class, key_class, att_t, lse_t, att_grad_t
    )
    down_t = down_t.reshape(3 * head_width, n_own)
    halo_down_t = halo_down_t.reshape(2 * head_width, n_halo)

    flat_m, flat_t = flat[:head_width], flat[head_width:]
    qkv_for_peer = head_gradient_sent(
        down_t, own_rows, halo_down_t, halo_rows, flat_t, mixed_low, mixed_other
    )
    qkv_for_peer, att_grad_m = lax.optimization_barrier((qkv_for_peer, att_grad_m))
    qkv_from_peer = swap(qkv_for_peer, "hi")
    down_m, halo_down_m = attend_backward(
        plan_back, own_m, halo_m, query_class, key_class, att_m, lse_m, att_grad_m, lambda arrays: far(*arrays)
    )
    down_m = down_m.reshape(3 * head_width, n_own)
    halo_down_m = halo_down_m.reshape(2 * head_width, n_halo)

    def halo_part(at):
        return dot_tt(halo_down_t[:, at], qkv_theirs[:, head_width:]) + dot_tt(
            halo_down_m[:, at], qkv_mine[:, head_width:]
        )

    strides = bits("dp")
    pairs = ((down_t, qkv_theirs), (down_m, qkv_mine))
    halo_got = swap(halo_part(slice(half, n_halo)).astype(bf16), "lo").astype(f32)
    back_sent = rows_back(second_half, pairs)
    back_sent, qkv_from_peer = lax.optimization_barrier((back_sent, qkv_from_peer))
    back_got = swap(back_sent, "lo")
    upper = (lax.axis_index("dp") % 2).astype(jnp.int32).reshape(1)
    operands = (down_m, own_rows, halo_down_m, halo_rows, flat_m, mixed_low, mixed_other)
    keep, send = head_gradient_split(upper, n_data, operands, qkv_from_peer)
    halo_send = (halo_part(slice(0, half)) + halo_got).astype(bf16)
    send, down_m, hidden, back_got = lax.optimization_barrier((send, down_m, hidden_m, back_got))
    got = swap(send, "dp", strides[0])
    back_mine = swap(halo_send, "hi")
    back_pair = rows_back(first_half, ((down_t, qkv_theirs), (down_m, qkv_mine)), (back_got,))
    output = feed_rows(half_place, hidden, rest, (feed_got, mixed, small_params))
    got, back_mine, back_pair, output = lax.optimization_barrier((got, back_mine, back_pair, output))
    keep, send = fold_halves(keep, got, "dp", strides[1])
    got = swap(send, "dp", strides[1])
    back_other = swap(back_mine, "lo")
    theirs = jnp.concatenate(
        [grad_rest[:, ff_local : 2 * ff_local], grad_rest[:, 3 * ff_local : 4 * ff_local]], axis=1
    )
    got, back_other, theirs = lax.optimization_barrier((got, back_other, theirs))
    from_peer = swap(theirs, "hi")
    keep, send = fold_halves(keep, got, "dp", strides[2])
    send, back_other = lax.optimization_barrier((send, back_other))
    got = swap(send, "dp", strides[2])
    place = jnp.stack([low, high * (n_own - n_halo) + low * rows]).astype(jnp.int32)
    input_grad, late_sums = first_norm_back(
        place, back_mine, back_other, back_pair, tokens, grad_mixed, small_params, early_sums
    )
    got, late_sums = lax.optimization_barrier((got, late_sums))
    for stride in strides[3:]:
        keep, send = fold_halves(keep, got, "dp", stride)
        got = swap(send, "dp", stride)
    *grads, summed = finish_grads(n_data, keep, got, grad_rest, from_peer, late_sums, 3 * head_width)
    summed = sum_all(summed)
    norm, *updated = optimizer(
        n_data,
        summed,
        grads,
        (
            (w_qkv, first_qkv, second_qkv),
            (w_out, first_out, second_out),
            (w_up, first_up, second_up),
            (w_down.T, first_down.T, second_down.T),
            (small_params, first_small, second_small),
            tuple(array.reshape(-1, 128) for array in (up_bias, first_bias, second_bias)),
        ),
    )
    updated[9:12] = [array.T for array in updated[9:12]]
    updated[15:18] = [array.reshape(-1) for array in updated[15:18]]
    return (output, input_grad, norm[0, 0], *updated)


def solution(mesh):
    n_data, n_model = mesh.devices.shape
    split = Mesh(mesh.devices.reshape(n_data, 2, n_model // 2), ("dp", "hi", "lo"))
    model = ("hi", "lo")
    rows = P(("dp", "hi", "lo"), None)
    by_row = P("dp", model)
    by_column = P(model, "dp")
    states = (by_row, by_column, by_row, by_column, P(), P())
    in_specs = (rows, rows, P("dp"), *states, *states, *states)
    updated = []
    for spec in states:
        updated.extend([spec, spec, spec])
    out_specs = (rows, rows, P(), *updated)
    return jax.shard_map(body, mesh=split, in_specs=in_specs, out_specs=out_specs, check_vma=False)
```
